32 devices in a mesh: dp: 8 (over z, core), fsdp: 4 (over y, x).
Axes of the slice: x: 2, y: 2, z: 4, core: 2. Of those that a mesh axis runs over, the one named last changes fastest.
Arguments:
- tokens: bfloat16 [32768, 1280], P(('dp', 'fsdp')), may hold values from -6 to 6
- cotangent: bfloat16 [32768, 1280], P(('dp', 'fsdp')), may hold values from -6 to 6
- picture: int32 [32768], P(('dp', 'fsdp')), may hold values from -1 to 319, as said below
- adapter: int32 [32768], P(('dp', 'fsdp')), may hold values from -1 to 7, as said below
- patch_row: int32 [32768], P(('dp', 'fsdp')), may hold values from -1 to 127, as said below
- patch_col: int32 [32768], P(('dp', 'fsdp')), may hold values from -1 to 31, as said below
- qkv_weight: bfloat16 [1280, 3840], P(('dp', 'fsdp')), may hold values from -0.15625 to 0.15625
- qkv_bias: float32 [3840], replicated, may hold values from -3 to 3
- proj_weight: bfloat16 [1280, 1280], P(('dp', 'fsdp')), may hold values from -2.5 to 2.5
- proj_bias: float32 [1280], replicated, may hold values from -2 to 2
- fc1_weight: bfloat16 [1280, 5120], P(('dp', 'fsdp')), may hold values from -0.15625 to 0.15625
- fc1_bias: float32 [5120], replicated, may hold values from -3 to 3
- fc2_weight: bfloat16 [5120, 1280], P(('dp', 'fsdp')), may hold values from -0.078125 to 0.078125
- fc2_bias: float32 [1280], replicated, may hold values from -2 to 2
- norm1_gain: float32 [1280], replicated, may hold values from 0.5 to 1.5
- norm1_bias: float32 [1280], replicated, may hold values from -1 to 1
- norm2_gain: float32 [1280], replicated, may hold values from 0.5 to 1.5
- norm2_bias: float32 [1280], replicated, may hold values from -1 to 1
- qkv_down: bfloat16 [1280, 128], P(('dp', 'fsdp')), may hold values from -0.15625 to 0.15625
- qkv_up: bfloat16 [128, 3840], P(None, ('dp', 'fsdp')), may hold values from -1.5 to 1.5
- proj_down: bfloat16 [1280, 128], P(('dp', 'fsdp')), may hold values from -2.5 to 2.5
- proj_up: bfloat16 [128, 1280], P(None, ('dp', 'fsdp')), may hold values from -1.5 to 1.5
- fc1_down: bfloat16 [1280, 128], P(('dp', 'fsdp')), may hold values from -0.15625 to 0.15625
- fc1_up: bfloat16 [128, 5120], P(None, ('dp', 'fsdp')), may hold values from -1.5 to 1.5
- fc2_down: bfloat16 [5120, 128], P(('dp', 'fsdp')), may hold values from -0.078125 to 0.078125
- fc2_up: bfloat16 [128, 1280], P(None, ('dp', 'fsdp')), may hold values from -1.5 to 1.5
Outputs:
- block_out: bfloat16 [32768, 1280], P(('dp', 'fsdp'))
- tokens_grad: float32 [32768, 1280], P(('dp', 'fsdp'))
- qkv_down_grad: float32 [1280, 128], P(('dp', 'fsdp'))
- qkv_up_grad: float32 [128, 3840], P(None, ('dp', 'fsdp'))
- proj_down_grad: float32 [1280, 128], P(('dp', 'fsdp'))
- proj_up_grad: float32 [128, 1280], P(None, ('dp', 'fsdp'))
- fc1_down_grad: float32 [1280, 128], P(('dp', 'fsdp'))
- fc1_up_grad: float32 [128, 5120], P(None, ('dp', 'fsdp'))
- fc2_down_grad: float32 [5120, 128], P(('dp', 'fsdp'))
- fc2_up_grad: float32 [128, 1280], P(None, ('dp', 'fsdp'))
The draws below stay inside these ranges and needn't reach their ends.
Inputs may be any that keep to these rules, and one draw needn't show every extreme that they name: Each row of 1024 consecutive tokens holds whole pictures of 100 to 1024 patches, each a run of consecutive tokens with a number of its own, then padding (-1) to the row's end; one row is a single picture of 1024 patches, and every other row ends in padding. All tokens of a picture share one adapter; padding tokens have -1. `patch_row`: A picture's patches are numbered row by row in a width of 8 to 32 columns; the row that holds a single picture of 1024 patches uses 8 columns; -1 for padding. `patch_col`: column of the patch in the same numbering; -1 for padding.
All inputs are finite; a program needn't handle non-finite values.
Results may differ from the reference program's by a relative error of at most 0.014.
The reference program's roundings to bfloat16 on the way count: a program that leaves them out, or rounds other values in their place, can miss the bound.
Values may be sent and summed in bfloat16 or wider, within the bound.
No kernel may reach another device: no remote copies, remote signals or barrier semaphores. Data moves between devices by JAX's collectives and lax.ppermute only.
A program may use at most 512 MiB of HBM per device.

```python
import math
import jax
import jax.numpy as jnp
from jax import lax

D = 1280
HEADS = 16
HD = 80
FF = 5120
RANK = 16
ADAPTERS = 8
ADAPT_COLS = 128
PMIN = 100
PMAX = 1024
ROW = 1024
ROWS = 32
TOKENS = 32768


def arrangement(key):
    folded = jax.random.fold_in(key, 7321)
    size_key, row_key, width_key, adapter_key = jax.random.split(folded, 4)
    slot_count = ROW // PMIN
    lengths = jax.random.randint(size_key, (ROWS, slot_count), PMIN, PMAX)
    forced = jax.random.randint(row_key, (), 0, ROWS)
    row_ids = jnp.arange(ROWS, dtype=jnp.int32)[:, None]
    slot_ids = jnp.arange(slot_count, dtype=jnp.int32)[None, :]
    is_forced = row_ids == forced
    lengths = jnp.where(is_forced & (slot_ids == 0), PMAX, lengths)
    run_ends = jnp.cumsum(lengths, axis=1)
    ceiling = jnp.where(is_forced, ROW, ROW - 1)
    fitting = run_ends <= ceiling
    filled = jnp.max(jnp.where(fitting, run_ends, 0), axis=1)
    run_starts = run_ends - lengths
    places = jnp.arange(ROW, dtype=jnp.int32)
    owners = jnp.sum((run_ends[:, None, :] <= places[None, :, None]).astype(jnp.int32), axis=2)
    owners = jnp.minimum(owners, slot_count - 1)
    matches = (owners[:, :, None] == slot_ids[:, None, :]).astype(jnp.int32)
    in_use = places[None, :] < filled[:, None]
    offsets = places[None, :] - jnp.sum(matches * run_starts[:, None, :], axis=2)
    widths = jax.random.randint(width_key, (ROWS, slot_count), 8, 33)
    widths = jnp.where(is_forced & (slot_ids == 0), 8, widths)
    token_width = jnp.sum(matches * widths[:, None, :], axis=2)
    chosen = jax.random.randint(adapter_key, (ROWS, slot_count), 0, ADAPTERS)
    chosen = jnp.where(slot_ids == 0, row_ids % ADAPTERS, chosen)
    token_adapter = jnp.sum(matches * chosen[:, None, :], axis=2)
    numbers = jnp.where(in_use, row_ids * slot_count + owners, -1).reshape(-1)
    adapters_out = jnp.where(in_use, token_adapter, -1).reshape(-1)
    rows_out = jnp.where(in_use, offsets // token_width, -1).reshape(-1)
    cols_out = jnp.where(in_use, offsets % token_width, -1).reshape(-1)
    return (numbers, adapters_out, rows_out, cols_out)


def draw_picture(key, part):
    return arrangement(key)[0]


def draw_adapter(key, part):
    return arrangement(key)[1]


def draw_patch_row(key, part):
    return arrangement(key)[2]


def draw_patch_col(key, part):
    return arrangement(key)[3]


def block_scale(rng, shape, cuts, least, largest):
    def one(dim, blocks):
        heights = jax.random.uniform(jax.random.fold_in(jax.random.fold_in(rng, 6), dim), (blocks,), jnp.float32, least / len(cuts), largest / len(cuts))
        return jnp.repeat(jnp.exp(heights), shape[dim] // blocks).reshape((-1,) + (1,) * (len(shape) - dim - 1))

    level = one(*cuts[0])
    for cut in cuts[1:]:
        level = level * one(*cut)
    return level


def normal_values(own_key, shape, deviation, bound, cuts=(), held_as=jnp.bfloat16):
    drawn = deviation * jax.random.normal(own_key, shape, jnp.float32)
    if cuts:
        drawn = drawn * block_scale(own_key, shape, cuts, -0.22, 0.18)
    return jnp.clip(drawn, -bound, bound).astype(held_as)


def setup_inputs(seed: int = 0) -> dict:
    seeds = jax.random.split(jax.random.key(seed), 27)
    tokens = normal_values(seeds[0], (TOKENS, D), 1.0, 6.0, ((0, 32),))
    cotangent = normal_values(seeds[1], (TOKENS, D), 1.0, 6.0, ((0, 32),))
    picture = draw_picture(jax.random.fold_in(seeds[26], 71), 0)
    adapter = draw_adapter(jax.random.fold_in(seeds[26], 71), 0)
    patch_row = draw_patch_row(jax.random.fold_in(seeds[26], 71), 0)
    patch_col = draw_patch_col(jax.random.fold_in(seeds[26], 71), 0)
    qkv_weight = normal_values(seeds[6], (D, 3 * D), D ** -0.5, 0.15625, ((0, 32),))
    qkv_bias = normal_values(seeds[7], (3 * D,), 0.5, 3.0, (), jnp.float32)
    proj_weight = normal_values(seeds[8], (D, D), (max(4, D // 256)) ** -0.5, 2.5, ((0, 32),))
    proj_bias = normal_values(seeds[9], (D,), 0.3, 2.0, (), jnp.float32)
    fc1_weight = normal_values(seeds[10], (D, FF), D ** -0.5, 0.15625, ((0, 32),))
    fc1_bias = normal_values(seeds[11], (FF,), 0.5, 3.0, (), jnp.float32)
    fc2_weight = normal_values(seeds[12], (FF, D), FF ** -0.5, 0.078125, ((0, 32),))
    fc2_bias = normal_values(seeds[13], (D,), 0.3, 2.0, (), jnp.float32)
    norm1_gain = jnp.clip(1.0 + 0.1 * jax.random.normal(seeds[14], (D,), jnp.float32), 0.5, 1.5)
    norm1_bias = normal_values(seeds[15], (D,), 0.2, 1.0, (), jnp.float32)
    norm2_gain = jnp.clip(1.0 + 0.1 * jax.random.normal(seeds[16], (D,), jnp.float32), 0.5, 1.5)
    norm2_bias = normal_values(seeds[17], (D,), 0.2, 1.0, (), jnp.float32)
    qkv_down = normal_values(seeds[18], (D, ADAPT_COLS), D ** -0.5, 0.15625, ((0, 32),))
    qkv_up = normal_values(seeds[19], (ADAPT_COLS, 3 * D), RANK ** -0.5, 1.5, ((1, 32),))
    proj_down = normal_values(seeds[20], (D, ADAPT_COLS), (max(4, D // 256)) ** -0.5, 2.5, ((0, 32),))
    proj_up = normal_values(seeds[21], (ADAPT_COLS, D), RANK ** -0.5, 1.5, ((1, 32),))
    fc1_down = normal_values(seeds[22], (D, ADAPT_COLS), D ** -0.5, 0.15625, ((0, 32),))
    fc1_up = normal_values(seeds[23], (ADAPT_COLS, FF), RANK ** -0.5, 1.5, ((1, 32),))
    fc2_down = normal_values(seeds[24], (FF, ADAPT_COLS), FF ** -0.5, 0.078125, ((0, 32),))
    fc2_up = normal_values(seeds[25], (ADAPT_COLS, D), RANK ** -0.5, 1.5, ((1, 32),))
    return dict(tokens=tokens, cotangent=cotangent, picture=picture, adapter=adapter, patch_row=patch_row, patch_col=patch_col, qkv_weight=qkv_weight, qkv_bias=qkv_bias, proj_weight=proj_weight, proj_bias=proj_bias, fc1_weight=fc1_weight, fc1_bias=fc1_bias, fc2_weight=fc2_weight, fc2_bias=fc2_bias, norm1_gain=norm1_gain, norm1_bias=norm1_bias, norm2_gain=norm2_gain, norm2_bias=norm2_bias, qkv_down=qkv_down, qkv_up=qkv_up, proj_down=proj_down, proj_up=proj_up, fc1_down=fc1_down, fc1_up=fc1_up, fc2_down=fc2_down, fc2_up=fc2_up)


@jax.custom_vjp
def low(v):
    return lax.optimization_barrier(v.astype(jnp.bfloat16)).astype(jnp.float32)

@jax.custom_vjp
def low_back(v):
    return v

def low_keep(v):
    return (low(v), None)

def low_pass(kept, grad):
    return (grad,)

def back_keep(v):
    return (v, None)

def back_low(kept, grad):
    return (low(grad),)
low.defvjp(low_keep, low_pass)
low_back.defvjp(back_keep, back_low)
EPS = 1e-06
HIGH = lax.Precision.HIGHEST

def product(left, right):
    return jnp.dot(left, right, precision=HIGH, preferred_element_type=jnp.float32)

def layer_norm(values, gain, shift):
    centre = lax.optimization_barrier(jnp.mean(values, axis=-1, keepdims=True))
    centred = values - centre
    variance = lax.optimization_barrier(jnp.mean(centred * centred, axis=-1, keepdims=True))
    return centred * lax.rsqrt(variance + EPS) * gain + shift

def adapted(inputs, weight, bias, down_map, up_map, selector):
    inner = low_back(low(product(inputs, down_map) * selector))
    return low_back(product(inputs, weight) + bias + product(inner, up_map))

def rotary_tables(patch_row, patch_col, head_size):
    quarter = head_size // 4
    inverse = 1.0 / 10000.0 ** (jnp.arange(quarter, dtype=jnp.float32) * 2.0 / (head_size // 2))
    angles = jnp.concatenate([patch_row.astype(jnp.float32)[:, None] * inverse, patch_col.astype(jnp.float32)[:, None] * inverse], axis=1)
    angles = jnp.concatenate([angles, angles], axis=1)
    return (jnp.cos(angles), jnp.sin(angles))

def rotate(tensor, cosine, sine):
    half_size = tensor.shape[-1] // 2
    turned = jnp.concatenate([-tensor[..., half_size:], tensor[..., :half_size]], axis=-1)
    return tensor * cosine[:, None, :] + turned * sine[:, None, :]

def row_attention(pieces):
    query_rows, key_rows, value_rows, picture_row = pieces
    scores = low_back(jnp.einsum('qhd,khd->hqk', query_rows, key_rows, precision=HIGH) * (1.0 / math.sqrt(HD)))
    same = picture_row[:, None] == picture_row[None, :]
    scores = jnp.where(same[None], scores, -1e+30)
    shifted = scores - lax.optimization_barrier(jnp.max(scores, axis=-1, keepdims=True))
    expo = jnp.exp(shifted)
    probs = low(expo / lax.optimization_barrier(jnp.sum(expo, axis=-1, keepdims=True)))
    return jnp.einsum('hqk,khd->qhd', probs, value_rows, precision=HIGH)

def forward(inputs, adapt, frozen, labels):
    qkv_weight, qkv_bias, proj_weight, proj_bias, fc1_weight, fc1_bias, fc2_weight, fc2_bias, norm1_gain, norm1_bias, norm2_gain, norm2_bias = frozen
    picture, adapter, patch_row, patch_col = labels
    qkv_down, qkv_up, proj_down, proj_up, fc1_down, fc1_up, fc2_down, fc2_up = adapt
    count = inputs.shape[0]
    selector = (jnp.arange(ADAPT_COLS, dtype=jnp.int32)[None, :] // RANK == adapter[:, None]).astype(inputs.dtype)
    normed = low(layer_norm(inputs, norm1_gain, norm1_bias))
    mixed = adapted(normed, qkv_weight, qkv_bias, qkv_down, qkv_up, selector)
    cosine, sine = rotary_tables(patch_row, patch_col, HD)
    split = mixed.reshape(count, 3, HEADS, HD)
    queries = low(rotate(split[:, 0], cosine, sine))
    keyset = low(rotate(split[:, 1], cosine, sine))
    valueset = low(split[:, 2])
    row_count = count // ROW
    attended = lax.map(jax.checkpoint(row_attention), (queries.reshape(row_count, ROW, HEADS, HD), keyset.reshape(row_count, ROW, HEADS, HD), valueset.reshape(row_count, ROW, HEADS, HD), picture.reshape(row_count, ROW)))
    attended = low_back(low(attended.reshape(count, D)))
    middle = inputs + adapted(attended, proj_weight, proj_bias, proj_down, proj_up, selector)
    normed_two = low(layer_norm(middle, norm2_gain, norm2_bias))
    hidden = adapted(normed_two, fc1_weight, fc1_bias, fc1_down, fc1_up, selector)
    active = low(hidden * jax.nn.sigmoid(1.702 * hidden))
    output = adapted(active, fc2_weight, fc2_bias, fc2_down, fc2_up, selector)
    valid = (picture >= 0).astype(inputs.dtype)[:, None]
    return (middle + output) * valid

def reference(tokens, cotangent, picture, adapter, patch_row, patch_col, qkv_weight, qkv_bias, proj_weight, proj_bias, fc1_weight, fc1_bias, fc2_weight, fc2_bias, norm1_gain, norm1_bias, norm2_gain, norm2_bias, qkv_down, qkv_up, proj_down, proj_up, fc1_down, fc1_up, fc2_down, fc2_up):
    frozen = tuple((item.astype(jnp.float32) for item in (qkv_weight, qkv_bias, proj_weight, proj_bias, fc1_weight, fc1_bias, fc2_weight, fc2_bias, norm1_gain, norm1_bias, norm2_gain, norm2_bias)))
    adapt = tuple((item.astype(jnp.float32) for item in (qkv_down, qkv_up, proj_down, proj_up, fc1_down, fc1_up, fc2_down, fc2_up)))
    group = math.gcd(ROWS, max(1, 4096 // ROW))
    sections = ROWS // group
    span_tokens = group * ROW
    inputs = tokens.astype(jnp.float32).reshape(sections, span_tokens, D)
    pulls = cotangent.astype(jnp.float32).reshape(sections, span_tokens, D)
    labels = tuple((item.reshape(sections, span_tokens) for item in (picture, adapter, patch_row, patch_col)))

    def one_section(totals, pieces):
        section_in, section_pull, section_pic, section_ada, section_row, section_col = pieces

        def run(values, adapters_now):
            return forward(values, adapters_now, frozen, (section_pic, section_ada, section_row, section_col))
        result, puller = jax.vjp(run, section_in, adapt)
        grad_in, grad_adapt = puller(section_pull)
        totals = tuple((total + piece for total, piece in zip(totals, grad_adapt)))
        return (totals, (result, grad_in))
    start = tuple((jnp.zeros_like(item) for item in adapt))
    totals, (results, grads) = lax.scan(one_section, start, (inputs, pulls) + labels)
    factor = 1.0 / math.sqrt(TOKENS)
    return (results.reshape(TOKENS, D).astype(jnp.bfloat16), grads.reshape(TOKENS, D), totals[0] * factor, totals[1] * factor, totals[2] * factor, totals[3] * factor, totals[4] * factor, totals[5] * factor, totals[6] * factor, totals[7] * factor)
```

```python
import math

import jax
import jax.numpy as jnp
from jax import lax
from jax.sharding import PartitionSpec as P

HEADS = 16
HD = 80
RANK = 16


EPS = 1e-06


def product(left, right):
    return jnp.dot(left, right, preferred_element_type=jnp.float32)


def outer_rows(left, right):
    return lax.dot_general(
        left, right, (((0,), (0,)), ((), ())), preferred_element_type=jnp.float32
    )


def transposed(left, right):
    return lax.dot_general(
        left, right, (((1,), (1,)), ((), ())), preferred_element_type=jnp.float32
    )


def normalize(values, gain, shift):
    centre = jnp.mean(values, axis=-1, keepdims=True)
    centred = values - centre
    spread = lax.rsqrt(jnp.mean(centred * centred, axis=-1, keepdims=True) + EPS)
    unit = centred * spread
    return (unit * gain + shift, unit, spread)


def normalize_back(grad_out, unit, spread, gain):
    scaled = grad_out * gain
    return spread * (
        scaled
        - jnp.mean(scaled, axis=-1, keepdims=True)
        - unit * jnp.mean(scaled * unit, axis=-1, keepdims=True)
    )


def adapted(inputs, weight, bias, down_map, up_map, selector):
    inner = (product(inputs, down_map) * selector).astype(jnp.bfloat16)
    return (product(inputs, weight) + bias + product(inner, up_map), inner)


def adapted_back(grad_low, inputs, inner, weight, down_map, up_map, selector):
    inner_grad = (transposed(grad_low, up_map) * selector).astype(jnp.bfloat16)
    grad_in = transposed(grad_low, weight) + transposed(inner_grad, down_map)
    return (grad_in, outer_rows(inputs, inner_grad), outer_rows(inner, grad_low))


def rotary_tables(patch_row, patch_col, head_size):
    quarter = head_size // 4
    inverse = 1.0 / 10000.0 ** (jnp.arange(quarter, dtype=jnp.float32) * 2.0 / (head_size // 2))
    angles = jnp.concatenate(
        [
            patch_row.astype(jnp.float32)[:, None] * inverse,
            patch_col.astype(jnp.float32)[:, None] * inverse,
        ],
        axis=1,
    )
    angles = jnp.concatenate([angles, angles], axis=1)
    return (jnp.cos(angles), jnp.sin(angles))


def rotate(tensor, cosine, sine):
    half_size = tensor.shape[-1] // 2
    turned = jnp.concatenate([-tensor[..., half_size:], tensor[..., :half_size]], axis=-1)
    return tensor * cosine[:, None, :] + turned * sine[:, None, :]


def rotate_back(grads, cosine, sine):
    half_size = grads.shape[-1] // 2
    moved = grads * sine[:, None, :]
    return grads * cosine[:, None, :] + jnp.concatenate(
        [moved[..., half_size:], -moved[..., :half_size]], axis=-1
    )


def block_scores(query_block, key_rows, picture_block, picture, scale):
    scores = (
        jnp.einsum("qhd,khd->hqk", query_block, key_rows, preferred_element_type=jnp.float32)
        * scale
    )
    same = picture_block[:, None] == picture[None, :]
    return jnp.where(same[None], scores, -1e30)


def attend(query_rows, key_rows, value_rows, picture, scale):
    total_rows = query_rows.shape[0]
    stride_rows = min(512, total_rows)
    results = []
    logsums = []
    for begin_row in range(0, total_rows, stride_rows):
        scores = block_scores(
            query_rows[begin_row : begin_row + stride_rows],
            key_rows,
            picture[begin_row : begin_row + stride_rows],
            picture,
            scale,
        )
        highest = jnp.max(scores, axis=-1, keepdims=True)
        expo = jnp.exp(scores - highest)
        weight_sum = jnp.sum(expo, axis=-1, keepdims=True)
        probs_low = (expo / weight_sum).astype(jnp.bfloat16)
        results.append(
            jnp.einsum("hqk,khd->qhd", probs_low, value_rows, preferred_element_type=jnp.float32)
        )
        logsums.append(highest + jnp.log(weight_sum))
    return (jnp.concatenate(results, axis=0), jnp.concatenate(logsums, axis=1))


def attend_back(grad_rows, query_rows, key_rows, value_rows, picture, logsum, scale):
    total_rows = query_rows.shape[0]
    stride_rows = min(512, total_rows)
    key_grad = jnp.zeros(key_rows.shape, jnp.float32)
    value_grad = jnp.zeros(value_rows.shape, jnp.float32)
    query_parts = []
    for begin_row in range(0, total_rows, stride_rows):
        query_block = query_rows[begin_row : begin_row + stride_rows]
        grad_block = grad_rows[begin_row : begin_row + stride_rows]
        scores = block_scores(
            query_block, key_rows, picture[begin_row : begin_row + stride_rows], picture, scale
        )
        probs = jnp.exp(scores - logsum[:, begin_row : begin_row + stride_rows])
        probs_low = probs.astype(jnp.bfloat16)
        value_grad = value_grad + jnp.einsum(
            "hqk,qhd->khd", probs_low, grad_block, preferred_element_type=jnp.float32
        )
        prob_grad = jnp.einsum(
            "qhd,khd->hqk", grad_block, value_rows, preferred_element_type=jnp.float32
        )
        centre = jnp.sum(probs * prob_grad, axis=-1, keepdims=True)
        score_grad = (probs * (prob_grad - centre)).astype(jnp.bfloat16)
        query_parts.append(
            jnp.einsum("hqk,khd->qhd", score_grad, key_rows, preferred_element_type=jnp.float32)
            * scale
        )
        key_grad = (
            key_grad
            + jnp.einsum(
                "hqk,qhd->khd", score_grad, query_block, preferred_element_type=jnp.float32
            )
            * scale
        )
    return (jnp.concatenate(query_parts, axis=0), key_grad, value_grad)


def fold_rows(up_shard, rows):
    turned = up_shard.T
    pieces = turned.shape[0] // rows
    return jnp.concatenate([turned[i * rows : (i + 1) * rows] for i in range(pieces)], axis=1)


def unfold_rows(block, devices):
    rows = block.shape[0] // devices
    pieces = block.shape[1] // 128
    split = block.reshape(devices, rows, pieces, 128)
    return split.transpose(0, 2, 1, 3).reshape(-1, 128)


def gather_rows(packed):
    return lax.all_gather(packed, ("dp", "fsdp"), axis=0, tiled=True)


def halve(value, dim, axis, bit):
    size = lax.axis_size(axis)
    mine = (lax.axis_index(axis) >> bit) & 1
    send = lax.dynamic_index_in_dim(value, 1 - mine, dim, keepdims=False).astype(jnp.bfloat16)
    keep = lax.dynamic_index_in_dim(value, mine, dim, keepdims=False).astype(jnp.float32)
    got = lax.ppermute(send, axis, [(i, i ^ (1 << bit)) for i in range(size)])
    return keep + got.astype(jnp.float32)


def scatter_sum(stacked):
    dp_bits = lax.axis_size("dp").bit_length() - 1
    fs_bits = lax.axis_size("fsdp").bit_length() - 1
    rows = stacked.shape[1:]
    value = stacked.reshape((2,) * (dp_bits + fs_bits) + rows)
    names = [("dp", b) for b in reversed(range(dp_bits))] + [("fsdp", b) for b in reversed(range(fs_bits))]
    order = [("dp", 0)] + [("fsdp", b) for b in range(fs_bits)] + [("dp", b) for b in range(1, dp_bits)]
    for axis, bit in order:
        dim = names.index((axis, bit))
        names.pop(dim)
        value = halve(value, dim, axis, bit)
    return value


def local(
    tokens,
    cotangent,
    picture,
    adapter,
    patch_row,
    patch_col,
    qkv_weight,
    qkv_bias,
    proj_weight,
    proj_bias,
    fc1_weight,
    fc1_bias,
    fc2_weight,
    fc2_bias,
    norm1_gain,
    norm1_bias,
    norm2_gain,
    norm2_bias,
    qkv_down,
    qkv_up,
    proj_down,
    proj_up,
    fc1_down,
    fc1_up,
    fc2_down,
    fc2_up,
):
    devices = lax.axis_size(("dp", "fsdp"))
    rows = proj_weight.shape[0]
    width = proj_weight.shape[1]
    first = gather_rows(jnp.concatenate([qkv_weight, qkv_down, fold_rows(qkv_up, rows)], axis=1))
    second = gather_rows(
        jnp.concatenate(
            [
                fc1_weight,
                proj_weight,
                fc1_down,
                proj_down,
                fold_rows(proj_up, rows),
                fold_rows(fc1_up, rows),
                fold_rows(fc2_up, rows),
            ],
            axis=1,
        )
    )
    third = gather_rows(jnp.concatenate([fc2_weight, fc2_down], axis=1))
    q_cols = qkv_weight.shape[1]
    f_cols = fc1_weight.shape[1]
    w_qkv = first[:, :q_cols]
    a_qkv = first[:, q_cols : q_cols + 128]
    b_qkv = unfold_rows(first[:, q_cols + 128 :], devices).T
    w_fc1 = second[:, :f_cols]
    w_proj = second[:, f_cols : f_cols + width]
    base = f_cols + width
    a_fc1 = second[:, base : base + 128]
    a_proj = second[:, base + 128 : base + 256]
    b_proj = unfold_rows(second[:, base + 256 : base + 384], devices).T
    b_fc1 = unfold_rows(second[:, base + 384 : base + 384 + 4 * 128], devices).T
    b_fc2 = unfold_rows(second[:, base + 384 + 4 * 128 :], devices).T
    w_fc2 = third[:, :width]
    a_fc2 = third[:, width:]
    row_count = tokens.shape[0]
    column_count = qkv_down.shape[1]
    scale = 1.0 / math.sqrt(HD)
    tokens_wide = tokens.astype(jnp.float32)
    valid = (picture >= 0).astype(jnp.float32)[:, None]
    selector = (
        lax.broadcasted_iota(jnp.int32, (1, column_count), 1) // RANK == adapter[:, None]
    ).astype(jnp.float32)
    normed, unit_one, spread_one = normalize(tokens_wide, norm1_gain, norm1_bias)
    normed_low = normed.astype(jnp.bfloat16)
    mixed, inner_qkv = adapted(normed_low, w_qkv, qkv_bias, a_qkv, b_qkv, selector)
    cosine, sine = rotary_tables(patch_row, patch_col, HD)
    split = mixed.reshape(row_count, 3, HEADS, HD)
    query_rows = rotate(split[:, 0], cosine, sine).astype(jnp.bfloat16)
    key_rows = rotate(split[:, 1], cosine, sine).astype(jnp.bfloat16)
    value_rows = split[:, 2].astype(jnp.bfloat16)
    attended, logsum = attend(query_rows, key_rows, value_rows, picture, scale)
    attended_low = attended.reshape(row_count, -1).astype(jnp.bfloat16)
    branch, inner_proj = adapted(attended_low, w_proj, proj_bias, a_proj, b_proj, selector)
    middle = tokens_wide + branch
    normed_two, unit_two, spread_two = normalize(middle, norm2_gain, norm2_bias)
    normed_two_low = normed_two.astype(jnp.bfloat16)
    hidden, inner_fc1 = adapted(normed_two_low, w_fc1, fc1_bias, a_fc1, b_fc1, selector)
    sigma = jax.nn.sigmoid(1.702 * hidden)
    active_low = (hidden * sigma).astype(jnp.bfloat16)
    output, inner_fc2 = adapted(active_low, w_fc2, fc2_bias, a_fc2, b_fc2, selector)
    block_out = ((middle + output) * valid).astype(jnp.bfloat16)
    grad_out = cotangent.astype(jnp.float32) * valid
    grad_out_low = grad_out.astype(jnp.bfloat16)
    grad_active, fc2_down_term, fc2_up_term = adapted_back(
        grad_out_low, active_low, inner_fc2, w_fc2, a_fc2, b_fc2, selector
    )
    grad_hidden = (grad_active * (sigma + 1.702 * hidden * sigma * (1.0 - sigma))).astype(
        jnp.bfloat16
    )
    grad_normed_two, fc1_down_term, fc1_up_term = adapted_back(
        grad_hidden, normed_two_low, inner_fc1, w_fc1, a_fc1, b_fc1, selector
    )
    grad_middle = grad_out + normalize_back(grad_normed_two, unit_two, spread_two, norm2_gain)
    grad_branch = grad_middle.astype(jnp.bfloat16)
    grad_attended, proj_down_term, proj_up_term = adapted_back(
        grad_branch, attended_low, inner_proj, w_proj, a_proj, b_proj, selector
    )
    grad_heads = grad_attended.astype(jnp.bfloat16).reshape(row_count, HEADS, HD)
    query_grad, key_grad, value_grad = attend_back(
        grad_heads, query_rows, key_rows, value_rows, picture, logsum, scale
    )
    grad_mixed = (
        jnp.concatenate(
            [
                rotate_back(query_grad, cosine, sine),
                rotate_back(key_grad, cosine, sine),
                value_grad,
            ],
            axis=1,
        )
        .reshape(row_count, -1)
        .astype(jnp.bfloat16)
    )
    grad_normed, qkv_down_term, qkv_up_term = adapted_back(
        grad_mixed, normed_low, inner_qkv, w_qkv, a_qkv, b_qkv, selector
    )
    tokens_grad = grad_middle + normalize_back(grad_normed, unit_one, spread_one, norm1_gain)
    factor = 1.0 / math.sqrt(row_count * devices)

    def stack(terms):
        return jnp.concatenate([t.reshape(devices, -1, 128) for t in terms], axis=1)

    early = factor * scatter_sum(
        stack([proj_down_term, proj_up_term.T, fc1_down_term, fc1_up_term.T, fc2_down_term, fc2_up_term.T])
    )
    late = factor * scatter_sum(stack([qkv_down_term, qkv_up_term.T]))
    return (
        block_out,
        tokens_grad,
        late[:rows],
        late[rows:].T,
        early[:rows],
        early[rows : 2 * rows].T,
        early[2 * rows : 3 * rows],
        early[3 * rows : 7 * rows].T,
        early[7 * rows : 11 * rows],
        early[11 * rows :].T,
    )


def solution(mesh):
    return jax.shard_map(
        local,
        mesh=mesh,
        in_specs=(
            P(("dp", "fsdp"), None),
            P(("dp", "fsdp"), None),
            P(("dp", "fsdp")),
            P(("dp", "fsdp")),
            P(("dp", "fsdp")),
            P(("dp", "fsdp")),
            P(("dp", "fsdp"), None),
            P(),
            P(("dp", "fsdp"), None),
            P(),
            P(("dp", "fsdp"), None),
            P(),
            P(("dp", "fsdp"), None),
            P(),
            P(),
            P(),
            P(),
            P(),
            P(("dp", "fsdp"), None),
            P(None, ("dp", "fsdp")),
            P(("dp", "fsdp"), None),
            P(None, ("dp", "fsdp")),
            P(("dp", "fsdp"), None),
            P(None, ("dp", "fsdp")),
            P(("dp", "fsdp"), None),
            P(None, ("dp", "fsdp")),
        ),
        out_specs=(
            P(("dp", "fsdp"), None),
            P(("dp", "fsdp"), None),
            P(("dp", "fsdp"), None),
            P(None, ("dp", "fsdp")),
            P(("dp", "fsdp"), None),
            P(None, ("dp", "fsdp")),
            P(("dp", "fsdp"), None),
            P(None, ("dp", "fsdp")),
            P(("dp", "fsdp"), None),
            P(None, ("dp", "fsdp")),
        ),
        check_vma=False,
    )
```

```python
import math

import jax
import jax.numpy as jnp
from jax import lax
from jax.experimental import pallas as pl
from jax.experimental.pallas import tpu as pltpu
from jax.sharding import PartitionSpec as P

HEADS = 16
HD = 80
RANK = 16


EPS = 1e-06


BIG = 2.0**60
LOG2E = 1.4426950408889634
BF = jnp.bfloat16
F32 = jnp.float32


def normalize_back(grad_out, unit, spread, gain):
    scaled = grad_out * gain
    return spread * (
        scaled
        - jnp.mean(scaled, axis=-1, keepdims=True)
        - unit * jnp.mean(scaled * unit, axis=-1, keepdims=True)
    )


def rotary_tables(patch_row, patch_col, head_size):
    quarter = head_size // 4
    inverse = 1.0 / 10000.0 ** (jnp.arange(quarter, dtype=jnp.float32) * 2.0 / (head_size // 2))
    angles = jnp.concatenate(
        [
            patch_row.astype(jnp.float32)[:, None] * inverse,
            patch_col.astype(jnp.float32)[:, None] * inverse,
        ],
        axis=1,
    )
    angles = jnp.concatenate([angles, angles], axis=1)
    return (jnp.cos(angles), jnp.sin(angles))


def mm(left, right):
    return lax.dot_general(left, right, (((1,), (0,)), ((), ())), preferred_element_type=F32)


def mm_nt(left, right):
    return lax.dot_general(left, right, (((1,), (1,)), ((), ())), preferred_element_type=F32)


def call(body, name, grid, in_specs, out_specs, out_shape, scratch=(), flops=0, moved=0):
    return pl.pallas_call(
        body,
        name=name,
        grid=grid,
        in_specs=in_specs,
        out_specs=out_specs,
        out_shape=out_shape,
        scratch_shapes=scratch,
        cost_estimate=pl.CostEstimate(flops=flops, transcendentals=0, bytes_accessed=moved),
        compiler_params=pltpu.CompilerParams(
            dimension_semantics=("arbitrary",) * len(grid), vmem_limit_bytes=56 * 1024 * 1024
        ),
    )


def whole(shape):
    return pl.BlockSpec(shape, lambda *_: (0,) * len(shape))


def pick(adapter_ref, count):
    lanes = lax.broadcasted_iota(jnp.int32, (count, 128), 1) // RANK
    return (lanes == adapter_ref[...]).astype(F32)


def turn(values, low):
    size = values.shape[1]
    left = pltpu.roll(values, size - HD // 2, 1)
    right = pltpu.roll(values, HD // 2, 1)
    return jnp.where(low, left, right)


def qkv_body(x_ref, w_ref, a_ref, bt_ref, bias_ref, ad_ref, cos_ref, sin_ref, out_ref, inner_ref):
    part = pl.program_id(0)
    rows = x_ref.shape[0]
    step = 256

    @pl.when(part == 0)
    def _():
        inner_ref[...] = (mm(x_ref[...], a_ref[...]) * pick(ad_ref, rows)).astype(BF)

    def one(start, rotated):
        sl = pl.ds(start, step)
        y = mm(x_ref[sl, :], w_ref[...]) + mm_nt(inner_ref[sl, :], bt_ref[...]) + bias_ref[...]
        if rotated:
            low = lax.broadcasted_iota(jnp.int32, (step, 640), 1) % HD < HD // 2
            for begin in (0, 640):
                piece = y[:, begin : begin + 640]
                done = piece * cos_ref[sl, :] + turn(piece, low) * sin_ref[sl, :]
                out_ref[sl, begin : begin + 640] = done.astype(BF)
        else:
            out_ref[sl, :] = y.astype(BF)

    @pl.when(part < 2)
    def _():
        for i in range(0, rows, step):
            one(i, True)

    @pl.when(part == 2)
    def _():
        for i in range(0, rows, step):
            one(i, False)


def qkv_call(x, pack, bt, bias, adapter, cos_t, sin_t):
    n, d = x.shape
    return call(
        qkv_body,
        "qkv_rotary",
        (3,),
        [
            whole((n, d)),
            pl.BlockSpec((d, d), lambda j: (0, j)),
            pl.BlockSpec((d, 128), lambda j: (0, 3 * d // 128)),
            pl.BlockSpec((d, 128), lambda j: (j, 0)),
            pl.BlockSpec((1, d), lambda j: (0, j)),
            whole((n, 1)),
            whole((n, 640)),
            whole((n, 640)),
        ],
        [pl.BlockSpec((n, d), lambda j: (0, j)), whole((n, 128))],
        [jax.ShapeDtypeStruct((n, 3 * d), BF), jax.ShapeDtypeStruct((n, 128), BF)],
        flops=2 * n * d * 3 * d,
        moved=8 * d * d + 12 * n * d,
    )(x, pack, pack, bt, bias, adapter, cos_t, sin_t)


def attend_body(q_ref, k_ref, v_ref, qm_ref, km_ref, out_ref, lse_ref):
    rows = q_ref.shape[0]
    step = 256
    factor = LOG2E / math.sqrt(HD)
    lanes = lax.broadcasted_iota(jnp.int32, (step, 128), 1)
    for i in range(0, rows, step):
        lse_ref[i : i + step, :] = jnp.zeros((step, 128), F32)
    for h in range(8):
        cols = slice(HD * h, HD * h + HD)
        keys = jnp.concatenate([k_ref[:, cols], km_ref[...]], axis=1)
        vals = v_ref[:, cols]
        for i in range(0, rows, step):
            query = jnp.concatenate([q_ref[i : i + step, cols], qm_ref[i : i + step, :]], axis=1)
            s = mm_nt(query, keys)
            top = jnp.max(s, axis=1, keepdims=True)
            e = jnp.exp2((s - top) * factor)
            total = jnp.sum(e, axis=1, keepdims=True)
            o = mm(e.astype(BF), vals) * (1.0 / total)
            out_ref[i : i + step, cols] = o.astype(BF)
            lse = top + jnp.log(total) * math.sqrt(HD)
            lse_ref[i : i + step, :] = jnp.where(lanes == h, lse, lse_ref[i : i + step, :])


def attend_call(qkv, qm, km):
    n = qkv.shape[0]
    d = qkv.shape[1] // 3
    groups = d // 640
    return call(
        attend_body,
        "attend",
        (groups,),
        [
            pl.BlockSpec((n, 640), lambda g: (0, g)),
            pl.BlockSpec((n, 640), lambda g: (0, groups + g)),
            pl.BlockSpec((n, 640), lambda g: (0, 2 * groups + g)),
            whole((n, 48)),
            whole((n, 48)),
        ],
        [pl.BlockSpec((n, 640), lambda g: (0, g)), pl.BlockSpec((n, 128), lambda g: (0, g))],
        [jax.ShapeDtypeStruct((n, d), BF), jax.ShapeDtypeStruct((n, 128 * groups), F32)],
        flops=4 * n * n * d,
        moved=8 * n * d,
    )(qkv, qkv, qkv, qm, km)


def split_low(values, count):
    parts = []
    for _ in range(count):
        part = values.astype(BF)
        parts.append(part)
        values = values - part.astype(F32)
    return parts


def attend_back_body(
    q_ref, k_ref, v_ref, g_ref, o_ref, lse_ref, qm_ref, km_ref, cos_ref, sin_ref,
    dq_ref, dk_ref, dv_ref, dq_s, dk_s,
):
    rows = q_ref.shape[0]
    step = 256
    factor = LOG2E / math.sqrt(HD)
    scale = 1.0 / math.sqrt(HD)
    lanes = lax.broadcasted_iota(jnp.int32, (rows, 48), 1)
    ones_two = jnp.where((lanes == 16) | (lanes == 17), 1.0, 0.0).astype(BF)
    for h in range(8):
        cols = slice(HD * h, HD * h + HD)
        gh = g_ref[:, cols]
        delta = jnp.sum(gh.astype(F32) * o_ref[:, cols].astype(F32), axis=1, keepdims=True)
        d_hi, d_lo = split_low(-delta, 2)
        l_hi, l_mid, l_lo = split_low(-lse_ref[:, h : h + 1], 3)
        q_aug = jnp.where(
            lanes == 16,
            l_hi.astype(F32),
            jnp.where(
                lanes == 17,
                l_mid.astype(F32),
                jnp.where(lanes == 18, l_lo.astype(F32), qm_ref[...].astype(F32)),
            ),
        ).astype(BF)
        g_aug = jnp.where(
            lanes == 16, d_hi.astype(F32), jnp.where(lanes == 17, d_lo.astype(F32), 0.0)
        ).astype(BF)
        query = jnp.concatenate([q_ref[:, cols], q_aug], axis=1)
        grads = jnp.concatenate([gh, g_aug], axis=1)
        keys = jnp.concatenate([k_ref[:, cols], km_ref[...]], axis=1)
        vals = jnp.concatenate([v_ref[:, cols], ones_two], axis=1)
        keys_t = keys.T
        dk = jnp.zeros((rows, 128), F32)
        dv = jnp.zeros((rows, 128), F32)
        for i in range(0, rows, step):
            qb = query[i : i + step, :]
            gb = grads[i : i + step, :]
            p = jnp.exp2(mm_nt(keys, qb) * factor)
            dp = mm_nt(vals, gb)
            ds = (p * dp).astype(BF)
            dv = dv + mm(p.astype(BF), gb)
            dk = dk + mm(ds, qb)
            dq = mm(keys_t, ds)
            dq_s[i : i + step, cols] = dq.T[:, :HD]
        dk_s[:, cols] = dk[:, :HD]
        dv_ref[:, cols] = dv[:, :HD].astype(BF)
    low = lax.broadcasted_iota(jnp.int32, (step, 640), 1) % HD < HD // 2
    for i in range(0, rows, step):
        sl = slice(i, i + step)
        for src, dst in ((dq_s, dq_ref), (dk_s, dk_ref)):
            piece = src[sl, :] * scale
            dst[sl, :] = (piece * cos_ref[sl, :] - turn(piece, low) * sin_ref[sl, :]).astype(BF)


def attend_back_call(qkv, grads, attended, lse, qm, km, cos_t, sin_t):
    n = qkv.shape[0]
    d = qkv.shape[1] // 3
    groups = d // 640
    block = pl.BlockSpec((n, 640), lambda g: (0, g))
    return call(
        attend_back_body,
        "attend_back",
        (groups,),
        [
            block,
            pl.BlockSpec((n, 640), lambda g: (0, groups + g)),
            pl.BlockSpec((n, 640), lambda g: (0, 2 * groups + g)),
            block,
            block,
            pl.BlockSpec((n, 128), lambda g: (0, g)),
            whole((n, 48)),
            whole((n, 48)),
            whole((n, 640)),
            whole((n, 640)),
        ],
        [block, block, block],
        [jax.ShapeDtypeStruct((n, d), BF)] * 3,
        [pltpu.VMEM((n, 640), F32), pltpu.VMEM((n, 640), F32)],
        flops=10 * n * n * d,
        moved=16 * n * d,
    )(qkv, qkv, qkv, grads, attended, lse, qm, km, cos_t, sin_t)


def tables(picture, patch_row, patch_col):
    cosine, sine = rotary_tables(patch_row, patch_col, HD)
    half = HD // 2
    signed = jnp.concatenate([-sine[:, :half], sine[:, half:]], axis=1)
    count = picture.shape[0]
    change = (picture[1:] != picture[:-1]).astype(jnp.int32)
    places = lax.broadcasted_iota(jnp.int32, (count, count - 1), 0)
    before = lax.broadcasted_iota(jnp.int32, (count, count - 1), 1) < places
    index = jnp.sum(jnp.where(before, change[None, :], 0), axis=1)
    lanes = lax.broadcasted_iota(jnp.int32, (1, 48), 1)
    own = lanes == index[:, None]
    qm = jnp.where(own | (lanes >= 16), 0.0, -BIG).astype(BF)
    km = (own | ((lanes >= 16) & (lanes < 19))).astype(BF)
    return (jnp.tile(cosine, (1, 8)), jnp.tile(signed, (1, 8)), qm, km)


def stats(values):
    centre = jnp.mean(values, axis=-1, keepdims=True)
    centred = values - centre
    spread = lax.rsqrt(jnp.mean(centred * centred, axis=-1, keepdims=True) + EPS)
    return centred * spread, spread


def once(shape, index):
    return pl.BlockSpec(shape, index, pipeline_mode=pl.Buffered(1))


def proj_body(
    att_ref, w_ref, a_ref, bt_ref, bias_ref, ad_ref, tok_ref, gain_ref, shift_ref,
    mid_ref, norm_ref, inner_ref,
):
    rows = att_ref.shape[0]
    x = att_ref[...]
    inner = (mm(x, a_ref[...]) * pick(ad_ref, rows)).astype(BF)
    inner_ref[...] = inner
    middle = tok_ref[...].astype(F32) + (mm(x, w_ref[...]) + bias_ref[...] + mm_nt(inner, bt_ref[...]))
    mid_ref[...] = middle
    unit, _ = stats(middle)
    norm_ref[...] = (unit * gain_ref[...] + shift_ref[...]).astype(BF)


def proj_call(att, pack, first_col, a_col, bt, bias, adapter, tokens, gain, shift):
    n, d = att.shape
    step = 256
    row = pl.BlockSpec((step, d), lambda i: (i, 0))
    return call(
        proj_body,
        "proj_norm",
        (n // step,),
        [
            row,
            once((d, d), lambda i: (0, first_col // d)),
            once((d, 128), lambda i: (0, a_col // 128)),
            whole((d, 128)),
            whole((1, d)),
            pl.BlockSpec((step, 1), lambda i: (i, 0)),
            row,
            whole((1, d)),
            whole((1, d)),
        ],
        [row, row, pl.BlockSpec((step, 128), lambda i: (i, 0))],
        [
            jax.ShapeDtypeStruct((n, d), F32),
            jax.ShapeDtypeStruct((n, d), BF),
            jax.ShapeDtypeStruct((n, 128), BF),
        ],
        flops=2 * n * d * d,
        moved=2 * d * d + 10 * n * d,
    )(att, pack, pack, bt, bias, adapter, tokens, gain, shift)


def feed_body(
    x_ref, g_ref, w1_ref, w2_ref, a1_ref, bt1_ref, b1_ref, a2_ref, bt2_ref, b2_ref, ad_ref, val_ref, mid_ref,
    out_ref, gx_ref, ta1_ref, tb1_ref, ta2_ref, tb2_ref,
    acc_ref, in1_ref, in1t_ref, ig2_ref, ig2t_ref, in2_ref, ig1_ref, act_ref, gh_ref,
):
    j = pl.program_id(0)
    rows = x_ref.shape[0]
    step = 256

    @pl.when(j == 0)
    def _():
        sel = pick(ad_ref, rows)
        in1 = (mm(x_ref[...], a1_ref[...]) * sel).astype(BF)
        in1_ref[...] = in1
        in1t_ref[...] = in1.T
        ig2 = (mm(g_ref[...], bt2_ref[...]) * sel).astype(BF)
        ig2_ref[...] = ig2
        ig2t_ref[...] = ig2.T
        acc_ref[...] = jnp.zeros_like(acc_ref)
        gx_ref[...] = jnp.zeros_like(gx_ref)
        in2_ref[...] = jnp.zeros_like(in2_ref)
        ig1_ref[...] = jnp.zeros_like(ig1_ref)

    for i in range(0, rows, step):
        sl = slice(i, i + step)
        h = mm(x_ref[sl, :], w1_ref[...]) + mm_nt(in1_ref[sl, :], bt1_ref[...]) + b1_ref[...]
        ga = mm_nt(g_ref[sl, :], w2_ref[...]) + mm_nt(ig2_ref[sl, :], a2_ref[...])
        s = 0.5 * jnp.tanh(0.851 * h) + 0.5
        act = (h * s).astype(BF)
        gh = (ga * (s + 1.702 * h * s * (1.0 - s))).astype(BF)
        act_ref[sl, :] = act
        gh_ref[sl, :] = gh
        acc_ref[sl, :] += mm(act, w2_ref[...])
        in2_ref[sl, :] += mm(act, a2_ref[...])
        gx_ref[sl, :] += mm_nt(gh, w1_ref[...])
        ig1_ref[sl, :] += mm(gh, bt1_ref[...])
    ta2_ref[...] = mm(ig2t_ref[...], act_ref[...]).T.astype(BF)
    tb1_ref[...] = mm(in1t_ref[...], gh_ref[...]).T.astype(BF)

    @pl.when(j == pl.num_programs(0) - 1)
    def _():
        sel = pick(ad_ref, rows)
        in2 = (in2_ref[...] * sel).astype(BF)
        ig1 = (ig1_ref[...] * sel).astype(BF)
        for i in range(0, rows, step):
            sl = slice(i, i + step)
            out = acc_ref[sl, :] + b2_ref[...] + mm_nt(in2[sl, :], bt2_ref[...])
            out_ref[sl, :] = ((mid_ref[sl, :] + out) * val_ref[sl, :]).astype(BF)
            gx_ref[sl, :] += mm_nt(ig1[sl, :], a1_ref[...])
        ta1_ref[...] = mm(ig1.T, x_ref[...]).T.astype(BF)
        tb2_ref[...] = mm(in2.T, g_ref[...]).T.astype(BF)


def feed_call(x, grads, pack, a1_col, bt1, b1, pack2, bt2, b2, adapter, valid, middle):
    n, d = x.shape
    ff = bt1.shape[0]
    tile = 512
    full = once((n, d), lambda j: (0, 0))
    thin = once((d, 128), lambda j: (0, 0))
    return call(
        feed_body,
        "feed_forward",
        (ff // tile,),
        [
            full,
            full,
            pl.BlockSpec((d, tile), lambda j: (0, j)),
            pl.BlockSpec((tile, d), lambda j: (j, 0)),
            once((d, 128), lambda j: (0, a1_col // 128)),
            pl.BlockSpec((tile, 128), lambda j: (j, 0)),
            pl.BlockSpec((1, tile), lambda j: (0, j)),
            pl.BlockSpec((tile, 128), lambda j: (j, d // 128)),
            thin,
            whole((1, d)),
            once((n, 1), lambda j: (0, 0)),
            once((n, 1), lambda j: (0, 0)),
            full,
        ],
        [
            full,
            full,
            thin,
            pl.BlockSpec((tile, 128), lambda j: (j, 0)),
            pl.BlockSpec((tile, 128), lambda j: (j, 0)),
            thin,
        ],
        [
            jax.ShapeDtypeStruct((n, d), BF),
            jax.ShapeDtypeStruct((n, d), F32),
            jax.ShapeDtypeStruct((d, 128), BF),
            jax.ShapeDtypeStruct((ff, 128), BF),
            jax.ShapeDtypeStruct((ff, 128), BF),
            jax.ShapeDtypeStruct((d, 128), BF),
        ],
        [
            pltpu.VMEM((n, d), F32),
            pltpu.VMEM((n, 128), BF),
            pltpu.VMEM((128, n), BF),
            pltpu.VMEM((n, 128), BF),
            pltpu.VMEM((128, n), BF),
            pltpu.VMEM((n, 128), F32),
            pltpu.VMEM((n, 128), F32),
            pltpu.VMEM((n, tile), BF),
            pltpu.VMEM((n, tile), BF),
        ],
        flops=8 * n * d * ff,
        moved=4 * d * ff + 20 * n * d,
    )(x, grads, pack, pack2, pack, bt1, b1, pack2, bt2, b2, adapter, valid, middle)


def proj_back_body(
    gx_ref, mid_ref, cot_ref, val_ref, gain_ref, w_ref, a_ref, bt_ref, ad_ref, att_ref, inner_ref,
    gm_ref, ga_ref, ta_ref, tb_ref, ta_s, tb_s,
):
    i = pl.program_id(0)
    rows = gx_ref.shape[0]
    unit, spread = stats(mid_ref[...])
    gm = cot_ref[...].astype(F32) * val_ref[...] + normalize_back(gx_ref[...], unit, spread, gain_ref[...])
    gm_ref[...] = gm
    gb = gm.astype(BF)
    ig = (mm(gb, bt_ref[...]) * pick(ad_ref, rows)).astype(BF)
    ga_ref[...] = (mm_nt(gb, w_ref[...]) + mm_nt(ig, a_ref[...])).astype(BF)
    ta = mm(ig.T, att_ref[...])
    tb = mm(inner_ref[...].T, gb)

    @pl.when(i == 0)
    def _():
        ta_s[...] = ta
        tb_s[...] = tb

    @pl.when(i > 0)
    def _():
        ta_s[...] += ta
        tb_s[...] += tb

    @pl.when(i == pl.num_programs(0) - 1)
    def _():
        ta_ref[...] = ta_s[...].T.astype(BF)
        tb_ref[...] = tb_s[...].T.astype(BF)


def proj_back_call(gx, middle, cot, valid, gain, pack, first_col, a_col, bt, adapter, att, inner):
    n, d = gx.shape
    step = 256
    row = pl.BlockSpec((step, d), lambda i: (i, 0))
    one = pl.BlockSpec((step, 1), lambda i: (i, 0))
    thin = once((d, 128), lambda i: (0, 0))
    return call(
        proj_back_body,
        "proj_back",
        (n // step,),
        [
            row,
            row,
            row,
            one,
            whole((1, d)),
            once((d, d), lambda i: (0, first_col // d)),
            once((d, 128), lambda i: (0, a_col // 128)),
            thin,
            one,
            row,
            pl.BlockSpec((step, 128), lambda i: (i, 0)),
        ],
        [row, row, thin, thin],
        [
            jax.ShapeDtypeStruct((n, d), F32),
            jax.ShapeDtypeStruct((n, d), BF),
            jax.ShapeDtypeStruct((d, 128), BF),
            jax.ShapeDtypeStruct((d, 128), BF),
        ],
        [pltpu.VMEM((128, d), F32), pltpu.VMEM((128, d), F32)],
        flops=2 * n * d * d,
        moved=2 * d * d + 18 * n * d,
    )(gx, middle, cot, valid, gain, pack, pack, bt, adapter, att, inner)


def qkv_terms_body(gq_ref, gk_ref, gv_ref, x_ref, bt_ref, inner_ref, ad_ref, ig_ref, ta_ref, tb_ref):
    d = x_ref.shape[1]
    inner_t = inner_ref[...].T
    total = None
    for part, ref in enumerate((gq_ref, gk_ref, gv_ref)):
        g = ref[...]
        sl = slice(part * d, part * d + d)
        piece = mm(g, bt_ref[sl, :])
        total = piece if total is None else total + piece
        tb_ref[sl, :] = mm(inner_t, g).T.astype(BF)
    ig = (total * pick(ad_ref, x_ref.shape[0])).astype(BF)
    ig_ref[...] = ig
    ta_ref[...] = mm(ig.T, x_ref[...]).T.astype(BF)


def qkv_terms_call(gq, gk, gv, x, bt, inner, adapter):
    n, d = x.shape
    return call(
        qkv_terms_body,
        "qkv_terms",
        (1,),
        [whole(v.shape) for v in (gq, gk, gv, x, bt, inner, adapter)],
        [whole((n, 128)), whole((d, 128)), whole((3 * d, 128))],
        [
            jax.ShapeDtypeStruct((n, 128), BF),
            jax.ShapeDtypeStruct((d, 128), BF),
            jax.ShapeDtypeStruct((3 * d, 128), BF),
        ],
        flops=4 * n * d * 128 * 4,
        moved=10 * n * d,
    )(gq, gk, gv, x, bt, inner, adapter)


def qkv_back_rows(gq_ref, gk_ref, gv_ref, w_ref, ig_ref, a_ref, tok_ref, gain_ref, gm_ref, out_ref):
    d = tok_ref.shape[1]
    grad = mm_nt(gq_ref[...], w_ref[:, :d]) + mm_nt(gk_ref[...], w_ref[:, d : 2 * d])
    grad = grad + mm_nt(gv_ref[...], w_ref[:, 2 * d :]) + mm_nt(ig_ref[...], a_ref[...])
    unit, spread = stats(tok_ref[...].astype(F32))
    out_ref[...] = gm_ref[...] + normalize_back(grad, unit, spread, gain_ref[...])


def qkv_back_call(gq, gk, gv, pack, ig, tokens, gain, gm):
    n, d = tokens.shape
    step = 256
    row = pl.BlockSpec((step, d), lambda i: (i, 0))
    return call(
        qkv_back_rows,
        "qkv_back",
        (n // step,),
        [
            row,
            row,
            row,
            once((d, 3 * d), lambda i: (0, 0)),
            pl.BlockSpec((step, 128), lambda i: (i, 0)),
            once((d, 128), lambda i: (0, 3 * d // 128)),
            row,
            whole((1, d)),
            row,
        ],
        row,
        jax.ShapeDtypeStruct((n, d), F32),
        flops=6 * n * d * d,
        moved=6 * d * d + 18 * n * d,
    )(gq, gk, gv, pack, ig, pack, tokens, gain, gm)


def fold_rows(up_shard, rows):
    turned = up_shard.T
    pieces = turned.shape[0] // rows
    return jnp.concatenate([turned[i * rows : (i + 1) * rows] for i in range(pieces)], axis=1)


def unfold_rows(block, devices):
    rows = block.shape[0] // devices
    pieces = block.shape[1] // 128
    split = block.reshape(devices, rows, pieces, 128)
    return split.transpose(0, 2, 1, 3).reshape(-1, 128)


def gather_rows(packed):
    return lax.all_gather(packed, ("dp", "fsdp"), axis=0, tiled=True)


def halve(value, dim, axis, bit):
    size = lax.axis_size(axis)
    mine = (lax.axis_index(axis) >> bit) & 1
    send = lax.dynamic_index_in_dim(value, 1 - mine, dim, keepdims=False).astype(jnp.bfloat16)
    keep = lax.dynamic_index_in_dim(value, mine, dim, keepdims=False).astype(jnp.float32)
    got = lax.ppermute(send, axis, [(i, i ^ (1 << bit)) for i in range(size)])
    return keep + got.astype(jnp.float32)


def scatter_sum(stacked):
    dp_bits = lax.axis_size("dp").bit_length() - 1
    fs_bits = lax.axis_size("fsdp").bit_length() - 1
    rows = stacked.shape[1:]
    value = stacked.reshape((2,) * (dp_bits + fs_bits) + rows)
    names = [("dp", b) for b in reversed(range(dp_bits))] + [("fsdp", b) for b in reversed(range(fs_bits))]
    order = [("dp", 0)] + [("fsdp", b) for b in range(fs_bits)] + [("dp", b) for b in range(1, dp_bits)]
    for axis, bit in order:
        dim = names.index((axis, bit))
        names.pop(dim)
        value = halve(value, dim, axis, bit)
    return value


def local(
    tokens,
    cotangent,
    picture,
    adapter,
    patch_row,
    patch_col,
    qkv_weight,
    qkv_bias,
    proj_weight,
    proj_bias,
    fc1_weight,
    fc1_bias,
    fc2_weight,
    fc2_bias,
    norm1_gain,
    norm1_bias,
    norm2_gain,
    norm2_bias,
    qkv_down,
    qkv_up,
    proj_down,
    proj_up,
    fc1_down,
    fc1_up,
    fc2_down,
    fc2_up,
):
    devices = lax.axis_size(("dp", "fsdp"))
    rows = proj_weight.shape[0]
    width = proj_weight.shape[1]
    first = gather_rows(jnp.concatenate([qkv_weight, qkv_down, fold_rows(qkv_up, rows)], axis=1))
    second = gather_rows(
        jnp.concatenate(
            [
                fc1_weight,
                proj_weight,
                fc1_down,
                proj_down,
                fold_rows(proj_up, rows),
                fold_rows(fc1_up, rows),
                fold_rows(fc2_up, rows),
            ],
            axis=1,
        )
    )
    third = gather_rows(jnp.concatenate([fc2_weight, fc2_down], axis=1))
    q_cols = qkv_weight.shape[1]
    f_cols = fc1_weight.shape[1]
    base = f_cols + width
    bt_qkv = unfold_rows(first[:, q_cols + 128 :], devices)
    bt_proj = second[:, base + 256 : base + 384]
    bt_fc1 = unfold_rows(second[:, base + 384 : base + 384 + 4 * 128], devices)
    bt_fc2 = second[:, base + 384 + 4 * 128 :]
    row_count = tokens.shape[0]
    ad = adapter[:, None]
    valid = (picture >= 0).astype(F32)[:, None]
    cos_t, sin_t, qm, km = tables(picture, patch_row, patch_col)
    unit_one, _ = stats(tokens.astype(F32))
    normed = (unit_one * norm1_gain + norm1_bias).astype(BF)
    grad_low = (cotangent.astype(F32) * valid).astype(BF)
    qkv, inner_qkv = qkv_call(normed, first, bt_qkv, qkv_bias[None], ad, cos_t, sin_t)
    attended, lse = attend_call(qkv, qm, km)
    middle, normed_two, inner_proj = proj_call(
        attended, second, f_cols, base + 128, bt_proj, proj_bias[None], ad, tokens, norm2_gain[None], norm2_bias[None]
    )
    block_out, grad_two, ta_fc1, tb_fc1, ta_fc2, tb_fc2 = feed_call(
        normed_two, grad_low, second, base, bt_fc1, fc1_bias[None], third, bt_fc2, fc2_bias[None], ad, valid, middle
    )
    grad_middle, grad_att, ta_proj, tb_proj = proj_back_call(
        grad_two, middle, cotangent, valid, norm2_gain[None], second, f_cols, base + 128, bt_proj, ad, attended, inner_proj
    )
    gq, gk, gv = attend_back_call(qkv, grad_att, attended, lse, qm, km, cos_t, sin_t)
    ig_qkv, ta_qkv, tb_qkv = qkv_terms_call(gq, gk, gv, normed, bt_qkv, inner_qkv, ad)
    tokens_grad = qkv_back_call(gq, gk, gv, first, ig_qkv, tokens, norm1_gain[None], grad_middle)
    factor = 1.0 / math.sqrt(row_count * devices)

    def stack(terms):
        return jnp.concatenate([t.reshape(devices, -1, 128) for t in terms], axis=1)

    early = factor * scatter_sum(stack([ta_proj, tb_proj, ta_fc1, tb_fc1, ta_fc2, tb_fc2]))
    late = factor * scatter_sum(stack([ta_qkv, tb_qkv]))
    return (
        block_out,
        tokens_grad,
        late[:rows],
        late[rows:].T,
        early[:rows],
        early[rows : 2 * rows].T,
        early[2 * rows : 3 * rows],
        early[3 * rows : 7 * rows].T,
        early[7 * rows : 11 * rows],
        early[11 * rows :].T,
    )


def solution(mesh):
    return jax.shard_map(
        local,
        mesh=mesh,
        in_specs=(
            P(("dp", "fsdp"), None),
            P(("dp", "fsdp"), None),
            P(("dp", "fsdp")),
            P(("dp", "fsdp")),
            P(("dp", "fsdp")),
            P(("dp", "fsdp")),
            P(("dp", "fsdp"), None),
            P(),
            P(("dp", "fsdp"), None),
            P(),
            P(("dp", "fsdp"), None),
            P(),
            P(("dp", "fsdp"), None),
            P(),
            P(),
            P(),
            P(),
            P(),
            P(("dp", "fsdp"), None),
            P(None, ("dp", "fsdp")),
            P(("dp", "fsdp"), None),
            P(None, ("dp", "fsdp")),
            P(("dp", "fsdp"), None),
            P(None, ("dp", "fsdp")),
            P(("dp", "fsdp"), None),
            P(None, ("dp", "fsdp")),
        ),
        out_specs=(
            P(("dp", "fsdp"), None),
            P(("dp", "fsdp"), None),
            P(("dp", "fsdp"), None),
            P(None, ("dp", "fsdp")),
            P(("dp", "fsdp"), None),
            P(None, ("dp", "fsdp")),
            P(("dp", "fsdp"), None),
            P(None, ("dp", "fsdp")),
            P(("dp", "fsdp"), None),
            P(None, ("dp", "fsdp")),
        ),
        check_vma=False,
    )
```

```python
import functools
import math

import jax
import jax.numpy as jnp
from jax import lax
from jax.experimental import pallas as pl
from jax.experimental.pallas import tpu as pltpu
from jax.sharding import PartitionSpec as P

HEADS = 16
HD = 80
RANK = 16


EPS = 1e-06


BIG = 2.0**60
LOG2E = 1.4426950408889634
BF = jnp.bfloat16
F32 = jnp.float32


def normalize_back(grad_out, unit, spread, gain):
    scaled = grad_out * gain
    return spread * (
        scaled
        - jnp.mean(scaled, axis=-1, keepdims=True)
        - unit * jnp.mean(scaled * unit, axis=-1, keepdims=True)
    )


def rotary_tables(patch_row, patch_col, head_size):
    quarter = head_size // 4
    inverse = 1.0 / 10000.0 ** (jnp.arange(quarter, dtype=jnp.float32) * 2.0 / (head_size // 2))
    angles = jnp.concatenate(
        [
            patch_row.astype(jnp.float32)[:, None] * inverse,
            patch_col.astype(jnp.float32)[:, None] * inverse,
        ],
        axis=1,
    )
    angles = jnp.concatenate([angles, angles], axis=1)
    return (jnp.cos(angles), jnp.sin(angles))


def mm(left, right):
    return lax.dot_general(left, right, (((1,), (0,)), ((), ())), preferred_element_type=F32)


def mm_nt(left, right):
    return lax.dot_general(left, right, (((1,), (1,)), ((), ())), preferred_element_type=F32)


def call(body, name, grid, in_specs, out_specs, out_shape, scratch=(), flops=0, moved=0):
    return pl.pallas_call(
        body,
        name=name,
        grid=grid,
        in_specs=in_specs,
        out_specs=out_specs,
        out_shape=out_shape,
        scratch_shapes=scratch,
        cost_estimate=pl.CostEstimate(flops=flops, transcendentals=0, bytes_accessed=moved),
        compiler_params=pltpu.CompilerParams(
            dimension_semantics=("arbitrary",) * len(grid), vmem_limit_bytes=56 * 1024 * 1024
        ),
    )


def whole(shape):
    return pl.BlockSpec(shape, lambda *_: (0,) * len(shape))


def pick(adapter_ref, count):
    lanes = lax.broadcasted_iota(jnp.int32, (count, 128), 1) // RANK
    return (lanes == adapter_ref[...]).astype(F32)


def turn(values, low):
    size = values.shape[1]
    left = pltpu.roll(values, size - HD // 2, 1)
    right = pltpu.roll(values, HD // 2, 1)
    return jnp.where(low, left, right)


def qkv_body(x_ref, w_ref, a_ref, bt_ref, bias_ref, ad_ref, cos_ref, sin_ref, out_ref, inner_ref):
    part = pl.program_id(0)
    rows = x_ref.shape[0]
    step = 256

    @pl.when(part == 0)
    def _():
        inner_ref[...] = (mm(x_ref[...], a_ref[...]) * pick(ad_ref, rows)).astype(BF)

    def one(start, rotated):
        sl = pl.ds(start, step)
        y = mm(x_ref[sl, :], w_ref[...]) + mm_nt(inner_ref[sl, :], bt_ref[...]) + bias_ref[...]
        if rotated:
            low = lax.broadcasted_iota(jnp.int32, (step, 640), 1) % HD < HD // 2
            for begin in (0, 640):
                piece = y[:, begin : begin + 640]
                done = piece * cos_ref[sl, :] + turn(piece, low) * sin_ref[sl, :]
                out_ref[sl, begin : begin + 640] = done.astype(BF)
        else:
            out_ref[sl, :] = y.astype(BF)

    @pl.when(part < 2)
    def _():
        for i in range(0, rows, step):
            one(i, True)

    @pl.when(part == 2)
    def _():
        for i in range(0, rows, step):
            one(i, False)


def qkv_call(x, pack, bt, bias, adapter, cos_t, sin_t):
    n, d = x.shape
    return call(
        qkv_body,
        "qkv_rotary",
        (3,),
        [
            whole((n, d)),
            pl.BlockSpec((d, d), lambda j: (0, j)),
            pl.BlockSpec((d, 128), lambda j: (0, 3 * d // 128)),
            pl.BlockSpec((d, 128), lambda j: (j, 0)),
            pl.BlockSpec((1, d), lambda j: (0, j)),
            whole((n, 1)),
            whole((n, 640)),
            whole((n, 640)),
        ],
        [pl.BlockSpec((n, d), lambda j: (0, j)), whole((n, 128))],
        [jax.ShapeDtypeStruct((n, 3 * d), BF), jax.ShapeDtypeStruct((n, 128), BF)],
        flops=2 * n * d * 3 * d,
        moved=8 * d * d + 12 * n * d,
    )(x, pack, pack, bt, bias, adapter, cos_t, sin_t)


def attend_body(q_ref, k_ref, v_ref, qm_ref, km_ref, out_ref, lse_ref):
    rows = q_ref.shape[0]
    step = 256
    factor = LOG2E / math.sqrt(HD)
    lanes = lax.broadcasted_iota(jnp.int32, (step, 128), 1)
    for i in range(0, rows, step):
        lse_ref[i : i + step, :] = jnp.zeros((step, 128), F32)
    for h in range(8):
        cols = slice(HD * h, HD * h + HD)
        keys = jnp.concatenate([k_ref[:, cols], km_ref[...]], axis=1)
        vals = v_ref[:, cols]
        for i in range(0, rows, step):
            query = jnp.concatenate([q_ref[i : i + step, cols], qm_ref[i : i + step, :]], axis=1)
            s = mm_nt(query, keys)
            top = jnp.max(s, axis=1, keepdims=True)
            e = jnp.exp2((s - top) * factor)
            total = jnp.sum(e, axis=1, keepdims=True)
            o = mm(e.astype(BF), vals) * (1.0 / total)
            out_ref[i : i + step, cols] = o.astype(BF)
            lse = top + jnp.log(total) * math.sqrt(HD)
            lse_ref[i : i + step, :] = jnp.where(lanes == h, lse, lse_ref[i : i + step, :])


def attend_call(qkv, qm, km):
    n = qkv.shape[0]
    d = qkv.shape[1] // 3
    groups = d // 640
    return call(
        attend_body,
        "attend",
        (groups,),
        [
            pl.BlockSpec((n, 640), lambda g: (0, g)),
            pl.BlockSpec((n, 640), lambda g: (0, groups + g)),
            pl.BlockSpec((n, 640), lambda g: (0, 2 * groups + g)),
            whole((n, 48)),
            whole((n, 48)),
        ],
        [pl.BlockSpec((n, 640), lambda g: (0, g)), pl.BlockSpec((n, 128), lambda g: (0, g))],
        [jax.ShapeDtypeStruct((n, d), BF), jax.ShapeDtypeStruct((n, 128 * groups), F32)],
        flops=4 * n * n * d,
        moved=8 * n * d,
    )(qkv, qkv, qkv, qm, km)


def split_low(values, count):
    parts = []
    for _ in range(count):
        part = values.astype(BF)
        parts.append(part)
        values = values - part.astype(F32)
    return parts


def attend_back_body(
    q_ref, k_ref, v_ref, g_ref, o_ref, lse_ref, qm_ref, km_ref, cos_ref, sin_ref,
    *rest,
):
    dq_ref, dk_ref, dv_ref, dq_s, dk_s = rest[-5:]
    rows = q_ref.shape[0]
    step = 256
    factor = LOG2E / math.sqrt(HD)
    scale = 1.0 / math.sqrt(HD)
    lanes = lax.broadcasted_iota(jnp.int32, (rows, 48), 1)
    ones_two = jnp.where((lanes == 16) | (lanes == 17), 1.0, 0.0).astype(BF)
    for h in range(8):
        cols = slice(HD * h, HD * h + HD)
        gh = g_ref[:, cols]
        delta = jnp.sum(gh.astype(F32) * o_ref[:, cols].astype(F32), axis=1, keepdims=True)
        d_hi, d_lo = split_low(-delta, 2)
        l_hi, l_mid, l_lo = split_low(-lse_ref[:, h : h + 1], 3)
        q_aug = jnp.where(
            lanes == 16,
            l_hi.astype(F32),
            jnp.where(
                lanes == 17,
                l_mid.astype(F32),
                jnp.where(lanes == 18, l_lo.astype(F32), qm_ref[...].astype(F32)),
            ),
        ).astype(BF)
        g_aug = jnp.where(
            lanes == 16, d_hi.astype(F32), jnp.where(lanes == 17, d_lo.astype(F32), 0.0)
        ).astype(BF)
        query = jnp.concatenate([q_ref[:, cols], q_aug], axis=1)
        grads = jnp.concatenate([gh, g_aug], axis=1)
        keys = jnp.concatenate([k_ref[:, cols], km_ref[...]], axis=1)
        vals = jnp.concatenate([v_ref[:, cols], ones_two], axis=1)
        keys_t = keys.T
        dk = jnp.zeros((rows, 128), F32)
        dv = jnp.zeros((rows, 128), F32)
        for i in range(0, rows, step):
            qb = query[i : i + step, :]
            gb = grads[i : i + step, :]
            p = jnp.exp2(mm_nt(keys, qb) * factor)
            dp = mm_nt(vals, gb)
            ds = (p * dp).astype(BF)
            dv = dv + mm(p.astype(BF), gb)
            dk = dk + mm(ds, qb)
            dq = mm(keys_t, ds)
            dq_s[i : i + step, cols] = dq.T[:, :HD]
        dk_s[:, cols] = dk[:, :HD]
        dv_ref[:, cols] = dv[:, :HD].astype(BF)
    low = lax.broadcasted_iota(jnp.int32, (step, 640), 1) % HD < HD // 2
    for i in range(0, rows, step):
        sl = slice(i, i + step)
        for src, dst in ((dq_s, dq_ref), (dk_s, dk_ref)):
            piece = src[sl, :] * scale
            dst[sl, :] = (piece * cos_ref[sl, :] - turn(piece, low) * sin_ref[sl, :]).astype(BF)


def attend_back_call(qkv, grads, attended, lse, qm, km, cos_t, sin_t, group, earlier):
    n = qkv.shape[0]
    d = qkv.shape[1] // 3
    groups = d // 640
    block = pl.BlockSpec((n, 640), lambda g: (0, group))
    kept = [pl.BlockSpec(memory_space=pl.ANY)] * len(earlier)
    return pl.pallas_call(
        attend_back_body,
        name="attend_back",
        grid=(1,),
        in_specs=[
            block,
            pl.BlockSpec((n, 640), lambda g: (0, groups + group)),
            pl.BlockSpec((n, 640), lambda g: (0, 2 * groups + group)),
            block,
            block,
            pl.BlockSpec((n, 128), lambda g: (0, group)),
            whole((n, 48)),
            whole((n, 48)),
            whole((n, 640)),
            whole((n, 640)),
        ]
        + kept,
        out_specs=[block, block, block],
        out_shape=[jax.ShapeDtypeStruct((n, d), BF)] * 3,
        scratch_shapes=[pltpu.VMEM((n, 640), F32), pltpu.VMEM((n, 640), F32)],
        input_output_aliases={10 + i: i for i in range(len(earlier))},
        cost_estimate=pl.CostEstimate(flops=5 * n * n * d, transcendentals=0, bytes_accessed=8 * n * d),
        compiler_params=pltpu.CompilerParams(
            dimension_semantics=("arbitrary",), vmem_limit_bytes=56 * 1024 * 1024
        ),
    )(qkv, qkv, qkv, grads, attended, lse, qm, km, cos_t, sin_t, *earlier)


def tables(picture, patch_row, patch_col):
    cosine, sine = rotary_tables(patch_row, patch_col, HD)
    half = HD // 2
    signed = jnp.concatenate([-sine[:, :half], sine[:, half:]], axis=1)
    count = picture.shape[0]
    change = (picture[1:] != picture[:-1]).astype(jnp.int32)
    places = lax.broadcasted_iota(jnp.int32, (count, count - 1), 0)
    before = lax.broadcasted_iota(jnp.int32, (count, count - 1), 1) < places
    index = jnp.sum(jnp.where(before, change[None, :], 0), axis=1)
    lanes = lax.broadcasted_iota(jnp.int32, (1, 48), 1)
    own = lanes == index[:, None]
    qm = jnp.where(own | (lanes >= 16), 0.0, -BIG).astype(BF)
    km = (own | ((lanes >= 16) & (lanes < 19))).astype(BF)
    return (*widen_call(cosine, signed), qm, km)


def stats(values):
    centre = jnp.mean(values, axis=-1, keepdims=True)
    centred = values - centre
    spread = lax.rsqrt(jnp.mean(centred * centred, axis=-1, keepdims=True) + EPS)
    return centred * spread, spread


def once(shape, index):
    return pl.BlockSpec(shape, index, pipeline_mode=pl.Buffered(1))


def proj_body(
    att_ref, w_ref, a_ref, bt_ref, bias_ref, ad_ref, tok_ref, gain_ref, shift_ref,
    mid_ref, norm_ref, inner_ref,
):
    rows = att_ref.shape[0]
    x = att_ref[...]
    inner = (mm(x, a_ref[...]) * pick(ad_ref, rows)).astype(BF)
    inner_ref[...] = inner
    middle = tok_ref[...].astype(F32) + (mm(x, w_ref[...]) + bias_ref[...] + mm_nt(inner, bt_ref[...]))
    mid_ref[...] = middle
    unit, _ = stats(middle)
    norm_ref[...] = (unit * gain_ref[...] + shift_ref[...]).astype(BF)


def proj_call(att, pack, first_col, a_col, bt_col, bias, adapter, tokens, gain, shift):
    n, d = att.shape
    step = 256
    row = pl.BlockSpec((step, d), lambda i: (i, 0))
    return call(
        proj_body,
        "proj_norm",
        (n // step,),
        [
            row,
            once((d, d), lambda i: (0, first_col // d)),
            once((d, 128), lambda i: (0, a_col // 128)),
            once((d, 128), lambda i: (0, bt_col // 128)),
            whole((1, d)),
            pl.BlockSpec((step, 1), lambda i: (i, 0)),
            row,
            whole((1, d)),
            whole((1, d)),
        ],
        [row, row, pl.BlockSpec((step, 128), lambda i: (i, 0))],
        [
            jax.ShapeDtypeStruct((n, d), F32),
            jax.ShapeDtypeStruct((n, d), BF),
            jax.ShapeDtypeStruct((n, 128), BF),
        ],
        flops=2 * n * d * d,
        moved=2 * d * d + 10 * n * d,
    )(att, pack, pack, pack, bias, adapter, tokens, gain, shift)


def feed_body(*refs, parts, first, last):
    refs = list(refs)
    take = lambda count: [refs.pop(0) for _ in range(count)]
    x_ref, g_ref = take(2)
    w1, w2, bt1, a2, b1 = take(parts), take(parts), take(parts), take(parts), take(parts)
    ad_ref, a1_ref, bt2_ref = take(3)
    if first:
        base_ref, b2_ref = take(2)
    else:
        base_ref, gx_in, in1_ref, ig2_ref, in2_in, ig1_in = take(6)
        val_ref = take(1)[0]
    if first:
        acc_ref, gx_ref, in1_out, ig2_out, in2_out, ig1_out = take(6)
    if last:
        out_ref, gx_ref, ta1_ref, tb2_ref = take(4)
    ta2, tb1 = take(parts), take(parts)
    if last:
        ta1_s, tb2_s = take(2)
    ta2_s, tb1_s = take(parts), take(parts)
    sums = ta2_s + tb1_s + ([ta1_s, tb2_s] if last else [])
    i = pl.program_id(0)
    end = i == pl.num_programs(0) - 1

    @pl.when(i == 0)
    def _():
        for ref in sums:
            ref[...] = jnp.zeros_like(ref)

    sub = 256 if first else 512
    for begin in range(0, x_ref.shape[0], sub):
        sl = pl.ds(begin, sub)
        x = x_ref[sl, :]
        g = g_ref[sl, :]
        sel = pick(ad_ref.at[sl, :], sub)
        if first:
            in1 = (mm(x, a1_ref[...]) * sel).astype(BF)
            ig2 = (mm(g, bt2_ref[...]) * sel).astype(BF)
            in1_out[sl, :] = in1
            ig2_out[sl, :] = ig2
            acc = base_ref[sl, :] + b2_ref[...]
            gx = in2 = ig1 = None
        else:
            in1 = in1_ref[sl, :]
            ig2 = ig2_ref[sl, :]
            acc, gx, in2, ig1 = base_ref[sl, :], gx_in[sl, :], in2_in[sl, :], ig1_in[sl, :]
        in1_t = in1.T
        ig2_t = ig2.T
        for q in range(parts):
            h = mm(x, w1[q][...]) + mm_nt(in1, bt1[q][...]) + b1[q][...]
            ga = mm_nt(g, w2[q][...]) + mm_nt(ig2, a2[q][...])
            s = 0.5 * jnp.tanh(0.851 * h) + 0.5
            act = (h * s).astype(BF)
            gh = (ga * (s + 1.702 * h * s * (1.0 - s))).astype(BF)
            more = (mm_nt(gh, w1[q][...]), mm(act, a2[q][...]), mm(gh, bt1[q][...]))
            acc = acc + mm(act, w2[q][...])
            gx, in2, ig1 = more if gx is None else (gx + more[0], in2 + more[1], ig1 + more[2])
            ta2_s[q][...] += mm(ig2_t, act)
            tb1_s[q][...] += mm(in1_t, gh)
        if last:
            low2 = (in2 * sel).astype(BF)
            low1 = (ig1 * sel).astype(BF)
            out_ref[sl, :] = ((acc + mm_nt(low2, bt2_ref[...])) * val_ref[sl, :]).astype(BF)
            gx_ref[sl, :] = gx + mm_nt(low1, a1_ref[...])
            ta1_s[...] += mm(low1.T, x)
            tb2_s[...] += mm(low2.T, g)
        else:
            acc_ref[sl, :] = acc
            gx_ref[sl, :] = gx
            in2_out[sl, :] = in2
            ig1_out[sl, :] = ig1

    @pl.when(end)
    def _():
        for q in range(parts):
            ta2[q][...] = ta2_s[q][...].T.astype(BF)
            tb1[q][...] = tb1_s[q][...].T.astype(BF)
        if last:
            ta1_ref[...] = ta1_s[...].T.astype(BF)
            tb2_ref[...] = tb2_s[...].T.astype(BF)


def feed_call(x, grads, w2, w1, bt1, a2, b1, adapter, a1, bt2, state, first, last):
    n, d = x.shape
    parts = len(w1)
    step = 512
    row = pl.BlockSpec((step, d), lambda i: (i, 0))
    thin_row = pl.BlockSpec((step, 128), lambda i: (i, 0))
    one = pl.BlockSpec((step, 1), lambda i: (i, 0))
    thin = once((d, 128), lambda i: (0, 0))
    line = once((1, d), lambda i: (0, 0))

    def wide(col):
        return once((d, d), lambda i: (0, col // d))

    def narrow(col):
        return once((d, 128), lambda i: (0, col // 128))

    in_specs = [row, row] + [wide(c) for _, c in w1] + [wide(c) for _, c in w2]
    in_specs += [narrow(c) for _, c in bt1] + [narrow(c) for _, c in a2] + [line] * parts
    in_specs += [one, narrow(a1[1]), narrow(bt2[1])]
    args = [x, grads] + [v for v, _ in w1 + w2 + bt1 + a2] + list(b1) + [adapter, a1[0], bt2[0]]
    if first:
        in_specs += [row, line]
    else:
        in_specs += [row, row, thin_row, thin_row, thin_row, thin_row, one]
    args += list(state)
    out_specs, out_shape, scratch = [], [], []
    if first:
        out_specs += [row, row, thin_row, thin_row, thin_row, thin_row]
        out_shape += [jax.ShapeDtypeStruct((n, d), F32)] * 2
        out_shape += [jax.ShapeDtypeStruct((n, 128), BF)] * 2 + [jax.ShapeDtypeStruct((n, 128), F32)] * 2
    if last:
        out_specs += [row, row, thin, thin]
        out_shape += [jax.ShapeDtypeStruct((n, d), BF), jax.ShapeDtypeStruct((n, d), F32)]
        out_shape += [jax.ShapeDtypeStruct((d, 128), BF)] * 2
        scratch += [pltpu.VMEM((128, d), F32)] * 2
    out_specs += [thin] * (2 * parts)
    out_shape += [jax.ShapeDtypeStruct((d, 128), BF)] * (2 * parts)
    scratch += [pltpu.VMEM((128, d), F32)] * (2 * parts)
    return call(
        functools.partial(feed_body, parts=parts, first=first, last=last),
        "feed_first" if first else "feed_last",
        (n // step,),
        in_specs,
        out_specs,
        out_shape,
        scratch,
        flops=8 * n * d * d * parts,
        moved=4 * d * d * parts + 24 * n * d,
    )(*args)


def proj_back_body(
    gx_ref, mid_ref, cot_ref, val_ref, gain_ref, w_ref, a_ref, bt_ref, ad_ref, att_ref, inner_ref,
    gm_ref, ga_ref, ta_ref, tb_ref, ta_s, tb_s,
):
    i = pl.program_id(0)
    rows = gx_ref.shape[0]
    unit, spread = stats(mid_ref[...])
    gm = cot_ref[...].astype(F32) * val_ref[...] + normalize_back(gx_ref[...], unit, spread, gain_ref[...])
    gm_ref[...] = gm
    gb = gm.astype(BF)
    ig = (mm(gb, bt_ref[...]) * pick(ad_ref, rows)).astype(BF)
    ga_ref[...] = (mm_nt(gb, w_ref[...]) + mm_nt(ig, a_ref[...])).astype(BF)
    ta = mm(ig.T, att_ref[...])
    tb = mm(inner_ref[...].T, gb)

    @pl.when(i == 0)
    def _():
        ta_s[...] = ta
        tb_s[...] = tb

    @pl.when(i > 0)
    def _():
        ta_s[...] += ta
        tb_s[...] += tb

    @pl.when(i == pl.num_programs(0) - 1)
    def _():
        ta_ref[...] = ta_s[...].T.astype(BF)
        tb_ref[...] = tb_s[...].T.astype(BF)


def proj_back_call(gx, middle, cot, valid, gain, pack, first_col, a_col, bt_col, adapter, att, inner):
    n, d = gx.shape
    step = 256
    row = pl.BlockSpec((step, d), lambda i: (i, 0))
    one = pl.BlockSpec((step, 1), lambda i: (i, 0))
    thin = once((d, 128), lambda i: (0, 0))
    return call(
        proj_back_body,
        "proj_back",
        (n // step,),
        [
            row,
            row,
            row,
            one,
            whole((1, d)),
            once((d, d), lambda i: (0, first_col // d)),
            once((d, 128), lambda i: (0, a_col // 128)),
            once((d, 128), lambda i: (0, bt_col // 128)),
            one,
            row,
            pl.BlockSpec((step, 128), lambda i: (i, 0)),
        ],
        [row, row, thin, thin],
        [
            jax.ShapeDtypeStruct((n, d), F32),
            jax.ShapeDtypeStruct((n, d), BF),
            jax.ShapeDtypeStruct((d, 128), BF),
            jax.ShapeDtypeStruct((d, 128), BF),
        ],
        [pltpu.VMEM((128, d), F32), pltpu.VMEM((128, d), F32)],
        flops=2 * n * d * d,
        moved=2 * d * d + 18 * n * d,
    )(gx, middle, cot, valid, gain, pack, pack, pack, adapter, att, inner)


def qkv_terms_body(gq_ref, gk_ref, gv_ref, x_ref, bt_ref, inner_ref, ad_ref, ig_ref, ta_ref, tb_ref):
    d = x_ref.shape[1]
    inner_t = inner_ref[...].T
    total = None
    for part, ref in enumerate((gq_ref, gk_ref, gv_ref)):
        g = ref[...]
        sl = slice(part * d, part * d + d)
        piece = mm(g, bt_ref[sl, :])
        total = piece if total is None else total + piece
        tb_ref[sl, :] = mm(inner_t, g).T.astype(BF)
    ig = (total * pick(ad_ref, x_ref.shape[0])).astype(BF)
    ig_ref[...] = ig
    ta_ref[...] = mm(ig.T, x_ref[...]).T.astype(BF)


def qkv_terms_call(gq, gk, gv, x, bt, inner, adapter):
    n, d = x.shape
    return call(
        qkv_terms_body,
        "qkv_terms",
        (1,),
        [whole(v.shape) for v in (gq, gk, gv, x, bt, inner, adapter)],
        [whole((n, 128)), whole((d, 128)), whole((3 * d, 128))],
        [
            jax.ShapeDtypeStruct((n, 128), BF),
            jax.ShapeDtypeStruct((d, 128), BF),
            jax.ShapeDtypeStruct((3 * d, 128), BF),
        ],
        flops=4 * n * d * 128 * 4,
        moved=10 * n * d,
    )(gq, gk, gv, x, bt, inner, adapter)


def qkv_back_rows(gq_ref, gk_ref, gv_ref, w_ref, ig_ref, a_ref, tok_ref, gain_ref, gm_ref, out_ref):
    d = tok_ref.shape[1]
    grad = mm_nt(gq_ref[...], w_ref[:, :d]) + mm_nt(gk_ref[...], w_ref[:, d : 2 * d])
    grad = grad + mm_nt(gv_ref[...], w_ref[:, 2 * d :]) + mm_nt(ig_ref[...], a_ref[...])
    unit, spread = stats(tok_ref[...].astype(F32))
    out_ref[...] = gm_ref[...] + normalize_back(grad, unit, spread, gain_ref[...])


def qkv_back_call(gq, gk, gv, pack, ig, tokens, gain, gm, half):
    n, d = tokens.shape
    step = 256
    steps = n // step // 2
    row = pl.BlockSpec((step, d), lambda i: (half * steps + i, 0))
    return pl.pallas_call(
        qkv_back_rows,
        name="qkv_back",
        grid=(steps,),
        in_specs=[
            row,
            row,
            row,
            once((d, 3 * d), lambda i: (0, 0)),
            pl.BlockSpec((step, 128), lambda i: (half * steps + i, 0)),
            once((d, 128), lambda i: (0, 3 * d // 128)),
            row,
            whole((1, d)),
            row,
        ],
        out_specs=row,
        out_shape=jax.ShapeDtypeStruct((n, d), F32),
        input_output_aliases={8: 0},
        cost_estimate=pl.CostEstimate(flops=3 * n * d * d, transcendentals=0, bytes_accessed=6 * d * d + 9 * n * d),
        compiler_params=pltpu.CompilerParams(
            dimension_semantics=("arbitrary",), vmem_limit_bytes=56 * 1024 * 1024
        ),
    )(gq, gk, gv, pack, ig, pack, tokens, gain, gm)


def unfold_rows(block, devices):
    rows = block.shape[0] // devices
    pieces = block.shape[1] // 128
    split = block.reshape(devices, rows, pieces, 128)
    return split.transpose(0, 2, 1, 3).reshape(-1, 128)


def gather_rows(packed):
    return lax.all_gather(packed, ("dp", "fsdp"), axis=0, tiled=True)


def place_body(table_ref, *refs, pieces):
    out_ref = refs[-1]
    mask = table_ref[2]
    begin = 0
    for ref in refs[:pieces]:
        end = begin + ref.shape[-1]
        for k in range(ref.shape[1]):
            out_ref[mask ^ k, 0, 0, :, begin:end] = ref[0, k]
        begin = end


class Gather:
    def __init__(self, *parts):
        self.zs, self.fs = lax.axis_size("dp") // 2, lax.axis_size("fsdp")
        self.rows, self.cols = parts[0].shape[0], sum(p.shape[1] for p in parts)
        self.parts = list(parts)
        self.phase = 0

    def swap(self, value, axis, mask):
        return lax.ppermute(value, axis, [(i, i ^ mask) for i in range(lax.axis_size(axis))])

    def start(self):
        z_masks, f_masks = list(range(2, 2 * self.zs, 2)), list(range(1, self.fs))
        orders = [[("dp", z_masks), ("fsdp", f_masks)], [("fsdp", f_masks), ("dp", z_masks)]]
        self.got = []
        for part, order in zip(self.parts, orders):
            axis, masks = order[self.phase] if self.phase < 2 else ("dp", [1])
            self.got.append([part] + [self.swap(part, axis, m) for m in masks])

    def finish(self, *others):
        sizes = [len(group) for group in self.got]
        held = lax.optimization_barrier(tuple(v for group in self.got for v in group) + others)
        groups, at = [], 0
        for size in sizes:
            groups.append(held[at : at + size])
            at += size
        if self.phase == 0:
            self.parts = [jnp.stack(group) for group in groups]
        elif self.phase == 1:
            self.parts = [jnp.stack(group, axis=1 if i else 0) for i, group in enumerate(groups)]
        if self.phase < 2:
            held = lax.optimization_barrier(tuple(self.parts) + tuple(held[at:]))
            self.parts = list(held[: len(sizes)])
            at = len(sizes)
        else:
            self.far = [group[1] for group in groups[::-1]]
        self.phase += 1
        return held[at:]

    def place(self, side, earlier):
        zs, fs, rows, cols = self.zs, self.fs, self.rows, self.cols
        spot, column = lax.axis_index("dp"), lax.axis_index("fsdp")
        table = jnp.stack([(spot & 1) ^ side, column, spot >> 1]).astype(jnp.int32)
        parts = self.far if side else self.parts[::-1]
        specs = [pl.BlockSpec((1, zs, rows, p.shape[-1]), lambda m, t: (m, 0, 0, 0)) for p in parts]
        specs += [pl.BlockSpec(memory_space=pl.ANY)] * len(earlier)
        return pl.pallas_call(
            functools.partial(place_body, pieces=len(parts)),
            name="place_blocks",
            grid_spec=pltpu.PrefetchScalarGridSpec(
                num_scalar_prefetch=1,
                grid=(fs,),
                in_specs=specs,
                out_specs=pl.BlockSpec((zs, 1, 1, rows, cols), lambda m, t: (0, t[0], t[1] ^ m, 0, 0)),
            ),
            out_shape=jax.ShapeDtypeStruct((zs, 2, fs, rows, cols), BF),
            input_output_aliases={1 + len(parts): 0} if earlier else {},
            cost_estimate=pl.CostEstimate(flops=0, transcendentals=0, bytes_accessed=4 * zs * fs * rows * cols),
            compiler_params=pltpu.CompilerParams(vmem_limit_bytes=48 * 1024 * 1024),
        )(table, *parts, *earlier)


def widen_body(cos_ref, sin_ref, cos_out, sin_out):
    for src, dst in ((cos_ref, cos_out), (sin_ref, sin_out)):
        value = src[...]
        dst[...] = jnp.concatenate([value] * 8, axis=1)


def widen_call(cosine, signed):
    n = cosine.shape[0]
    out = jax.ShapeDtypeStruct((n, 8 * HD), F32)
    specs = [whole((n, 8 * HD))] * 2
    return call(widen_body, "widen_tables", (1,), [whole(cosine.shape)] * 2, specs, [out, out], moved=72 * n * HD)(
        cosine, signed
    )


def pack_body(
    qkv_w, proj_w, fc1_w, fc2_w, qkv_a, proj_a, fc1_a, fc2_a, qkv_b, proj_b, fc1_b, fc2_b, *outs, devices, cut, groups
):
    rows, d = proj_w.shape
    quarters = fc1_w.shape[1] // d

    def turned(ref):
        flipped = ref[...].astype(F32).T
        return [flipped[i * rows : (i + 1) * rows].astype(BF) for i in range(flipped.shape[0] // rows)]

    def fill(out, pieces):
        at = 0
        for piece in pieces:
            out[:, at : at + piece.shape[1]] = piece
            at += piece.shape[1]

    fill(outs[1], [qkv_w[:, :cut]])
    fill(outs[0], [qkv_w[:, cut:], qkv_a[...]] + turned(qkv_b))
    up1 = turned(fc1_b)
    for out, group in zip(outs[2:], groups):
        pieces = [fc2_w[q * rows : (q + 1) * rows, :] for q in group]
        for q in group:
            starts = [(i * quarters + q) * rows for i in range(devices)]
            pieces.append(jnp.concatenate([fc1_w[:, c : c + rows] for c in starts], axis=1))
        if group[0] == 0:
            pieces.append(proj_w[...])
        pieces += [up1[q] for q in group]
        pieces += [fc2_a[q * rows : (q + 1) * rows, :] for q in group]
        if group[0] == 0:
            pieces += [fc1_a[...], proj_a[...]] + turned(proj_b) + turned(fc2_b)
        fill(out, pieces)


def pack_call(arrays, devices, groups):
    rows, d = arrays[1].shape
    total = arrays[0].shape[1] + 4 * 128
    cut = total // 128 // 3 * 128
    widths = [total - cut, cut] + [len(g) * (2 * d + 256) + (d + 512 if g[0] == 0 else 0) for g in groups]
    return call(
        functools.partial(pack_body, devices=devices, cut=cut, groups=groups),
        "pack_shards",
        (1,),
        [whole(v.shape) for v in arrays],
        [whole((rows, w)) for w in widths],
        [jax.ShapeDtypeStruct((rows, w), BF) for w in widths],
        moved=4 * rows * sum(widths),
    )(*arrays)


class Scatter:
    def __init__(self, stacked):
        zs, fs = lax.axis_size("dp") // 2, lax.axis_size("fsdp")
        self.value = stacked.reshape((zs, 2, fs) + stacked.shape[1:])
        self.phases = [("dp", 1, [1], 1), ("fsdp", 1, list(range(1, fs)), 0), ("dp", 0, list(range(2, 2 * zs, 2)), 1)]
        self.open = None

    def start(self):
        axis, dim, masks, shift = self.phases.pop(0)
        size = lax.axis_size(axis)
        place = lax.axis_index(axis)
        if dim == 1 and axis == "dp":
            place, spots = place & 1, [(m, 1) for m in masks]
        else:
            place, spots = place >> shift, [(m, m >> shift) for m in masks]
        pick_one = lambda at: lax.dynamic_index_in_dim(self.value, at, dim, keepdims=False)
        pieces = [pick_one(place)]
        for mask, off in spots:
            send = pick_one(place ^ off).astype(BF)
            pieces.append(lax.ppermute(send, axis, [(i, i ^ mask) for i in range(size)]))
        self.open = pieces

    def finish(self, *others):
        total = self.open[0].astype(F32)
        for piece in self.open[1:]:
            total = total + piece.astype(F32)
        held = lax.optimization_barrier((total,) + others)
        self.value = held[0]
        return held[1:]


def local(
    tokens,
    cotangent,
    picture,
    adapter,
    patch_row,
    patch_col,
    qkv_weight,
    qkv_bias,
    proj_weight,
    proj_bias,
    fc1_weight,
    fc1_bias,
    fc2_weight,
    fc2_bias,
    norm1_gain,
    norm1_bias,
    norm2_gain,
    norm2_bias,
    qkv_down,
    qkv_up,
    proj_down,
    proj_up,
    fc1_down,
    fc1_up,
    fc2_down,
    fc2_up,
):
    devices = lax.axis_size(("dp", "fsdp"))
    rows, d = proj_weight.shape
    quarters = fc1_weight.shape[1] // d
    q_cols = qkv_weight.shape[1]
    groups = [list(range(quarters // 2)), list(range(quarters // 2, quarters))]
    shards = (qkv_weight, proj_weight, fc1_weight, fc2_weight, qkv_down, proj_down, fc1_down, fc2_down)
    shards += (qkv_up, proj_up, fc1_up, fc2_up)
    part_b, part_a, pack_a, pack_b = pack_call(shards, devices, groups)
    one = Gather(part_b, part_a)
    one.start()

    def spots(source, count, extra):
        wide = [(source, q * d) for q in range(2 * count)]
        base = (2 * count + extra) * d
        thin = [(source, base + q * 128) for q in range(2 * count)]
        return [wide[:count], wide[count:], thin[:count], thin[count:]]

    count = len(groups[0])
    row_count = tokens.shape[0]
    unit_one, _ = stats(tokens.astype(F32))
    normed = (unit_one * norm1_gain + norm1_bias).astype(BF)
    (normed,) = one.finish(normed)
    second = gather_rows(pack_a)
    third = gather_rows(pack_b)
    proj_col = 2 * count * d
    a1_col = proj_col + d + 2 * count * 128
    ap_col, btp_col, bt2_col = a1_col + 128, a1_col + 256, a1_col + 384
    one.start()
    ad = adapter[:, None]
    valid = (picture >= 0).astype(F32)[:, None]
    grad_low = (cotangent.astype(F32) * valid).astype(BF)
    bias1 = fc1_bias.reshape(devices, quarters, rows).transpose(1, 0, 2).reshape(quarters, 1, d)
    small = [qkv_bias[None], proj_bias[None], norm1_gain[None], norm2_gain[None], norm2_bias[None], fc2_bias[None]]
    small += [bias1[q] for q in range(quarters)] + [ad, valid, grad_low, *tables(picture, patch_row, patch_col)]
    small = one.finish(*small)
    bias_qkv, bias_proj, gain1, gain2, shift2, bias2, *bias1 = small[: 6 + quarters]
    ad, valid, grad_low, cos_t, sin_t, qm, km = small[6 + quarters :]
    one.start()
    first = one.place(0, ())
    (first,) = one.finish(first)
    first = one.place(1, (first,)).reshape(devices * rows, -1)
    bt_qkv = unfold_rows(first[:, q_cols + 128 :], devices)
    qkv, inner_qkv = qkv_call(normed, first, bt_qkv, bias_qkv, ad, cos_t, sin_t)
    attended, lse = attend_call(qkv, qm, km)
    middle, normed_two, inner_proj = proj_call(
        attended, second, proj_col, ap_col, btp_col, bias_proj, ad, tokens, gain2, shift2
    )
    a1, bt2 = (second, a1_col), (second, bt2_col)
    early = spots(second, count, 1)
    final = spots(third, quarters - count, 0)
    acc, grad_x, in1, ig2, in2, ig1, *terms_a = feed_call(
        normed_two, grad_low, *early, bias1[:count], ad, a1, bt2, (middle, bias2), True, False
    )
    na, nb = count, quarters - count
    state = (acc, grad_x, in1, ig2, in2, ig1, valid)
    block_out, grad_two, ta_fc1, tb_fc2, *terms_b = feed_call(
        normed_two, grad_low, *final, bias1[count:], ad, a1, bt2, state, False, True
    )

    def stack(terms):
        return jnp.concatenate([t.reshape(devices, -1, 128) for t in terms], axis=1)

    feed_sum = Scatter(
        stack([ta_fc1, *terms_a[na:], *terms_b[nb:], *terms_a[:na], *terms_b[:nb], tb_fc2])
    )
    feed_sum.start()
    grad_middle, grad_att, ta_proj, tb_proj = proj_back_call(
        grad_two, middle, cotangent, valid, gain2, second, proj_col, ap_col, btp_col, ad, attended, inner_proj
    )
    (grad_att,) = feed_sum.finish(grad_att)
    feed_sum.start()
    halves = attend_back_call(qkv, grad_att, attended, lse, qm, km, cos_t, sin_t, 0, ())
    halves = feed_sum.finish(*halves)
    feed_sum.start()
    grads = attend_back_call(qkv, grad_att, attended, lse, qm, km, cos_t, sin_t, 1, halves)
    gq, gk, gv = feed_sum.finish(*grads)
    early = feed_sum.value
    ig_qkv, ta_qkv, tb_qkv = qkv_terms_call(gq, gk, gv, normed, bt_qkv, inner_qkv, ad)
    last_sum = Scatter(stack([ta_proj, tb_proj, ta_qkv, tb_qkv]))
    last_sum.start()
    back = functools.partial(qkv_back_call, gq, gk, gv, first, ig_qkv, tokens, gain1)
    held = back(grad_middle, 0)
    (held,) = last_sum.finish(held)
    last_sum.start()
    tokens_grad = back(held, 1)
    (tokens_grad,) = last_sum.finish(tokens_grad)
    last_sum.start()
    last_sum.finish()
    factor = 1.0 / math.sqrt(row_count * devices)
    early = factor * early
    late = factor * last_sum.value
    return (
        block_out,
        tokens_grad,
        late[2 * rows : 3 * rows],
        late[3 * rows :].T,
        late[:rows],
        late[rows : 2 * rows].T,
        early[:rows],
        early[rows : rows * (1 + quarters)].T,
        early[rows * (1 + quarters) : rows * (1 + 2 * quarters)],
        early[rows * (1 + 2 * quarters) :].T,
    )


def solution(mesh):
    return jax.shard_map(
        local,
        mesh=mesh,
        in_specs=(
            P(("dp", "fsdp"), None),
            P(("dp", "fsdp"), None),
            P(("dp", "fsdp")),
            P(("dp", "fsdp")),
            P(("dp", "fsdp")),
            P(("dp", "fsdp")),
            P(("dp", "fsdp"), None),
            P(),
            P(("dp", "fsdp"), None),
            P(),
            P(("dp", "fsdp"), None),
            P(),
            P(("dp", "fsdp"), None),
            P(),
            P(),
            P(),
            P(),
            P(),
            P(("dp", "fsdp"), None),
            P(None, ("dp", "fsdp")),
            P(("dp", "fsdp"), None),
            P(None, ("dp", "fsdp")),
            P(("dp", "fsdp"), None),
            P(None, ("dp", "fsdp")),
            P(("dp", "fsdp"), None),
            P(None, ("dp", "fsdp")),
        ),
        out_specs=(
            P(("dp", "fsdp"), None),
            P(("dp", "fsdp"), None),
            P(("dp", "fsdp"), None),
            P(None, ("dp", "fsdp")),
            P(("dp", "fsdp"), None),
            P(None, ("dp", "fsdp")),
            P(("dp", "fsdp"), None),
            P(None, ("dp", "fsdp")),
            P(("dp", "fsdp"), None),
            P(None, ("dp", "fsdp")),
        ),
        check_vma=False,
    )
```

```python
import functools
import math

import jax
import jax.numpy as jnp
from jax import lax
from jax.experimental import pallas as pl
from jax.experimental.pallas import tpu as pltpu
from jax.sharding import PartitionSpec as P

HEADS = 16
HD = 80
RANK = 16


EPS = 1e-06


BIG = 2.0**60
LOG2E = 1.4426950408889634
BF = jnp.bfloat16
F32 = jnp.float32


def normalize_back(grad_out, unit, spread, gain):
    scaled = grad_out * gain
    return spread * (
        scaled
        - jnp.mean(scaled, axis=-1, keepdims=True)
        - unit * jnp.mean(scaled * unit, axis=-1, keepdims=True)
    )


def rotary_tables(patch_row, patch_col, head_size):
    quarter = head_size // 4
    inverse = 1.0 / 10000.0 ** (jnp.arange(quarter, dtype=jnp.float32) * 2.0 / (head_size // 2))
    angles = jnp.concatenate(
        [
            patch_row.astype(jnp.float32)[:, None] * inverse,
            patch_col.astype(jnp.float32)[:, None] * inverse,
        ],
        axis=1,
    )
    angles = jnp.concatenate([angles, angles], axis=1)
    return (jnp.cos(angles), jnp.sin(angles))


def mm(left, right):
    return lax.dot_general(left, right, (((1,), (0,)), ((), ())), preferred_element_type=F32)


def mm_nt(left, right):
    return lax.dot_general(left, right, (((1,), (1,)), ((), ())), preferred_element_type=F32)


def call(body, name, grid, in_specs, out_specs, out_shape, scratch=(), flops=0, moved=0):
    return pl.pallas_call(
        body,
        name=name,
        grid=grid,
        in_specs=in_specs,
        out_specs=out_specs,
        out_shape=out_shape,
        scratch_shapes=scratch,
        cost_estimate=pl.CostEstimate(flops=flops, transcendentals=0, bytes_accessed=moved),
        compiler_params=pltpu.CompilerParams(
            dimension_semantics=("arbitrary",) * len(grid), vmem_limit_bytes=56 * 1024 * 1024
        ),
    )


def whole(shape):
    return pl.BlockSpec(shape, lambda *_: (0,) * len(shape))


def pick(adapter_ref, count):
    lanes = lax.broadcasted_iota(jnp.int32, (count, 128), 1) // RANK
    return (lanes == adapter_ref[...]).astype(F32)


def turn(values, low):
    size = values.shape[1]
    left = pltpu.roll(values, size - HD // 2, 1)
    right = pltpu.roll(values, HD // 2, 1)
    return jnp.where(low, left, right)


def qkv_body(x_ref, w_ref, a_ref, bt_ref, bias_ref, ad_ref, cos_ref, sin_ref, out_ref, inner_ref):
    part = pl.program_id(0)
    rows = x_ref.shape[0]
    step = 256

    @pl.when(part == 0)
    def _():
        inner_ref[...] = (mm(x_ref[...], a_ref[...]) * pick(ad_ref, rows)).astype(BF)

    def one(start, rotated):
        sl = pl.ds(start, step)
        y = mm(x_ref[sl, :], w_ref[...]) + mm_nt(inner_ref[sl, :], bt_ref[...]) + bias_ref[...]
        if rotated:
            low = lax.broadcasted_iota(jnp.int32, (step, 640), 1) % HD < HD // 2
            for begin in (0, 640):
                piece = y[:, begin : begin + 640]
                done = piece * cos_ref[sl, :] + turn(piece, low) * sin_ref[sl, :]
                out_ref[sl, begin : begin + 640] = done.astype(BF)
        else:
            out_ref[sl, :] = y.astype(BF)

    @pl.when(part < 2)
    def _():
        for i in range(0, rows, step):
            one(i, True)

    @pl.when(part == 2)
    def _():
        for i in range(0, rows, step):
            one(i, False)


def qkv_call(x, pack, bt, bias, adapter, cos_t, sin_t):
    n, d = x.shape
    return call(
        qkv_body,
        "qkv_rotary",
        (3,),
        [
            whole((n, d)),
            pl.BlockSpec((d, d), lambda j: (0, j)),
            pl.BlockSpec((d, 128), lambda j: (0, 3 * d // 128)),
            pl.BlockSpec((d, 128), lambda j: (j, 0)),
            pl.BlockSpec((1, d), lambda j: (0, j)),
            whole((n, 1)),
            whole((n, 640)),
            whole((n, 640)),
        ],
        [pl.BlockSpec((n, d), lambda j: (0, j)), whole((n, 128))],
        [jax.ShapeDtypeStruct((n, 3 * d), BF), jax.ShapeDtypeStruct((n, 128), BF)],
        flops=2 * n * d * 3 * d,
        moved=8 * d * d + 12 * n * d,
    )(x, pack, pack, bt, bias, adapter, cos_t, sin_t)


def attend_body(q_ref, k_ref, v_ref, qm_ref, km_ref, out_ref, lse_ref):
    rows = q_ref.shape[0]
    step = 256
    factor = LOG2E / math.sqrt(HD)
    lanes = lax.broadcasted_iota(jnp.int32, (step, 128), 1)
    for i in range(0, rows, step):
        lse_ref[i : i + step, :] = jnp.zeros((step, 128), F32)
    for h in range(8):
        cols = slice(HD * h, HD * h + HD)
        keys = jnp.concatenate([k_ref[:, cols], km_ref[...]], axis=1)
        vals = v_ref[:, cols]
        for i in range(0, rows, step):
            query = jnp.concatenate([q_ref[i : i + step, cols], qm_ref[i : i + step, :]], axis=1)
            s = mm_nt(query, keys)
            top = jnp.max(s, axis=1, keepdims=True)
            e = jnp.exp2((s - top) * factor)
            total = jnp.sum(e, axis=1, keepdims=True)
            o = mm(e.astype(BF), vals) * (1.0 / total)
            out_ref[i : i + step, cols] = o.astype(BF)
            lse = top + jnp.log(total) * math.sqrt(HD)
            lse_ref[i : i + step, :] = jnp.where(lanes == h, lse, lse_ref[i : i + step, :])


def attend_call(qkv, qm, km):
    n = qkv.shape[0]
    d = qkv.shape[1] // 3
    groups = d // 640
    return call(
        attend_body,
        "attend",
        (groups,),
        [
            pl.BlockSpec((n, 640), lambda g: (0, g)),
            pl.BlockSpec((n, 640), lambda g: (0, groups + g)),
            pl.BlockSpec((n, 640), lambda g: (0, 2 * groups + g)),
            whole((n, 48)),
            whole((n, 48)),
        ],
        [pl.BlockSpec((n, 640), lambda g: (0, g)), pl.BlockSpec((n, 128), lambda g: (0, g))],
        [jax.ShapeDtypeStruct((n, d), BF), jax.ShapeDtypeStruct((n, 128 * groups), F32)],
        flops=4 * n * n * d,
        moved=8 * n * d,
    )(qkv, qkv, qkv, qm, km)


def split_low(values, count):
    parts = []
    for _ in range(count):
        part = values.astype(BF)
        parts.append(part)
        values = values - part.astype(F32)
    return parts


def attend_back_body(
    q_ref, k_ref, v_ref, g_ref, o_ref, lse_ref, qm_ref, km_ref, cos_ref, sin_ref,
    dq_ref, dk_ref, dv_ref, dq_s, dk_s,
):
    rows = q_ref.shape[0]
    step = 256
    factor = LOG2E / math.sqrt(HD)
    scale = 1.0 / math.sqrt(HD)
    lanes = lax.broadcasted_iota(jnp.int32, (rows, 48), 1)
    ones_two = jnp.where((lanes == 16) | (lanes == 17), 1.0, 0.0).astype(BF)
    for h in range(8):
        cols = slice(HD * h, HD * h + HD)
        gh = g_ref[:, cols]
        delta = jnp.sum(gh.astype(F32) * o_ref[:, cols].astype(F32), axis=1, keepdims=True)
        d_hi, d_lo = split_low(-delta, 2)
        l_hi, l_mid, l_lo = split_low(-lse_ref[:, h : h + 1], 3)
        q_aug = jnp.where(
            lanes == 16,
            l_hi.astype(F32),
            jnp.where(
                lanes == 17,
                l_mid.astype(F32),
                jnp.where(lanes == 18, l_lo.astype(F32), qm_ref[...].astype(F32)),
            ),
        ).astype(BF)
        g_aug = jnp.where(
            lanes == 16, d_hi.astype(F32), jnp.where(lanes == 17, d_lo.astype(F32), 0.0)
        ).astype(BF)
        query = jnp.concatenate([q_ref[:, cols], q_aug], axis=1)
        grads = jnp.concatenate([gh, g_aug], axis=1)
        keys = jnp.concatenate([k_ref[:, cols], km_ref[...]], axis=1)
        vals = jnp.concatenate([v_ref[:, cols], ones_two], axis=1)
        keys_t = keys.T
        dk = jnp.zeros((rows, 128), F32)
        dv = jnp.zeros((rows, 128), F32)
        for i in range(0, rows, step):
            qb = query[i : i + step, :]
            gb = grads[i : i + step, :]
            p = jnp.exp2(mm_nt(keys, qb) * factor)
            dp = mm_nt(vals, gb)
            ds = (p * dp).astype(BF)
            dv = dv + mm(p.astype(BF), gb)
            dk = dk + mm(ds, qb)
            dq = mm(keys_t, ds)
            dq_s[i : i + step, cols] = dq.T[:, :HD]
        dk_s[:, cols] = dk[:, :HD]
        dv_ref[:, cols] = dv[:, :HD].astype(BF)
    low = lax.broadcasted_iota(jnp.int32, (step, 640), 1) % HD < HD // 2
    for i in range(0, rows, step):
        sl = slice(i, i + step)
        for src, dst in ((dq_s, dq_ref), (dk_s, dk_ref)):
            piece = src[sl, :] * scale
            dst[sl, :] = (piece * cos_ref[sl, :] - turn(piece, low) * sin_ref[sl, :]).astype(BF)


def attend_back_call(qkv, grads, attended, lse, qm, km, cos_t, sin_t):
    n = qkv.shape[0]
    d = qkv.shape[1] // 3
    groups = d // 640
    block = pl.BlockSpec((n, 640), lambda g: (0, g))
    return call(
        attend_back_body,
        "attend_back",
        (groups,),
        [
            block,
            pl.BlockSpec((n, 640), lambda g: (0, groups + g)),
            pl.BlockSpec((n, 640), lambda g: (0, 2 * groups + g)),
            block,
            block,
            pl.BlockSpec((n, 128), lambda g: (0, g)),
            whole((n, 48)),
            whole((n, 48)),
            whole((n, 640)),
            whole((n, 640)),
        ],
        [block, block, block],
        [jax.ShapeDtypeStruct((n, d), BF)] * 3,
        [pltpu.VMEM((n, 640), F32), pltpu.VMEM((n, 640), F32)],
        flops=10 * n * n * d,
        moved=16 * n * d,
    )(qkv, qkv, qkv, grads, attended, lse, qm, km, cos_t, sin_t)


def tables(picture, patch_row, patch_col):
    cosine, sine = rotary_tables(patch_row, patch_col, HD)
    half = HD // 2
    signed = jnp.concatenate([-sine[:, :half], sine[:, half:]], axis=1)
    count = picture.shape[0]
    change = (picture[1:] != picture[:-1]).astype(jnp.int32)
    places = lax.broadcasted_iota(jnp.int32, (count, count - 1), 0)
    before = lax.broadcasted_iota(jnp.int32, (count, count - 1), 1) < places
    index = jnp.sum(jnp.where(before, change[None, :], 0), axis=1)
    lanes = lax.broadcasted_iota(jnp.int32, (1, 48), 1)
    own = lanes == index[:, None]
    qm = jnp.where(own | (lanes >= 16), 0.0, -BIG).astype(BF)
    km = (own | ((lanes >= 16) & (lanes < 19))).astype(BF)
    return (*widen_call(cosine, signed), qm, km)


def stats(values):
    centre = jnp.mean(values, axis=-1, keepdims=True)
    centred = values - centre
    spread = lax.rsqrt(jnp.mean(centred * centred, axis=-1, keepdims=True) + EPS)
    return centred * spread, spread


def once(shape, index):
    return pl.BlockSpec(shape, index, pipeline_mode=pl.Buffered(1))


def proj_body(
    att_ref, w_ref, a_ref, bt_ref, bias_ref, ad_ref, tok_ref, gain_ref, shift_ref,
    mid_ref, norm_ref, inner_ref,
):
    rows = att_ref.shape[0]
    x = att_ref[...]
    inner = (mm(x, a_ref[...]) * pick(ad_ref, rows)).astype(BF)
    inner_ref[...] = inner
    middle = tok_ref[...].astype(F32) + (mm(x, w_ref[...]) + bias_ref[...] + mm_nt(inner, bt_ref[...]))
    mid_ref[...] = middle
    unit, _ = stats(middle)
    norm_ref[...] = (unit * gain_ref[...] + shift_ref[...]).astype(BF)


def proj_call(att, pack, first_col, a_col, bt_col, bias, adapter, tokens, gain, shift):
    n, d = att.shape
    step = 256
    row = pl.BlockSpec((step, d), lambda i: (i, 0))
    return call(
        proj_body,
        "proj_norm",
        (n // step,),
        [
            row,
            once((d, d), lambda i: (0, first_col // d)),
            once((d, 128), lambda i: (0, a_col // 128)),
            once((d, 128), lambda i: (0, bt_col // 128)),
            whole((1, d)),
            pl.BlockSpec((step, 1), lambda i: (i, 0)),
            row,
            whole((1, d)),
            whole((1, d)),
        ],
        [row, row, pl.BlockSpec((step, 128), lambda i: (i, 0))],
        [
            jax.ShapeDtypeStruct((n, d), F32),
            jax.ShapeDtypeStruct((n, d), BF),
            jax.ShapeDtypeStruct((n, 128), BF),
        ],
        flops=2 * n * d * d,
        moved=2 * d * d + 10 * n * d,
    )(att, pack, pack, pack, bias, adapter, tokens, gain, shift)


def feed_body(*refs, parts, first, last):
    refs = list(refs)
    take = lambda count: [refs.pop(0) for _ in range(count)]
    x_ref, g_ref = take(2)
    w1, w2, bt1, a2, b1 = take(parts), take(parts), take(parts), take(parts), take(parts)
    ad_ref, a1_ref, bt2_ref = take(3)
    if first:
        base_ref, b2_ref = take(2)
    else:
        base_ref, gx_in, in1_ref, ig2_ref, in2_in, ig1_in = take(6)
        val_ref = take(1)[0]
    if first:
        acc_ref, gx_ref, in1_out, ig2_out, in2_out, ig1_out = take(6)
    if last:
        out_ref, gx_ref, ta1_ref, tb2_ref = take(4)
    ta2, tb1 = take(parts), take(parts)
    if last:
        ta1_s, tb2_s = take(2)
    ta2_s, tb1_s = take(parts), take(parts)
    sums = ta2_s + tb1_s + ([ta1_s, tb2_s] if last else [])
    i = pl.program_id(0)
    end = i == pl.num_programs(0) - 1

    @pl.when(i == 0)
    def _():
        for ref in sums:
            ref[...] = jnp.zeros_like(ref)

    sub = 256
    for begin in range(0, x_ref.shape[0], sub):
        sl = pl.ds(begin, sub)
        x = x_ref[sl, :]
        g = g_ref[sl, :]
        sel = pick(ad_ref.at[sl, :], sub)
        if first:
            in1 = (mm(x, a1_ref[...]) * sel).astype(BF)
            ig2 = (mm(g, bt2_ref[...]) * sel).astype(BF)
            in1_out[sl, :] = in1
            ig2_out[sl, :] = ig2
            acc = base_ref[sl, :] + b2_ref[...]
            gx = in2 = ig1 = None
        else:
            in1 = in1_ref[sl, :]
            ig2 = ig2_ref[sl, :]
            acc, gx, in2, ig1 = base_ref[sl, :], gx_in[sl, :], in2_in[sl, :], ig1_in[sl, :]
        in1_t = in1.T
        ig2_t = ig2.T
        acts, ghs = [], []
        hs = [mm(x, w1[q][...]) + mm_nt(in1, bt1[q][...]) + b1[q][...] for q in range(parts)]
        gas = [mm_nt(g, w2[q][...]) + mm_nt(ig2, a2[q][...]) for q in range(parts)]
        for q in range(parts):
            h = hs[q]
            s = 0.5 * jnp.tanh(0.851 * h) + 0.5
            acts.append((h * s).astype(BF))
            ghs.append((gas[q] * (s + 1.702 * h * s * (1.0 - s))).astype(BF))
        for q in range(parts):
            act, gh = acts[q], ghs[q]
            more = (mm_nt(gh, w1[q][...]), mm(act, a2[q][...]), mm(gh, bt1[q][...]))
            acc = acc + mm(act, w2[q][...])
            gx, in2, ig1 = more if gx is None else (gx + more[0], in2 + more[1], ig1 + more[2])
            ta2_s[q][...] += mm(ig2_t, act)
            tb1_s[q][...] += mm(in1_t, gh)
        if last:
            low2 = (in2 * sel).astype(BF)
            low1 = (ig1 * sel).astype(BF)
            out_ref[sl, :] = ((acc + mm_nt(low2, bt2_ref[...])) * val_ref[sl, :]).astype(BF)
            gx_ref[sl, :] = gx + mm_nt(low1, a1_ref[...])
            ta1_s[...] += mm(low1.T, x)
            tb2_s[...] += mm(low2.T, g)
        else:
            acc_ref[sl, :] = acc
            gx_ref[sl, :] = gx
            in2_out[sl, :] = in2
            ig1_out[sl, :] = ig1

    @pl.when(end)
    def _():
        for q in range(parts):
            ta2[q][...] = ta2_s[q][...].T.astype(BF)
            tb1[q][...] = tb1_s[q][...].T.astype(BF)
        if last:
            ta1_ref[...] = ta1_s[...].T.astype(BF)
            tb2_ref[...] = tb2_s[...].T.astype(BF)


def feed_call(x, grads, w2, w1, bt1, a2, b1, adapter, a1, bt2, state, first, last):
    n, d = x.shape
    parts = len(w1)
    step = 512 if parts < 3 else 256
    row = pl.BlockSpec((step, d), lambda i: (i, 0))
    thin_row = pl.BlockSpec((step, 128), lambda i: (i, 0))
    one = pl.BlockSpec((step, 1), lambda i: (i, 0))
    thin = once((d, 128), lambda i: (0, 0))
    line = once((1, d), lambda i: (0, 0))

    def wide(col):
        return once((d, d), lambda i: (0, col // d))

    def narrow(col):
        return once((d, 128), lambda i: (0, col // 128))

    in_specs = [row, row] + [wide(c) for _, c in w1] + [wide(c) for _, c in w2]
    in_specs += [narrow(c) for _, c in bt1] + [narrow(c) for _, c in a2] + [line] * parts
    in_specs += [one, narrow(a1[1]), narrow(bt2[1])]
    args = [x, grads] + [v for v, _ in w1 + w2 + bt1 + a2] + list(b1) + [adapter, a1[0], bt2[0]]
    if first:
        in_specs += [row, line]
    else:
        in_specs += [row, row, thin_row, thin_row, thin_row, thin_row, one]
    args += list(state)
    out_specs, out_shape, scratch = [], [], []
    if first:
        out_specs += [row, row, thin_row, thin_row, thin_row, thin_row]
        out_shape += [jax.ShapeDtypeStruct((n, d), F32)] * 2
        out_shape += [jax.ShapeDtypeStruct((n, 128), BF)] * 2 + [jax.ShapeDtypeStruct((n, 128), F32)] * 2
    if last:
        out_specs += [row, row, thin, thin]
        out_shape += [jax.ShapeDtypeStruct((n, d), BF), jax.ShapeDtypeStruct((n, d), F32)]
        out_shape += [jax.ShapeDtypeStruct((d, 128), BF)] * 2
        scratch += [pltpu.VMEM((128, d), F32)] * 2
    out_specs += [thin] * (2 * parts)
    out_shape += [jax.ShapeDtypeStruct((d, 128), BF)] * (2 * parts)
    scratch += [pltpu.VMEM((128, d), F32)] * (2 * parts)
    return call(
        functools.partial(feed_body, parts=parts, first=first, last=last),
        "feed_first" if first else "feed_last",
        (n // step,),
        in_specs,
        out_specs,
        out_shape,
        scratch,
        flops=8 * n * d * d * parts,
        moved=4 * d * d * parts + 24 * n * d,
    )(*args)


def proj_back_body(
    gx_ref, mid_ref, cot_ref, val_ref, gain_ref, w_ref, a_ref, bt_ref, ad_ref, att_ref, inner_ref,
    gm_ref, ga_ref, ta_ref, tb_ref, ta_s, tb_s,
):
    i = pl.program_id(0)
    sub = 256

    @pl.when(i == 0)
    def _():
        ta_s[...] = jnp.zeros_like(ta_s)
        tb_s[...] = jnp.zeros_like(tb_s)

    for begin in range(0, gx_ref.shape[0], sub):
        sl = pl.ds(begin, sub)
        unit, spread = stats(mid_ref[sl, :])
        gm = cot_ref[sl, :].astype(F32) * val_ref[sl, :]
        gm = gm + normalize_back(gx_ref[sl, :], unit, spread, gain_ref[...])
        gm_ref[sl, :] = gm
        gb = gm.astype(BF)
        ig = (mm(gb, bt_ref[...]) * pick(ad_ref.at[sl, :], sub)).astype(BF)
        ga_ref[sl, :] = (mm_nt(gb, w_ref[...]) + mm_nt(ig, a_ref[...])).astype(BF)
        ta_s[...] += mm(ig.T, att_ref[sl, :])
        tb_s[...] += mm(inner_ref[sl, :].T, gb)

    @pl.when(i == pl.num_programs(0) - 1)
    def _():
        ta_ref[...] = ta_s[...].T.astype(BF)
        tb_ref[...] = tb_s[...].T.astype(BF)


def proj_back_call(gx, middle, cot, valid, gain, pack, first_col, a_col, bt_col, adapter, att, inner):
    n, d = gx.shape
    step = 256
    row = pl.BlockSpec((step, d), lambda i: (i, 0))
    one = pl.BlockSpec((step, 1), lambda i: (i, 0))
    thin = once((d, 128), lambda i: (0, 0))
    return call(
        proj_back_body,
        "proj_back",
        (n // step,),
        [
            row,
            row,
            row,
            one,
            whole((1, d)),
            once((d, d), lambda i: (0, first_col // d)),
            once((d, 128), lambda i: (0, a_col // 128)),
            once((d, 128), lambda i: (0, bt_col // 128)),
            one,
            row,
            pl.BlockSpec((step, 128), lambda i: (i, 0)),
        ],
        [row, row, thin, thin],
        [
            jax.ShapeDtypeStruct((n, d), F32),
            jax.ShapeDtypeStruct((n, d), BF),
            jax.ShapeDtypeStruct((d, 128), BF),
            jax.ShapeDtypeStruct((d, 128), BF),
        ],
        [pltpu.VMEM((128, d), F32), pltpu.VMEM((128, d), F32)],
        flops=2 * n * d * d,
        moved=2 * d * d + 18 * n * d,
    )(gx, middle, cot, valid, gain, pack, pack, pack, adapter, att, inner)


def qkv_terms_body(gq_ref, gk_ref, gv_ref, x_ref, bt_ref, inner_ref, ad_ref, ig_ref, ta_ref, tb_ref, ta_s, tb_s):
    i = pl.program_id(0)
    rows, d = x_ref.shape

    @pl.when(i == 0)
    def _():
        ta_s[...] = jnp.zeros_like(ta_s)
        tb_s[...] = jnp.zeros_like(tb_s)

    inner_t = inner_ref[...].T
    total = None
    for part, ref in enumerate((gq_ref, gk_ref, gv_ref)):
        g = ref[...]
        sl = slice(part * d, part * d + d)
        piece = mm(g, bt_ref[sl, :])
        total = piece if total is None else total + piece
        tb_s[:, sl] += mm(inner_t, g)
    ig = (total * pick(ad_ref, rows)).astype(BF)
    ig_ref[...] = ig
    ta_s[...] += mm(ig.T, x_ref[...])

    @pl.when(i == pl.num_programs(0) - 1)
    def _():
        ta_ref[...] = ta_s[...].T.astype(BF)
        tb_ref[...] = tb_s[...].T.astype(BF)


def qkv_terms_call(gq, gk, gv, x, bt, inner, adapter):
    n, d = x.shape
    step = 256
    row = pl.BlockSpec((step, d), lambda i: (i, 0))
    thin_row = pl.BlockSpec((step, 128), lambda i: (i, 0))
    return call(
        qkv_terms_body,
        "qkv_terms",
        (n // step,),
        [row, row, row, row, whole(bt.shape), thin_row, pl.BlockSpec((step, 1), lambda i: (i, 0))],
        [thin_row, whole((d, 128)), whole((3 * d, 128))],
        [
            jax.ShapeDtypeStruct((n, 128), BF),
            jax.ShapeDtypeStruct((d, 128), BF),
            jax.ShapeDtypeStruct((3 * d, 128), BF),
        ],
        [pltpu.VMEM((128, d), F32), pltpu.VMEM((128, 3 * d), F32)],
        flops=4 * n * d * 128 * 4,
        moved=10 * n * d,
    )(gq, gk, gv, x, bt, inner, adapter)


def qkv_back_body(gq_ref, gk_ref, gv_ref, w_ref, ig_ref, a_ref, tok_ref, gain_ref, gm_ref, out_ref, acc_ref):
    part = pl.program_id(0)
    sub = 256
    pieces = [pl.ds(begin, sub) for begin in range(0, tok_ref.shape[0], sub)]

    @pl.when(part == 0)
    def _():
        for sl in pieces:
            acc_ref[sl, :] = mm_nt(gq_ref[sl, :], w_ref[...]) + mm_nt(ig_ref[sl, :], a_ref[...])

    @pl.when(part == 1)
    def _():
        for sl in pieces:
            acc_ref[sl, :] += mm_nt(gk_ref[sl, :], w_ref[...])

    @pl.when(part == 2)
    def _():
        for sl in pieces:
            grad = acc_ref[sl, :] + mm_nt(gv_ref[sl, :], w_ref[...])
            unit, spread = stats(tok_ref[sl, :].astype(F32))
            out_ref[sl, :] = gm_ref[sl, :] + normalize_back(grad, unit, spread, gain_ref[...])


def qkv_back_call(gq, gk, gv, pack, ig, tokens, gain, gm, half):
    n, d = tokens.shape
    rows = n // 2
    row = pl.BlockSpec((rows, d), lambda p: (half, 0))
    return pl.pallas_call(
        qkv_back_body,
        name="qkv_back",
        grid=(3,),
        in_specs=[
            row,
            row,
            row,
            pl.BlockSpec((d, d), lambda p: (0, p)),
            pl.BlockSpec((rows, 128), lambda p: (half, 0)),
            once((d, 128), lambda p: (0, 3 * d // 128)),
            row,
            whole((1, d)),
            row,
        ],
        out_specs=row,
        out_shape=jax.ShapeDtypeStruct((n, d), F32),
        scratch_shapes=[pltpu.VMEM((rows, d), F32)],
        input_output_aliases={8: 0},
        cost_estimate=pl.CostEstimate(flops=3 * n * d * d, transcendentals=0, bytes_accessed=6 * d * d + 9 * n * d),
        compiler_params=pltpu.CompilerParams(
            dimension_semantics=("arbitrary",), vmem_limit_bytes=56 * 1024 * 1024
        ),
    )(gq, gk, gv, pack, ig, pack, tokens, gain, gm)


def unfold_rows(block, devices):
    rows = block.shape[0] // devices
    pieces = block.shape[1] // 128
    split = block.reshape(devices, rows, pieces, 128)
    return split.transpose(0, 2, 1, 3).reshape(-1, 128)


def gather_rows(packed):
    return lax.all_gather(packed, ("dp", "fsdp"), axis=0, tiled=True)


def place_body(table_ref, *refs, pieces):
    out_ref = refs[-1]
    mask = table_ref[2]
    begin = 0
    for ref in refs[:pieces]:
        end = begin + ref.shape[-1]
        for k in range(ref.shape[1]):
            out_ref[mask ^ k, 0, 0, :, begin:end] = ref[0, k]
        begin = end


class Gather:
    def __init__(self, *parts):
        self.zs, self.fs = lax.axis_size("dp") // 2, lax.axis_size("fsdp")
        self.rows, self.cols = parts[0].shape[0], sum(p.shape[1] for p in parts)
        self.parts = list(parts)
        self.phase = 0

    def swap(self, value, axis, mask):
        return lax.ppermute(value, axis, [(i, i ^ mask) for i in range(lax.axis_size(axis))])

    def start(self):
        z_masks, f_masks = list(range(2, 2 * self.zs, 2)), list(range(1, self.fs))
        orders = [[("dp", z_masks), ("fsdp", f_masks)], [("fsdp", f_masks), ("dp", z_masks)]]
        self.got = []
        for part, order in zip(self.parts, orders):
            axis, masks = order[self.phase] if self.phase < 2 else ("dp", [1])
            self.got.append([part] + [self.swap(part, axis, m) for m in masks])

    def finish(self, *others):
        sizes = [len(group) for group in self.got]
        held = lax.optimization_barrier(tuple(v for group in self.got for v in group) + others)
        groups, at = [], 0
        for size in sizes:
            groups.append(held[at : at + size])
            at += size
        if self.phase == 0:
            self.parts = [jnp.stack(group) for group in groups]
        elif self.phase == 1:
            self.parts = [jnp.stack(group, axis=1 if i else 0) for i, group in enumerate(groups)]
        if self.phase < 2:
            held = lax.optimization_barrier(tuple(self.parts) + tuple(held[at:]))
            self.parts = list(held[: len(sizes)])
            at = len(sizes)
        else:
            self.far = [group[1] for group in groups[::-1]]
        self.phase += 1
        return held[at:]

    def place(self, side, earlier):
        zs, fs, rows, cols = self.zs, self.fs, self.rows, self.cols
        spot, column = lax.axis_index("dp"), lax.axis_index("fsdp")
        table = jnp.stack([(spot & 1) ^ side, column, spot >> 1]).astype(jnp.int32)
        parts = self.far if side else self.parts[::-1]
        specs = [pl.BlockSpec((1, zs, rows, p.shape[-1]), lambda m, t: (m, 0, 0, 0)) for p in parts]
        specs += [pl.BlockSpec(memory_space=pl.ANY)] * len(earlier)
        return pl.pallas_call(
            functools.partial(place_body, pieces=len(parts)),
            name="place_blocks",
            grid_spec=pltpu.PrefetchScalarGridSpec(
                num_scalar_prefetch=1,
                grid=(fs,),
                in_specs=specs,
                out_specs=pl.BlockSpec((zs, 1, 1, rows, cols), lambda m, t: (0, t[0], t[1] ^ m, 0, 0)),
            ),
            out_shape=jax.ShapeDtypeStruct((zs, 2, fs, rows, cols), BF),
            input_output_aliases={1 + len(parts): 0} if earlier else {},
            cost_estimate=pl.CostEstimate(flops=0, transcendentals=0, bytes_accessed=4 * zs * fs * rows * cols),
            compiler_params=pltpu.CompilerParams(vmem_limit_bytes=48 * 1024 * 1024),
        )(table, *parts, *earlier)


def widen_body(cos_ref, sin_ref, cos_out, sin_out):
    for src, dst in ((cos_ref, cos_out), (sin_ref, sin_out)):
        value = src[...]
        dst[...] = jnp.concatenate([value] * 8, axis=1)


def widen_call(cosine, signed):
    n = cosine.shape[0]
    out = jax.ShapeDtypeStruct((n, 8 * HD), F32)
    specs = [whole((n, 8 * HD))] * 2
    return call(widen_body, "widen_tables", (1,), [whole(cosine.shape)] * 2, specs, [out, out], moved=72 * n * HD)(
        cosine, signed
    )


def pack_body(
    qkv_w, proj_w, fc1_w, fc2_w, qkv_a, proj_a, fc1_a, fc2_a, qkv_b, proj_b, fc1_b, fc2_b, *outs, devices, cut, groups
):
    rows, d = proj_w.shape
    quarters = fc1_w.shape[1] // d

    def turned(ref):
        flipped = ref[...].astype(F32)
        return [flipped[i * rows : (i + 1) * rows].astype(BF) for i in range(flipped.shape[0] // rows)]

    def fill(out, pieces):
        at = 0
        for piece in pieces:
            out[:, at : at + piece.shape[1]] = piece
            at += piece.shape[1]

    fill(outs[1], [qkv_w[:, :cut]])
    fill(outs[0], [qkv_w[:, cut:], qkv_a[...]] + turned(qkv_b))
    up1 = turned(fc1_b)
    for out, group in zip(outs[2:], groups):
        pieces = [fc2_w[q * rows : (q + 1) * rows, :] for q in group]
        for q in group:
            starts = [(i * quarters + q) * rows for i in range(devices)]
            pieces.append(jnp.concatenate([fc1_w[:, c : c + rows] for c in starts], axis=1))
        if group[0] == 0:
            pieces.append(proj_w[...])
        pieces += [up1[q] for q in group]
        pieces += [fc2_a[q * rows : (q + 1) * rows, :] for q in group]
        if group[0] == 0:
            pieces += [fc1_a[...], proj_a[...]] + turned(proj_b) + turned(fc2_b)
        fill(out, pieces)


def pack_call(arrays, devices, groups):
    rows, d = arrays[1].shape
    total = arrays[0].shape[1] + 4 * 128
    cut = total // 128 // 3 * 128
    widths = [total - cut, cut] + [len(g) * (2 * d + 256) + (d + 512 if g[0] == 0 else 0) for g in groups]
    return call(
        functools.partial(pack_body, devices=devices, cut=cut, groups=groups),
        "pack_shards",
        (1,),
        [whole(v.shape) for v in arrays],
        [whole((rows, w)) for w in widths],
        [jax.ShapeDtypeStruct((rows, w), BF) for w in widths],
        moved=4 * rows * sum(widths),
    )(*arrays)


class Scatter:
    def __init__(self, terms):
        zs, fs = lax.axis_size("dp") // 2, lax.axis_size("fsdp")
        self.values = [t.reshape(zs, 2, fs, -1, 128) for t in terms]
        self.phases = [("dp", 1, [1]), ("fsdp", 1, list(range(1, fs))), ("dp", 0, list(range(2, 2 * zs, 2)))]
        self.open = None

    def start(self):
        axis, dim, masks = self.phases.pop(0)
        size = lax.axis_size(axis)
        place = lax.axis_index(axis)
        shift = 0
        if axis == "dp":
            place, shift = (place & 1, 0) if dim else (place >> 1, 1)

        def pick_one(at):
            found = [lax.dynamic_index_in_dim(v, at, dim, keepdims=False) for v in self.values]
            return found[0] if len(found) == 1 else jnp.concatenate(found, axis=-2)

        sends = [pick_one(place ^ (mask >> shift)).astype(BF) for mask in masks]
        got = [lax.ppermute(v, axis, [(i, i ^ mask) for i in range(size)]) for v, mask in zip(sends, masks)]
        self.open = (lambda: pick_one(place), got)

    def finish(self, *others):
        mine, got = self.open
        held = lax.optimization_barrier(tuple(got) + others)
        total = mine().astype(F32)
        for piece in held[: len(got)]:
            total = total + piece.astype(F32)
        self.values = [total]
        return held[len(got) :]


def local(
    tokens,
    cotangent,
    picture,
    adapter,
    patch_row,
    patch_col,
    qkv_weight,
    qkv_bias,
    proj_weight,
    proj_bias,
    fc1_weight,
    fc1_bias,
    fc2_weight,
    fc2_bias,
    norm1_gain,
    norm1_bias,
    norm2_gain,
    norm2_bias,
    qkv_down,
    qkv_up,
    proj_down,
    proj_up,
    fc1_down,
    fc1_up,
    fc2_down,
    fc2_up,
):
    devices = lax.axis_size(("dp", "fsdp"))
    rows, d = proj_weight.shape
    quarters = fc1_weight.shape[1] // d
    q_cols = qkv_weight.shape[1]
    groups = [list(range(quarters - 1)), [quarters - 1]]
    shards = (qkv_weight, proj_weight, fc1_weight, fc2_weight, qkv_down, proj_down, fc1_down, fc2_down)
    shards += (qkv_up.T, proj_up.T, fc1_up.T, fc2_up.T)
    part_b, part_a, pack_a, pack_b = pack_call(shards, devices, groups)
    one = Gather(part_b, part_a)
    one.start()

    def spots(source, count, extra):
        wide = [(source, q * d) for q in range(2 * count)]
        base = (2 * count + extra) * d
        thin = [(source, base + q * 128) for q in range(2 * count)]
        return [wide[:count], wide[count:], thin[:count], thin[count:]]

    count = len(groups[0])
    row_count = tokens.shape[0]
    unit_one, _ = stats(tokens.astype(F32))
    normed = (unit_one * norm1_gain + norm1_bias).astype(BF)
    (normed,) = one.finish(normed)
    second = gather_rows(pack_a)
    third = gather_rows(pack_b)
    proj_col = 2 * count * d
    a1_col = proj_col + d + 2 * count * 128
    ap_col, btp_col, bt2_col = a1_col + 128, a1_col + 256, a1_col + 384
    one.start()
    ad = adapter[:, None]
    valid = (picture >= 0).astype(F32)[:, None]
    grad_low = (cotangent.astype(F32) * valid).astype(BF)
    bias1 = fc1_bias.reshape(devices, quarters, rows).transpose(1, 0, 2).reshape(quarters, 1, d)
    small = [qkv_bias[None], proj_bias[None], norm1_gain[None], norm2_gain[None], norm2_bias[None], fc2_bias[None]]
    small += [bias1[q] for q in range(quarters)] + [ad, valid, grad_low, *tables(picture, patch_row, patch_col)]
    small = one.finish(*small)
    bias_qkv, bias_proj, gain1, gain2, shift2, bias2, *bias1 = small[: 6 + quarters]
    ad, valid, grad_low, cos_t, sin_t, qm, km = small[6 + quarters :]
    one.start()
    first = one.place(0, ())
    (first,) = one.finish(first)
    first = one.place(1, (first,)).reshape(devices * rows, -1)
    bt_qkv = unfold_rows(first[:, q_cols + 128 :], devices)
    qkv, inner_qkv = qkv_call(normed, first, bt_qkv, bias_qkv, ad, cos_t, sin_t)
    attended, lse = attend_call(qkv, qm, km)
    middle, normed_two, inner_proj = proj_call(
        attended, second, proj_col, ap_col, btp_col, bias_proj, ad, tokens, gain2, shift2
    )
    a1, bt2 = (second, a1_col), (second, bt2_col)
    early = spots(second, count, 1)
    final = spots(third, quarters - count, 0)
    acc, grad_x, in1, ig2, in2, ig1, *terms_a = feed_call(
        normed_two, grad_low, *early, bias1[:count], ad, a1, bt2, (middle, bias2), True, False
    )
    na, nb = count, quarters - count
    state = (acc, grad_x, in1, ig2, in2, ig1, valid)
    block_out, grad_two, ta_fc1, tb_fc2, *terms_b = feed_call(
        normed_two, grad_low, *final, bias1[count:], ad, a1, bt2, state, False, True
    )

    feed_sum = Scatter([ta_fc1, *terms_a[na:], *terms_b[nb:], *terms_a[:na], *terms_b[:nb], tb_fc2])
    feed_sum.start()
    grad_middle, grad_att, ta_proj, tb_proj = proj_back_call(
        grad_two, middle, cotangent, valid, gain2, second, proj_col, ap_col, btp_col, ad, attended, inner_proj
    )
    (grad_att,) = feed_sum.finish(grad_att)
    feed_sum.start()
    grads = attend_back_call(qkv, grad_att, attended, lse, qm, km, cos_t, sin_t)
    gq, gk, gv = feed_sum.finish(*grads)
    feed_sum.start()
    ig_qkv, ta_qkv, tb_qkv = qkv_terms_call(gq, gk, gv, normed, bt_qkv, inner_qkv, ad)
    ig_qkv, ta_qkv, tb_qkv = feed_sum.finish(ig_qkv, ta_qkv, tb_qkv)
    last_sum = Scatter([ta_proj, tb_proj, ta_qkv, tb_qkv])
    last_sum.start()
    back = functools.partial(qkv_back_call, gq, gk, gv, first, ig_qkv, tokens, gain1)
    held = back(grad_middle, 0)
    (held,) = last_sum.finish(held)
    last_sum.start()
    tokens_grad = back(held, 1)
    (tokens_grad,) = last_sum.finish(tokens_grad)
    last_sum.start()
    last_sum.finish()
    early, late = feed_sum.values[0], last_sum.values[0]
    factor = 1.0 / math.sqrt(row_count * devices)
    early = factor * early
    late = factor * late
    return (
        block_out,
        tokens_grad,
        late[2 * rows : 3 * rows],
        late[3 * rows :].T,
        late[:rows],
        late[rows : 2 * rows].T,
        early[:rows],
        early[rows : rows * (1 + quarters)].T,
        early[rows * (1 + quarters) : rows * (1 + 2 * quarters)],
        early[rows * (1 + 2 * quarters) :].T,
    )


def solution(mesh):
    return jax.shard_map(
        local,
        mesh=mesh,
        in_specs=(
            P(("dp", "fsdp"), None),
            P(("dp", "fsdp"), None),
            P(("dp", "fsdp")),
            P(("dp", "fsdp")),
            P(("dp", "fsdp")),
            P(("dp", "fsdp")),
            P(("dp", "fsdp"), None),
            P(),
            P(("dp", "fsdp"), None),
            P(),
            P(("dp", "fsdp"), None),
            P(),
            P(("dp", "fsdp"), None),
            P(),
            P(),
            P(),
            P(),
            P(),
            P(("dp", "fsdp"), None),
            P(None, ("dp", "fsdp")),
            P(("dp", "fsdp"), None),
            P(None, ("dp", "fsdp")),
            P(("dp", "fsdp"), None),
            P(None, ("dp", "fsdp")),
            P(("dp", "fsdp"), None),
            P(None, ("dp", "fsdp")),
        ),
        out_specs=(
            P(("dp", "fsdp"), None),
            P(("dp", "fsdp"), None),
            P(("dp", "fsdp"), None),
            P(None, ("dp", "fsdp")),
            P(("dp", "fsdp"), None),
            P(None, ("dp", "fsdp")),
            P(("dp", "fsdp"), None),
            P(None, ("dp", "fsdp")),
            P(("dp", "fsdp"), None),
            P(None, ("dp", "fsdp")),
        ),
        check_vma=False,
    )
```

```python
import functools
import math

import jax
import jax.numpy as jnp
from jax import lax
from jax.experimental import pallas as pl
from jax.experimental.pallas import tpu as pltpu
from jax.sharding import PartitionSpec as P

HEADS = 16
HD = 80
RANK = 16


EPS = 1e-06


BIG = 2.0**60
LOG2E = 1.4426950408889634
BF = jnp.bfloat16
F32 = jnp.float32


def normalize_back(grad_out, unit, spread, gain):
    scaled = grad_out * gain
    return spread * (
        scaled
        - jnp.mean(scaled, axis=-1, keepdims=True)
        - unit * jnp.mean(scaled * unit, axis=-1, keepdims=True)
    )


def rotary_tables(patch_row, patch_col, head_size):
    quarter = head_size // 4
    inverse = 1.0 / 10000.0 ** (jnp.arange(quarter, dtype=jnp.float32) * 2.0 / (head_size // 2))
    angles = jnp.concatenate(
        [
            patch_row.astype(jnp.float32)[:, None] * inverse,
            patch_col.astype(jnp.float32)[:, None] * inverse,
        ],
        axis=1,
    )
    angles = jnp.concatenate([angles, angles], axis=1)
    return (jnp.cos(angles), jnp.sin(angles))


def mm(left, right):
    return lax.dot_general(left, right, (((1,), (0,)), ((), ())), preferred_element_type=F32)


def mm_nt(left, right):
    return lax.dot_general(left, right, (((1,), (1,)), ((), ())), preferred_element_type=F32)


def call(body, name, grid, in_specs, out_specs, out_shape, scratch=(), flops=0, moved=0):
    return pl.pallas_call(
        body,
        name=name,
        grid=grid,
        in_specs=in_specs,
        out_specs=out_specs,
        out_shape=out_shape,
        scratch_shapes=scratch,
        cost_estimate=pl.CostEstimate(flops=flops, transcendentals=0, bytes_accessed=moved),
        compiler_params=pltpu.CompilerParams(
            dimension_semantics=("arbitrary",) * len(grid), vmem_limit_bytes=56 * 1024 * 1024
        ),
    )


def whole(shape):
    return pl.BlockSpec(shape, lambda *_: (0,) * len(shape))


def pick(adapter_ref, count):
    lanes = lax.broadcasted_iota(jnp.int32, (count, 128), 1) // RANK
    return (lanes == adapter_ref[...]).astype(F32)


def turn(values, low):
    size = values.shape[1]
    left = pltpu.roll(values, size - HD // 2, 1)
    right = pltpu.roll(values, HD // 2, 1)
    return jnp.where(low, left, right)


def qkv_body(x_ref, w_ref, a_ref, bt_ref, bias_ref, ad_ref, cos_ref, sin_ref, out_ref, inner_ref):
    part = pl.program_id(0)
    rows = x_ref.shape[0]
    step = 256

    @pl.when(part == 0)
    def _():
        inner_ref[...] = (mm(x_ref[...], a_ref[...]) * pick(ad_ref, rows)).astype(BF)

    def one(start, rotated):
        sl = pl.ds(start, step)
        y = mm(x_ref[sl, :], w_ref[...]) + mm_nt(inner_ref[sl, :], bt_ref[...]) + bias_ref[...]
        if rotated:
            low = lax.broadcasted_iota(jnp.int32, (step, 640), 1) % HD < HD // 2
            for begin in (0, 640):
                piece = y[:, begin : begin + 640]
                done = piece * cos_ref[sl, :] + turn(piece, low) * sin_ref[sl, :]
                out_ref[sl, begin : begin + 640] = done.astype(BF)
        else:
            out_ref[sl, :] = y.astype(BF)

    @pl.when(part < 2)
    def _():
        for i in range(0, rows, step):
            one(i, True)

    @pl.when(part == 2)
    def _():
        for i in range(0, rows, step):
            one(i, False)


def qkv_call(x, pack, bt, bias, adapter, cos_t, sin_t):
    n, d = x.shape
    return call(
        qkv_body,
        "qkv_rotary",
        (3,),
        [
            whole((n, d)),
            pl.BlockSpec((d, d), lambda j: (0, j)),
            pl.BlockSpec((d, 128), lambda j: (0, 3 * d // 128)),
            pl.BlockSpec((d, 128), lambda j: (j, 0)),
            pl.BlockSpec((1, d), lambda j: (0, j)),
            whole((n, 1)),
            whole((n, 640)),
            whole((n, 640)),
        ],
        [pl.BlockSpec((n, d), lambda j: (0, j)), whole((n, 128))],
        [jax.ShapeDtypeStruct((n, 3 * d), BF), jax.ShapeDtypeStruct((n, 128), BF)],
        flops=2 * n * d * 3 * d,
        moved=8 * d * d + 12 * n * d,
    )(x, pack, pack, bt, bias, adapter, cos_t, sin_t)


def attend_body(q_ref, k_ref, v_ref, qm_ref, km_ref, out_ref, lse_ref):
    rows = q_ref.shape[0]
    step = 256
    factor = LOG2E / math.sqrt(HD)
    lanes = lax.broadcasted_iota(jnp.int32, (step, 128), 1)
    for i in range(0, rows, step):
        lse_ref[i : i + step, :] = jnp.zeros((step, 128), F32)
    for h in range(8):
        cols = slice(HD * h, HD * h + HD)
        keys = jnp.concatenate([k_ref[:, cols], km_ref[...]], axis=1)
        vals = v_ref[:, cols]
        for i in range(0, rows, step):
            query = jnp.concatenate([q_ref[i : i + step, cols], qm_ref[i : i + step, :]], axis=1)
            s = mm_nt(query, keys)
            top = jnp.max(s, axis=1, keepdims=True)
            e = jnp.exp2((s - top) * factor)
            total = jnp.sum(e, axis=1, keepdims=True)
            o = mm(e.astype(BF), vals) * (1.0 / total)
            out_ref[i : i + step, cols] = o.astype(BF)
            lse = top + jnp.log(total) * math.sqrt(HD)
            lse_ref[i : i + step, :] = jnp.where(lanes == h, lse, lse_ref[i : i + step, :])


def attend_call(qkv, qm, km):
    n = qkv.shape[0]
    d = qkv.shape[1] // 3
    groups = d // 640
    return call(
        attend_body,
        "attend",
        (groups,),
        [
            pl.BlockSpec((n, 640), lambda g: (0, g)),
            pl.BlockSpec((n, 640), lambda g: (0, groups + g)),
            pl.BlockSpec((n, 640), lambda g: (0, 2 * groups + g)),
            whole((n, 48)),
            whole((n, 48)),
        ],
        [pl.BlockSpec((n, 640), lambda g: (0, g)), pl.BlockSpec((n, 128), lambda g: (0, g))],
        [jax.ShapeDtypeStruct((n, d), BF), jax.ShapeDtypeStruct((n, 128 * groups), F32)],
        flops=4 * n * n * d,
        moved=8 * n * d,
    )(qkv, qkv, qkv, qm, km)


def split_low(values, count):
    parts = []
    for _ in range(count):
        part = values.astype(BF)
        parts.append(part)
        values = values - part.astype(F32)
    return parts


def attend_back_body(
    q_ref, k_ref, v_ref, g_ref, o_ref, lse_ref, qm_ref, km_ref, cos_ref, sin_ref,
    dq_ref, dk_ref, dv_ref, dq_s, dk_s,
):
    rows = q_ref.shape[0]
    step = 256
    factor = LOG2E / math.sqrt(HD)
    scale = 1.0 / math.sqrt(HD)
    lanes = lax.broadcasted_iota(jnp.int32, (rows, 48), 1)
    ones_two = jnp.where((lanes == 16) | (lanes == 17), 1.0, 0.0).astype(BF)
    for h in range(8):
        cols = slice(HD * h, HD * h + HD)
        gh = g_ref[:, cols]
        delta = jnp.sum(gh.astype(F32) * o_ref[:, cols].astype(F32), axis=1, keepdims=True)
        d_hi, d_lo = split_low(-delta, 2)
        l_hi, l_mid, l_lo = split_low(-lse_ref[:, h : h + 1], 3)
        q_aug = jnp.where(
            lanes == 16,
            l_hi.astype(F32),
            jnp.where(
                lanes == 17,
                l_mid.astype(F32),
                jnp.where(lanes == 18, l_lo.astype(F32), qm_ref[...].astype(F32)),
            ),
        ).astype(BF)
        g_aug = jnp.where(
            lanes == 16, d_hi.astype(F32), jnp.where(lanes == 17, d_lo.astype(F32), 0.0)
        ).astype(BF)
        query = jnp.concatenate([q_ref[:, cols], q_aug], axis=1)
        grads = jnp.concatenate([gh, g_aug], axis=1)
        keys = jnp.concatenate([k_ref[:, cols], km_ref[...]], axis=1)
        vals = jnp.concatenate([v_ref[:, cols], ones_two], axis=1)
        keys_t = keys.T
        dk = jnp.zeros((rows, 128), F32)
        dv = jnp.zeros((rows, 128), F32)
        for i in range(0, rows, step):
            qb = query[i : i + step, :]
            gb = grads[i : i + step, :]
            p = jnp.exp2(mm_nt(keys, qb) * factor)
            dp = mm_nt(vals, gb)
            ds = (p * dp).astype(BF)
            dv = dv + mm(p.astype(BF), gb)
            dk = dk + mm(ds, qb)
            dq = mm(keys_t, ds)
            dq_s[i : i + step, cols] = dq.T[:, :HD]
        dk_s[:, cols] = dk[:, :HD]
        dv_ref[:, cols] = dv[:, :HD].astype(BF)
    low = lax.broadcasted_iota(jnp.int32, (step, 640), 1) % HD < HD // 2
    for i in range(0, rows, step):
        sl = slice(i, i + step)
        for src, dst in ((dq_s, dq_ref), (dk_s, dk_ref)):
            piece = src[sl, :] * scale
            dst[sl, :] = (piece * cos_ref[sl, :] - turn(piece, low) * sin_ref[sl, :]).astype(BF)


def attend_back_call(qkv, grads, attended, lse, qm, km, cos_t, sin_t):
    n = qkv.shape[0]
    d = qkv.shape[1] // 3
    groups = d // 640
    block = pl.BlockSpec((n, 640), lambda g: (0, g))
    return call(
        attend_back_body,
        "attend_back",
        (groups,),
        [
            block,
            pl.BlockSpec((n, 640), lambda g: (0, groups + g)),
            pl.BlockSpec((n, 640), lambda g: (0, 2 * groups + g)),
            block,
            block,
            pl.BlockSpec((n, 128), lambda g: (0, g)),
            whole((n, 48)),
            whole((n, 48)),
            whole((n, 640)),
            whole((n, 640)),
        ],
        [block, block, block],
        [jax.ShapeDtypeStruct((n, d), BF)] * 3,
        [pltpu.VMEM((n, 640), F32), pltpu.VMEM((n, 640), F32)],
        flops=10 * n * n * d,
        moved=16 * n * d,
    )(qkv, qkv, qkv, grads, attended, lse, qm, km, cos_t, sin_t)


def tables(picture, patch_row, patch_col):
    cosine, sine = rotary_tables(patch_row, patch_col, HD)
    half = HD // 2
    signed = jnp.concatenate([-sine[:, :half], sine[:, half:]], axis=1)
    count = picture.shape[0]
    change = (picture[1:] != picture[:-1]).astype(jnp.int32)
    places = lax.broadcasted_iota(jnp.int32, (count, count - 1), 0)
    before = lax.broadcasted_iota(jnp.int32, (count, count - 1), 1) < places
    index = jnp.sum(jnp.where(before, change[None, :], 0), axis=1)
    lanes = lax.broadcasted_iota(jnp.int32, (1, 48), 1)
    own = lanes == index[:, None]
    qm = jnp.where(own | (lanes >= 16), 0.0, -BIG).astype(BF)
    km = (own | ((lanes >= 16) & (lanes < 19))).astype(BF)
    return (*widen_call(cosine, signed), qm, km)


def stats(values):
    centre = jnp.mean(values, axis=-1, keepdims=True)
    centred = values - centre
    spread = lax.rsqrt(jnp.mean(centred * centred, axis=-1, keepdims=True) + EPS)
    return centred * spread, spread


def once(shape, index):
    return pl.BlockSpec(shape, index, pipeline_mode=pl.Buffered(1))


def proj_body(
    att_ref, w_ref, a_ref, bt_ref, bias_ref, ad_ref, tok_ref, gain_ref, shift_ref,
    mid_ref, norm_ref, inner_ref,
):
    rows = att_ref.shape[0]
    x = att_ref[...]
    inner = (mm(x, a_ref[...]) * pick(ad_ref, rows)).astype(BF)
    inner_ref[...] = inner
    middle = tok_ref[...].astype(F32) + (mm(x, w_ref[...]) + bias_ref[...] + mm_nt(inner, bt_ref[...]))
    mid_ref[...] = middle
    unit, _ = stats(middle)
    norm_ref[...] = (unit * gain_ref[...] + shift_ref[...]).astype(BF)


def proj_call(att, pack, first_col, a_col, bt_col, bias, adapter, tokens, gain, shift):
    n, d = att.shape
    step = 256
    row = pl.BlockSpec((step, d), lambda i: (i, 0))
    return call(
        proj_body,
        "proj_norm",
        (n // step,),
        [
            row,
            once((d, d), lambda i: (0, first_col // d)),
            once((d, 128), lambda i: (0, a_col // 128)),
            once((d, 128), lambda i: (0, bt_col // 128)),
            whole((1, d)),
            pl.BlockSpec((step, 1), lambda i: (i, 0)),
            row,
            whole((1, d)),
            whole((1, d)),
        ],
        [row, row, pl.BlockSpec((step, 128), lambda i: (i, 0))],
        [
            jax.ShapeDtypeStruct((n, d), F32),
            jax.ShapeDtypeStruct((n, d), BF),
            jax.ShapeDtypeStruct((n, 128), BF),
        ],
        flops=2 * n * d * d,
        moved=2 * d * d + 10 * n * d,
    )(att, pack, pack, pack, bias, adapter, tokens, gain, shift)


def feed_body(*refs, parts, first, last):
    refs = list(refs)
    take = lambda count: [refs.pop(0) for _ in range(count)]
    x_ref, g_ref = take(2)
    w1, w2, bt1, a2, b1 = take(parts), take(parts), take(parts), take(parts), take(parts)
    ad_ref, a1_ref, bt2_ref = take(3)
    if first:
        base_ref, b2_ref = take(2)
    else:
        base_ref, gx_in, in1_ref, ig2_ref, in2_in, ig1_in = take(6)
        val_ref = take(1)[0]
    if first:
        acc_ref, gx_ref, in1_out, ig2_out, in2_out, ig1_out = take(6)
    if last:
        out_ref, gx_ref, ta1_ref, tb2_ref = take(4)
    ta2, tb1 = take(parts), take(parts)
    if last:
        ta1_s, tb2_s = take(2)
    ta2_s, tb1_s = take(parts), take(parts)
    sums = ta2_s + tb1_s + ([ta1_s, tb2_s] if last else [])
    i = pl.program_id(0)
    end = i == pl.num_programs(0) - 1

    @pl.when(i == 0)
    def _():
        for ref in sums:
            ref[...] = jnp.zeros_like(ref)

    sub = 256
    jobs = []
    for begin in range(0, x_ref.shape[0], sub):
        sl = pl.ds(begin, sub)
        x = x_ref[sl, :]
        g = g_ref[sl, :]
        sel = pick(ad_ref.at[sl, :], sub)
        if first:
            in1 = (mm(x, a1_ref[...]) * sel).astype(BF)
            ig2 = (mm(g, bt2_ref[...]) * sel).astype(BF)
            in1_out[sl, :] = in1
            ig2_out[sl, :] = ig2
            acc = base_ref[sl, :] + b2_ref[...]
            gx = in2 = ig1 = None
        else:
            in1 = in1_ref[sl, :]
            ig2 = ig2_ref[sl, :]
            acc, gx, in2, ig1 = base_ref[sl, :], gx_in[sl, :], in2_in[sl, :], ig1_in[sl, :]
        hs = [mm(x, w1[q][...]) + mm_nt(in1, bt1[q][...]) + b1[q][...] for q in range(parts)]
        gas = [mm_nt(g, w2[q][...]) + mm_nt(ig2, a2[q][...]) for q in range(parts)]
        jobs.append((sl, x, g, sel, in1, ig2, acc, gx, in2, ig1, hs, gas))
    lows = []
    for job in jobs:
        pairs = []
        for h, ga in zip(*job[-2:]):
            s = 0.5 * jnp.tanh(0.851 * h) + 0.5
            pairs.append(((h * s).astype(BF), (ga * (s + 1.702 * h * s * (1.0 - s))).astype(BF)))
        lows.append(pairs)
    for job, pairs in zip(jobs, lows):
        sl, x, g, sel, in1, ig2, acc, gx, in2, ig1, _, _ = job
        in1_t = in1.T
        ig2_t = ig2.T
        for q, (act, gh) in enumerate(pairs):
            more = (mm_nt(gh, w1[q][...]), mm(act, a2[q][...]), mm(gh, bt1[q][...]))
            acc = acc + mm(act, w2[q][...])
            gx, in2, ig1 = more if gx is None else (gx + more[0], in2 + more[1], ig1 + more[2])
            ta2_s[q][...] += mm(ig2_t, act)
            tb1_s[q][...] += mm(in1_t, gh)
        if last:
            low2 = (in2 * sel).astype(BF)
            low1 = (ig1 * sel).astype(BF)
            out_ref[sl, :] = ((acc + mm_nt(low2, bt2_ref[...])) * val_ref[sl, :]).astype(BF)
            gx_ref[sl, :] = gx + mm_nt(low1, a1_ref[...])
            ta1_s[...] += mm(low1.T, x)
            tb2_s[...] += mm(low2.T, g)
        else:
            acc_ref[sl, :] = acc
            gx_ref[sl, :] = gx
            in2_out[sl, :] = in2
            ig1_out[sl, :] = ig1

    @pl.when(end)
    def _():
        for q in range(parts):
            ta2[q][...] = ta2_s[q][...].T.astype(BF)
            tb1[q][...] = tb1_s[q][...].T.astype(BF)
        if last:
            ta1_ref[...] = ta1_s[...].T.astype(BF)
            tb2_ref[...] = tb2_s[...].T.astype(BF)


def feed_call(x, grads, w2, w1, bt1, a2, b1, adapter, a1, bt2, state, first, last):
    n, d = x.shape
    parts = len(w1)
    step = 512 if parts < 3 else 256
    row = pl.BlockSpec((step, d), lambda i: (i, 0))
    thin_row = pl.BlockSpec((step, 128), lambda i: (i, 0))
    one = pl.BlockSpec((step, 1), lambda i: (i, 0))
    thin = once((d, 128), lambda i: (0, 0))
    line = once((1, d), lambda i: (0, 0))

    def wide(col):
        return once((d, d), lambda i: (0, col // d))

    def narrow(col):
        return once((d, 128), lambda i: (0, col // 128))

    in_specs = [row, row] + [wide(c) for _, c in w1] + [wide(c) for _, c in w2]
    in_specs += [narrow(c) for _, c in bt1] + [narrow(c) for _, c in a2] + [line] * parts
    in_specs += [one, narrow(a1[1]), narrow(bt2[1])]
    args = [x, grads] + [v for v, _ in w1 + w2 + bt1 + a2] + list(b1) + [adapter, a1[0], bt2[0]]
    if first:
        in_specs += [row, line]
    else:
        in_specs += [row, row, thin_row, thin_row, thin_row, thin_row, one]
    args += list(state)
    out_specs, out_shape, scratch = [], [], []
    if first:
        out_specs += [row, row, thin_row, thin_row, thin_row, thin_row]
        out_shape += [jax.ShapeDtypeStruct((n, d), F32)] * 2
        out_shape += [jax.ShapeDtypeStruct((n, 128), BF)] * 2 + [jax.ShapeDtypeStruct((n, 128), F32)] * 2
    if last:
        out_specs += [row, row, thin, thin]
        out_shape += [jax.ShapeDtypeStruct((n, d), BF), jax.ShapeDtypeStruct((n, d), F32)]
        out_shape += [jax.ShapeDtypeStruct((d, 128), BF)] * 2
        scratch += [pltpu.VMEM((128, d), F32)] * 2
    out_specs += [thin] * (2 * parts)
    out_shape += [jax.ShapeDtypeStruct((d, 128), BF)] * (2 * parts)
    scratch += [pltpu.VMEM((128, d), F32)] * (2 * parts)
    return call(
        functools.partial(feed_body, parts=parts, first=first, last=last),
        "feed_first" if first else "feed_last",
        (n // step,),
        in_specs,
        out_specs,
        out_shape,
        scratch,
        flops=8 * n * d * d * parts,
        moved=4 * d * d * parts + 24 * n * d,
    )(*args)


def proj_back_body(
    gx_ref, mid_ref, cot_ref, val_ref, gain_ref, w_ref, a_ref, bt_ref, ad_ref, att_ref, inner_ref,
    gm_ref, ga_ref, ta_ref, tb_ref, ta_s, tb_s,
):
    i = pl.program_id(0)
    sub = 256

    @pl.when(i == 0)
    def _():
        ta_s[...] = jnp.zeros_like(ta_s)
        tb_s[...] = jnp.zeros_like(tb_s)

    for begin in range(0, gx_ref.shape[0], sub):
        sl = pl.ds(begin, sub)
        unit, spread = stats(mid_ref[sl, :])
        gm = cot_ref[sl, :].astype(F32) * val_ref[sl, :]
        gm = gm + normalize_back(gx_ref[sl, :], unit, spread, gain_ref[...])
        gm_ref[sl, :] = gm
        gb = gm.astype(BF)
        ig = (mm(gb, bt_ref[...]) * pick(ad_ref.at[sl, :], sub)).astype(BF)
        ga_ref[sl, :] = (mm_nt(gb, w_ref[...]) + mm_nt(ig, a_ref[...])).astype(BF)
        ta_s[...] += mm(ig.T, att_ref[sl, :])
        tb_s[...] += mm(inner_ref[sl, :].T, gb)

    @pl.when(i == pl.num_programs(0) - 1)
    def _():
        ta_ref[...] = ta_s[...].T.astype(BF)
        tb_ref[...] = tb_s[...].T.astype(BF)


def proj_back_call(gx, middle, cot, valid, gain, pack, first_col, a_col, bt_col, adapter, att, inner):
    n, d = gx.shape
    step = 256
    row = pl.BlockSpec((step, d), lambda i: (i, 0))
    one = pl.BlockSpec((step, 1), lambda i: (i, 0))
    thin = once((d, 128), lambda i: (0, 0))
    return call(
        proj_back_body,
        "proj_back",
        (n // step,),
        [
            row,
            row,
            row,
            one,
            whole((1, d)),
            once((d, d), lambda i: (0, first_col // d)),
            once((d, 128), lambda i: (0, a_col // 128)),
            once((d, 128), lambda i: (0, bt_col // 128)),
            one,
            row,
            pl.BlockSpec((step, 128), lambda i: (i, 0)),
        ],
        [row, row, thin, thin],
        [
            jax.ShapeDtypeStruct((n, d), F32),
            jax.ShapeDtypeStruct((n, d), BF),
            jax.ShapeDtypeStruct((d, 128), BF),
            jax.ShapeDtypeStruct((d, 128), BF),
        ],
        [pltpu.VMEM((128, d), F32), pltpu.VMEM((128, d), F32)],
        flops=2 * n * d * d,
        moved=2 * d * d + 18 * n * d,
    )(gx, middle, cot, valid, gain, pack, pack, pack, adapter, att, inner)


def qkv_terms_body(gq_ref, gk_ref, gv_ref, x_ref, bt_ref, inner_ref, ad_ref, ig_ref, ta_ref, tb_ref, ta_s, tb_s):
    i = pl.program_id(0)
    rows, d = x_ref.shape

    @pl.when(i == 0)
    def _():
        ta_s[...] = jnp.zeros_like(ta_s)
        tb_s[...] = jnp.zeros_like(tb_s)

    inner_t = inner_ref[...].T
    total = None
    for part, ref in enumerate((gq_ref, gk_ref, gv_ref)):
        g = ref[...]
        sl = slice(part * d, part * d + d)
        piece = mm(g, bt_ref[sl, :])
        total = piece if total is None else total + piece
        tb_s[:, sl] += mm(inner_t, g)
    ig = (total * pick(ad_ref, rows)).astype(BF)
    ig_ref[...] = ig
    ta_s[...] += mm(ig.T, x_ref[...])

    @pl.when(i == pl.num_programs(0) - 1)
    def _():
        ta_ref[...] = ta_s[...].T.astype(BF)
        tb_ref[...] = tb_s[...].T.astype(BF)


def qkv_terms_call(gq, gk, gv, x, bt, inner, adapter):
    n, d = x.shape
    step = 256
    row = pl.BlockSpec((step, d), lambda i: (i, 0))
    thin_row = pl.BlockSpec((step, 128), lambda i: (i, 0))
    return call(
        qkv_terms_body,
        "qkv_terms",
        (n // step,),
        [row, row, row, row, whole(bt.shape), thin_row, pl.BlockSpec((step, 1), lambda i: (i, 0))],
        [thin_row, whole((d, 128)), whole((3 * d, 128))],
        [
            jax.ShapeDtypeStruct((n, 128), BF),
            jax.ShapeDtypeStruct((d, 128), BF),
            jax.ShapeDtypeStruct((3 * d, 128), BF),
        ],
        [pltpu.VMEM((128, d), F32), pltpu.VMEM((128, 3 * d), F32)],
        flops=4 * n * d * 128 * 4,
        moved=10 * n * d,
    )(gq, gk, gv, x, bt, inner, adapter)


def qkv_back_body(gq_ref, gk_ref, gv_ref, w_ref, ig_ref, a_ref, tok_ref, gain_ref, gm_ref, out_ref, acc_ref):
    part = pl.program_id(0)
    sub = 256
    pieces = [pl.ds(begin, sub) for begin in range(0, tok_ref.shape[0], sub)]

    @pl.when(part == 0)
    def _():
        for sl in pieces:
            acc_ref[sl, :] = mm_nt(gq_ref[sl, :], w_ref[...]) + mm_nt(ig_ref[sl, :], a_ref[...])

    @pl.when(part == 1)
    def _():
        for sl in pieces:
            acc_ref[sl, :] += mm_nt(gk_ref[sl, :], w_ref[...])

    @pl.when(part == 2)
    def _():
        for sl in pieces:
            grad = acc_ref[sl, :] + mm_nt(gv_ref[sl, :], w_ref[...])
            unit, spread = stats(tok_ref[sl, :].astype(F32))
            out_ref[sl, :] = gm_ref[sl, :] + normalize_back(grad, unit, spread, gain_ref[...])


def qkv_back_call(gq, gk, gv, pack, ig, tokens, gain, gm, half):
    n, d = tokens.shape
    rows = n // 2
    row = pl.BlockSpec((rows, d), lambda p: (half, 0))
    return pl.pallas_call(
        qkv_back_body,
        name="qkv_back",
        grid=(3,),
        in_specs=[
            row,
            row,
            row,
            pl.BlockSpec((d, d), lambda p: (0, p)),
            pl.BlockSpec((rows, 128), lambda p: (half, 0)),
            once((d, 128), lambda p: (0, 3 * d // 128)),
            row,
            whole((1, d)),
            row,
        ],
        out_specs=row,
        out_shape=jax.ShapeDtypeStruct((n, d), F32),
        scratch_shapes=[pltpu.VMEM((rows, d), F32)],
        input_output_aliases={8: 0},
        cost_estimate=pl.CostEstimate(flops=3 * n * d * d, transcendentals=0, bytes_accessed=6 * d * d + 9 * n * d),
        compiler_params=pltpu.CompilerParams(
            dimension_semantics=("arbitrary",), vmem_limit_bytes=56 * 1024 * 1024
        ),
    )(gq, gk, gv, pack, ig, pack, tokens, gain, gm)


def unfold_rows(block, devices):
    rows = block.shape[0] // devices
    pieces = block.shape[1] // 128
    split = block.reshape(devices, rows, pieces, 128)
    return split.transpose(0, 2, 1, 3).reshape(-1, 128)


def gather_rows(packed):
    return lax.all_gather(packed, ("dp", "fsdp"), axis=0, tiled=True)


def place_body(table_ref, *refs, pieces):
    out_ref = refs[-1]
    mask = table_ref[2]
    begin = 0
    for ref in refs[:pieces]:
        end = begin + ref.shape[-1]
        for k in range(ref.shape[1]):
            out_ref[mask ^ k, 0, 0, :, begin:end] = ref[0, k]
        begin = end


class Gather:
    def __init__(self, *parts):
        self.zs, self.fs = lax.axis_size("dp") // 2, lax.axis_size("fsdp")
        self.rows, self.cols = parts[0].shape[0], sum(p.shape[1] for p in parts)
        self.parts = list(parts)
        self.phase = 0

    def swap(self, value, axis, mask):
        return lax.ppermute(value, axis, [(i, i ^ mask) for i in range(lax.axis_size(axis))])

    def start(self):
        z_masks, f_masks = list(range(2, 2 * self.zs, 2)), list(range(1, self.fs))
        orders = [[("dp", z_masks), ("fsdp", f_masks)], [("fsdp", f_masks), ("dp", z_masks)]]
        self.got = []
        for part, order in zip(self.parts, orders):
            axis, masks = order[self.phase] if self.phase < 2 else ("dp", [1])
            self.got.append([part] + [self.swap(part, axis, m) for m in masks])

    def finish(self, *others):
        sizes = [len(group) for group in self.got]
        held = lax.optimization_barrier(tuple(v for group in self.got for v in group) + others)
        groups, at = [], 0
        for size in sizes:
            groups.append(held[at : at + size])
            at += size
        if self.phase == 0:
            self.parts = [jnp.stack(group) for group in groups]
        elif self.phase == 1:
            self.parts = [jnp.stack(group, axis=1 if i else 0) for i, group in enumerate(groups)]
        if self.phase < 2:
            held = lax.optimization_barrier(tuple(self.parts) + tuple(held[at:]))
            self.parts = list(held[: len(sizes)])
            at = len(sizes)
        else:
            self.far = [group[1] for group in groups[::-1]]
        self.phase += 1
        return held[at:]

    def place(self, side, earlier):
        zs, fs, rows, cols = self.zs, self.fs, self.rows, self.cols
        spot, column = lax.axis_index("dp"), lax.axis_index("fsdp")
        table = jnp.stack([(spot & 1) ^ side, column, spot >> 1]).astype(jnp.int32)
        parts = self.far if side else self.parts[::-1]
        specs = [pl.BlockSpec((1, zs, rows, p.shape[-1]), lambda m, t: (m, 0, 0, 0)) for p in parts]
        specs += [pl.BlockSpec(memory_space=pl.ANY)] * len(earlier)
        return pl.pallas_call(
            functools.partial(place_body, pieces=len(parts)),
            name="place_blocks",
            grid_spec=pltpu.PrefetchScalarGridSpec(
                num_scalar_prefetch=1,
                grid=(fs,),
                in_specs=specs,
                out_specs=pl.BlockSpec((zs, 1, 1, rows, cols), lambda m, t: (0, t[0], t[1] ^ m, 0, 0)),
            ),
            out_shape=jax.ShapeDtypeStruct((zs, 2, fs, rows, cols), BF),
            input_output_aliases={1 + len(parts): 0} if earlier else {},
            cost_estimate=pl.CostEstimate(flops=0, transcendentals=0, bytes_accessed=4 * zs * fs * rows * cols),
            compiler_params=pltpu.CompilerParams(vmem_limit_bytes=48 * 1024 * 1024),
        )(table, *parts, *earlier)


def widen_body(cos_ref, sin_ref, cos_out, sin_out):
    for src, dst in ((cos_ref, cos_out), (sin_ref, sin_out)):
        value = src[...]
        dst[...] = jnp.concatenate([value] * 8, axis=1)


def widen_call(cosine, signed):
    n = cosine.shape[0]
    out = jax.ShapeDtypeStruct((n, 8 * HD), F32)
    specs = [whole((n, 8 * HD))] * 2
    return call(widen_body, "widen_tables", (1,), [whole(cosine.shape)] * 2, specs, [out, out], moved=72 * n * HD)(
        cosine, signed
    )


def pack_body(
    qkv_w, proj_w, fc1_w, fc2_w, qkv_a, proj_a, fc1_a, fc2_a, qkv_b, proj_b, fc1_b, fc2_b, *outs, devices, cut, groups
):
    rows, d = proj_w.shape
    quarters = fc1_w.shape[1] // d

    def turned(ref):
        flipped = ref[...].astype(F32)
        return [flipped[i * rows : (i + 1) * rows].astype(BF) for i in range(flipped.shape[0] // rows)]

    def fill(out, pieces):
        at = 0
        for piece in pieces:
            out[:, at : at + piece.shape[1]] = piece
            at += piece.shape[1]

    fill(outs[1], [qkv_w[:, :cut]])
    fill(outs[0], [qkv_w[:, cut:], qkv_a[...]] + turned(qkv_b))
    up1 = turned(fc1_b)
    for out, group in zip(outs[2:], groups):
        pieces = [fc2_w[q * rows : (q + 1) * rows, :] for q in group]
        for q in group:
            starts = [(i * quarters + q) * rows for i in range(devices)]
            pieces.append(jnp.concatenate([fc1_w[:, c : c + rows] for c in starts], axis=1))
        if group[0] == 0:
            pieces.append(proj_w[...])
        pieces += [up1[q] for q in group]
        pieces += [fc2_a[q * rows : (q + 1) * rows, :] for q in group]
        if group[0] == 0:
            pieces += [fc1_a[...], proj_a[...]] + turned(proj_b) + turned(fc2_b)
        fill(out, pieces)


def pack_call(arrays, devices, groups):
    rows, d = arrays[1].shape
    total = arrays[0].shape[1] + 4 * 128
    cut = total // 128 // 3 * 128
    widths = [total - cut, cut] + [len(g) * (2 * d + 256) + (d + 512 if g[0] == 0 else 0) for g in groups]
    return call(
        functools.partial(pack_body, devices=devices, cut=cut, groups=groups),
        "pack_shards",
        (1,),
        [whole(v.shape) for v in arrays],
        [whole((rows, w)) for w in widths],
        [jax.ShapeDtypeStruct((rows, w), BF) for w in widths],
        moved=4 * rows * sum(widths),
    )(*arrays)


class Scatter:
    def __init__(self, terms):
        zs, fs = lax.axis_size("dp") // 2, lax.axis_size("fsdp")
        self.values = [t.reshape(zs, 2, fs, -1, 128) for t in terms]
        self.phases = [("dp", 1, [1]), ("fsdp", 1, list(range(1, fs))), ("dp", 0, list(range(2, 2 * zs, 2)))]
        self.open = None

    def start(self):
        axis, dim, masks = self.phases.pop(0)
        size = lax.axis_size(axis)
        place = lax.axis_index(axis)
        shift = 0
        if axis == "dp":
            place, shift = (place & 1, 0) if dim else (place >> 1, 1)

        def pick_one(at):
            found = [lax.dynamic_index_in_dim(v, at, dim, keepdims=False) for v in self.values]
            return found[0] if len(found) == 1 else jnp.concatenate(found, axis=-2)

        sends = [pick_one(place ^ (mask >> shift)).astype(BF) for mask in masks]
        got = [lax.ppermute(v, axis, [(i, i ^ mask) for i in range(size)]) for v, mask in zip(sends, masks)]
        self.open = (lambda: pick_one(place), got)

    def finish(self, *others):
        mine, got = self.open
        held = lax.optimization_barrier(tuple(got) + others)
        total = mine().astype(F32)
        for piece in held[: len(got)]:
            total = total + piece.astype(F32)
        self.values = [total]
        return held[len(got) :]


def local(
    tokens,
    cotangent,
    picture,
    adapter,
    patch_row,
    patch_col,
    qkv_weight,
    qkv_bias,
    proj_weight,
    proj_bias,
    fc1_weight,
    fc1_bias,
    fc2_weight,
    fc2_bias,
    norm1_gain,
    norm1_bias,
    norm2_gain,
    norm2_bias,
    qkv_down,
    qkv_up,
    proj_down,
    proj_up,
    fc1_down,
    fc1_up,
    fc2_down,
    fc2_up,
):
    devices = lax.axis_size(("dp", "fsdp"))
    rows, d = proj_weight.shape
    quarters = fc1_weight.shape[1] // d
    q_cols = qkv_weight.shape[1]
    groups = [list(range(quarters - 1)), [quarters - 1]]
    shards = (qkv_weight, proj_weight, fc1_weight, fc2_weight, qkv_down, proj_down, fc1_down, fc2_down)
    shards += (qkv_up.T, proj_up.T, fc1_up.T, fc2_up.T)
    part_b, part_a, pack_a, pack_b = pack_call(shards, devices, groups)
    one = Gather(part_b, part_a)
    one.start()

    def spots(source, count, extra):
        wide = [(source, q * d) for q in range(2 * count)]
        base = (2 * count + extra) * d
        thin = [(source, base + q * 128) for q in range(2 * count)]
        return [wide[:count], wide[count:], thin[:count], thin[count:]]

    count = len(groups[0])
    row_count = tokens.shape[0]
    unit_one, _ = stats(tokens.astype(F32))
    normed = (unit_one * norm1_gain + norm1_bias).astype(BF)
    (normed,) = one.finish(normed)
    second = gather_rows(pack_a)
    third = gather_rows(pack_b)
    proj_col = 2 * count * d
    a1_col = proj_col + d + 2 * count * 128
    ap_col, btp_col, bt2_col = a1_col + 128, a1_col + 256, a1_col + 384
    one.start()
    ad = adapter[:, None]
    valid = (picture >= 0).astype(F32)[:, None]
    grad_low = (cotangent.astype(F32) * valid).astype(BF)
    bias1 = fc1_bias.reshape(devices, quarters, rows).transpose(1, 0, 2).reshape(quarters, 1, d)
    small = [qkv_bias[None], proj_bias[None], norm1_gain[None], norm2_gain[None], norm2_bias[None], fc2_bias[None]]
    small += [bias1[q] for q in range(quarters)] + [ad, valid, grad_low, *tables(picture, patch_row, patch_col)]
    small = one.finish(*small)
    bias_qkv, bias_proj, gain1, gain2, shift2, bias2, *bias1 = small[: 6 + quarters]
    ad, valid, grad_low, cos_t, sin_t, qm, km = small[6 + quarters :]
    one.start()
    first = one.place(0, ())
    (first,) = one.finish(first)
    first = one.place(1, (first,)).reshape(devices * rows, -1)
    bt_qkv = unfold_rows(first[:, q_cols + 128 :], devices)
    qkv, inner_qkv = qkv_call(normed, first, bt_qkv, bias_qkv, ad, cos_t, sin_t)
    attended, lse = attend_call(qkv, qm, km)
    middle, normed_two, inner_proj = proj_call(
        attended, second, proj_col, ap_col, btp_col, bias_proj, ad, tokens, gain2, shift2
    )
    a1, bt2 = (second, a1_col), (second, bt2_col)
    early = spots(second, count, 1)
    final = spots(third, quarters - count, 0)
    acc, grad_x, in1, ig2, in2, ig1, *terms_a = feed_call(
        normed_two, grad_low, *early, bias1[:count], ad, a1, bt2, (middle, bias2), True, False
    )
    na, nb = count, quarters - count
    state = (acc, grad_x, in1, ig2, in2, ig1, valid)
    block_out, grad_two, ta_fc1, tb_fc2, *terms_b = feed_call(
        normed_two, grad_low, *final, bias1[count:], ad, a1, bt2, state, False, True
    )

    feed_sum = Scatter([ta_fc1, *terms_a[na:], *terms_b[nb:], *terms_a[:na], *terms_b[:nb], tb_fc2])
    feed_sum.start()
    grad_middle, grad_att, ta_proj, tb_proj = proj_back_call(
        grad_two, middle, cotangent, valid, gain2, second, proj_col, ap_col, btp_col, ad, attended, inner_proj
    )
    (grad_att,) = feed_sum.finish(grad_att)
    feed_sum.start()
    grads = attend_back_call(qkv, grad_att, attended, lse, qm, km, cos_t, sin_t)
    gq, gk, gv = feed_sum.finish(*grads)
    feed_sum.start()
    ig_qkv, ta_qkv, tb_qkv = qkv_terms_call(gq, gk, gv, normed, bt_qkv, inner_qkv, ad)
    ig_qkv, ta_qkv, tb_qkv = feed_sum.finish(ig_qkv, ta_qkv, tb_qkv)
    last_sum = Scatter([ta_proj, tb_proj, ta_qkv, tb_qkv])
    last_sum.start()
    back = functools.partial(qkv_back_call, gq, gk, gv, first, ig_qkv, tokens, gain1)
    held = back(grad_middle, 0)
    (held,) = last_sum.finish(held)
    last_sum.start()
    tokens_grad = back(held, 1)
    (tokens_grad,) = last_sum.finish(tokens_grad)
    last_sum.start()
    last_sum.finish()
    early, late = feed_sum.values[0], last_sum.values[0]
    factor = 1.0 / math.sqrt(row_count * devices)
    early = factor * early
    late = factor * late
    return (
        block_out,
        tokens_grad,
        late[2 * rows : 3 * rows],
        late[3 * rows :].T,
        late[:rows],
        late[rows : 2 * rows].T,
        early[:rows],
        early[rows : rows * (1 + quarters)].T,
        early[rows * (1 + quarters) : rows * (1 + 2 * quarters)],
        early[rows * (1 + 2 * quarters) :].T,
    )


def solution(mesh):
    return jax.shard_map(
        local,
        mesh=mesh,
        in_specs=(
            P(("dp", "fsdp"), None),
            P(("dp", "fsdp"), None),
            P(("dp", "fsdp")),
            P(("dp", "fsdp")),
            P(("dp", "fsdp")),
            P(("dp", "fsdp")),
            P(("dp", "fsdp"), None),
            P(),
            P(("dp", "fsdp"), None),
            P(),
            P(("dp", "fsdp"), None),
            P(),
            P(("dp", "fsdp"), None),
            P(),
            P(),
            P(),
            P(),
            P(),
            P(("dp", "fsdp"), None),
            P(None, ("dp", "fsdp")),
            P(("dp", "fsdp"), None),
            P(None, ("dp", "fsdp")),
            P(("dp", "fsdp"), None),
            P(None, ("dp", "fsdp")),
            P(("dp", "fsdp"), None),
            P(None, ("dp", "fsdp")),
        ),
        out_specs=(
            P(("dp", "fsdp"), None),
            P(("dp", "fsdp"), None),
            P(("dp", "fsdp"), None),
            P(None, ("dp", "fsdp")),
            P(("dp", "fsdp"), None),
            P(None, ("dp", "fsdp")),
            P(("dp", "fsdp"), None),
            P(None, ("dp", "fsdp")),
            P(("dp", "fsdp"), None),
            P(None, ("dp", "fsdp")),
        ),
        check_vma=False,
    )
```

```python
import functools
import math

import jax
import jax.numpy as jnp
from jax import lax
from jax.experimental import pallas as pl
from jax.experimental.pallas import tpu as pltpu
from jax.sharding import PartitionSpec as P

HEADS = 16
HD = 80
RANK = 16


EPS = 1e-06


BIG = 2.0**60
LOG2E = 1.4426950408889634
BF = jnp.bfloat16
F32 = jnp.float32


def normalize_back(grad_out, unit, spread, gain):
    scaled = grad_out * gain
    return spread * (
        scaled
        - jnp.mean(scaled, axis=-1, keepdims=True)
        - unit * jnp.mean(scaled * unit, axis=-1, keepdims=True)
    )


def rotary_tables(patch_row, patch_col, head_size):
    quarter = head_size // 4
    inverse = 1.0 / 10000.0 ** (jnp.arange(quarter, dtype=jnp.float32) * 2.0 / (head_size // 2))
    angles = jnp.concatenate(
        [
            patch_row.astype(jnp.float32)[:, None] * inverse,
            patch_col.astype(jnp.float32)[:, None] * inverse,
        ],
        axis=1,
    )
    angles = jnp.concatenate([angles, angles], axis=1)
    return (jnp.cos(angles), jnp.sin(angles))


def mm(left, right):
    return lax.dot_general(left, right, (((1,), (0,)), ((), ())), preferred_element_type=F32)


def mm_nt(left, right):
    return lax.dot_general(left, right, (((1,), (1,)), ((), ())), preferred_element_type=F32)


def call(body, name, grid, in_specs, out_specs, out_shape, scratch=(), flops=0, moved=0):
    return pl.pallas_call(
        body,
        name=name,
        grid=grid,
        in_specs=in_specs,
        out_specs=out_specs,
        out_shape=out_shape,
        scratch_shapes=scratch,
        cost_estimate=pl.CostEstimate(flops=flops, transcendentals=0, bytes_accessed=moved),
        compiler_params=pltpu.CompilerParams(
            dimension_semantics=("arbitrary",) * len(grid), vmem_limit_bytes=56 * 1024 * 1024
        ),
    )


def whole(shape):
    return pl.BlockSpec(shape, lambda *_: (0,) * len(shape))


def pick(adapter_ref, count):
    lanes = lax.broadcasted_iota(jnp.int32, (count, 128), 1) // RANK
    return (lanes == adapter_ref[...]).astype(F32)


def turn(values, low):
    size = values.shape[1]
    left = pltpu.roll(values, size - HD // 2, 1)
    right = pltpu.roll(values, HD // 2, 1)
    return jnp.where(low, left, right)


def qkv_body(x_ref, w_ref, a_ref, bt_ref, bias_ref, ad_ref, cos_ref, sin_ref, out_ref, inner_ref):
    part = pl.program_id(0)
    rows = x_ref.shape[0]
    step = 256

    @pl.when(part == 0)
    def _():
        inner_ref[...] = (mm(x_ref[...], a_ref[...]) * pick(ad_ref, rows)).astype(BF)

    def one(start, rotated):
        sl = pl.ds(start, step)
        y = mm(x_ref[sl, :], w_ref[...]) + mm_nt(inner_ref[sl, :], bt_ref[...]) + bias_ref[...]
        if rotated:
            low = lax.broadcasted_iota(jnp.int32, (step, 640), 1) % HD < HD // 2
            for begin in (0, 640):
                piece = y[:, begin : begin + 640]
                done = piece * cos_ref[sl, :] + turn(piece, low) * sin_ref[sl, :]
                out_ref[sl, begin : begin + 640] = done.astype(BF)
        else:
            out_ref[sl, :] = y.astype(BF)

    @pl.when(part < 2)
    def _():
        for i in range(0, rows, step):
            one(i, True)

    @pl.when(part == 2)
    def _():
        for i in range(0, rows, step):
            one(i, False)


def qkv_call(x, pack, bt, bias, adapter, cos_t, sin_t):
    n, d = x.shape
    return call(
        qkv_body,
        "qkv_rotary",
        (3,),
        [
            whole((n, d)),
            pl.BlockSpec((d, d), lambda j: (0, j)),
            pl.BlockSpec((d, 128), lambda j: (0, 3 * d // 128)),
            pl.BlockSpec((d, 128), lambda j: (j, 0)),
            pl.BlockSpec((1, d), lambda j: (0, j)),
            whole((n, 1)),
            whole((n, 640)),
            whole((n, 640)),
        ],
        [pl.BlockSpec((n, d), lambda j: (0, j)), whole((n, 128))],
        [jax.ShapeDtypeStruct((n, 3 * d), BF), jax.ShapeDtypeStruct((n, 128), BF)],
        flops=2 * n * d * 3 * d,
        moved=8 * d * d + 12 * n * d,
    )(x, pack, pack, bt, bias, adapter, cos_t, sin_t)


def attend_body(q_ref, k_ref, v_ref, qm_ref, km_ref, out_ref, lse_ref):
    rows = q_ref.shape[0]
    step = 256
    factor = LOG2E / math.sqrt(HD)
    lanes = lax.broadcasted_iota(jnp.int32, (step, 128), 1)
    for i in range(0, rows, step):
        lse_ref[i : i + step, :] = jnp.zeros((step, 128), F32)
    for h in range(8):
        cols = slice(HD * h, HD * h + HD)
        keys = jnp.concatenate([k_ref[:, cols], km_ref[...]], axis=1)
        vals = v_ref[:, cols]
        for i in range(0, rows, step):
            query = jnp.concatenate([q_ref[i : i + step, cols], qm_ref[i : i + step, :]], axis=1)
            s = mm_nt(query, keys)
            top = jnp.max(s, axis=1, keepdims=True)
            e = jnp.exp2((s - top) * factor)
            total = jnp.sum(e, axis=1, keepdims=True)
            o = mm(e.astype(BF), vals) * (1.0 / total)
            out_ref[i : i + step, cols] = o.astype(BF)
            lse = top + jnp.log(total) * math.sqrt(HD)
            lse_ref[i : i + step, :] = jnp.where(lanes == h, lse, lse_ref[i : i + step, :])


def attend_call(qkv, qm, km):
    n = qkv.shape[0]
    d = qkv.shape[1] // 3
    groups = d // 640
    return call(
        attend_body,
        "attend",
        (groups,),
        [
            pl.BlockSpec((n, 640), lambda g: (0, g)),
            pl.BlockSpec((n, 640), lambda g: (0, groups + g)),
            pl.BlockSpec((n, 640), lambda g: (0, 2 * groups + g)),
            whole((n, 48)),
            whole((n, 48)),
        ],
        [pl.BlockSpec((n, 640), lambda g: (0, g)), pl.BlockSpec((n, 128), lambda g: (0, g))],
        [jax.ShapeDtypeStruct((n, d), BF), jax.ShapeDtypeStruct((n, 128 * groups), F32)],
        flops=4 * n * n * d,
        moved=8 * n * d,
    )(qkv, qkv, qkv, qm, km)


def split_low(values, count):
    parts = []
    for _ in range(count):
        part = values.astype(BF)
        parts.append(part)
        values = values - part.astype(F32)
    return parts


def attend_back_body(
    q_ref, k_ref, v_ref, g_ref, o_ref, lse_ref, qm_ref, km_ref, cos_ref, sin_ref,
    dq_ref, dk_ref, dv_ref, dq_s, dk_s,
):
    rows = q_ref.shape[0]
    step = 256
    factor = LOG2E / math.sqrt(HD)
    scale = 1.0 / math.sqrt(HD)
    lanes = lax.broadcasted_iota(jnp.int32, (rows, 48), 1)
    ones_two = jnp.where((lanes == 16) | (lanes == 17), 1.0, 0.0).astype(BF)
    for h in range(8):
        cols = slice(HD * h, HD * h + HD)
        gh = g_ref[:, cols]
        delta = jnp.sum(gh.astype(F32) * o_ref[:, cols].astype(F32), axis=1, keepdims=True)
        d_hi, d_lo = split_low(-delta, 2)
        l_hi, l_mid, l_lo = split_low(-lse_ref[:, h : h + 1], 3)
        q_aug = jnp.where(
            lanes == 16,
            l_hi.astype(F32),
            jnp.where(
                lanes == 17,
                l_mid.astype(F32),
                jnp.where(lanes == 18, l_lo.astype(F32), qm_ref[...].astype(F32)),
            ),
        ).astype(BF)
        g_aug = jnp.where(
            lanes == 16, d_hi.astype(F32), jnp.where(lanes == 17, d_lo.astype(F32), 0.0)
        ).astype(BF)
        query = jnp.concatenate([q_ref[:, cols], q_aug], axis=1)
        grads = jnp.concatenate([gh, g_aug], axis=1)
        keys = jnp.concatenate([k_ref[:, cols], km_ref[...]], axis=1)
        vals = jnp.concatenate([v_ref[:, cols], ones_two], axis=1)
        keys_t = keys.T
        dk = jnp.zeros((rows, 128), F32)
        dv = jnp.zeros((rows, 128), F32)
        for i in range(0, rows, step):
            qb = query[i : i + step, :]
            gb = grads[i : i + step, :]
            p = jnp.exp2(mm_nt(keys, qb) * factor)
            dp = mm_nt(vals, gb)
            ds = (p * dp).astype(BF)
            dv = dv + mm(p.astype(BF), gb)
            dk = dk + mm(ds, qb)
            dq = mm(keys_t, ds)
            dq_s[i : i + step, cols] = dq.T[:, :HD]
        dk_s[:, cols] = dk[:, :HD]
        dv_ref[:, cols] = dv[:, :HD].astype(BF)
    low = lax.broadcasted_iota(jnp.int32, (step, 640), 1) % HD < HD // 2
    for i in range(0, rows, step):
        sl = slice(i, i + step)
        for src, dst in ((dq_s, dq_ref), (dk_s, dk_ref)):
            piece = src[sl, :] * scale
            dst[sl, :] = (piece * cos_ref[sl, :] - turn(piece, low) * sin_ref[sl, :]).astype(BF)


def attend_back_call(qkv, grads, attended, lse, qm, km, cos_t, sin_t):
    n = qkv.shape[0]
    d = qkv.shape[1] // 3
    groups = d // 640
    block = pl.BlockSpec((n, 640), lambda g: (0, g))
    return call(
        attend_back_body,
        "attend_back",
        (groups,),
        [
            block,
            pl.BlockSpec((n, 640), lambda g: (0, groups + g)),
            pl.BlockSpec((n, 640), lambda g: (0, 2 * groups + g)),
            block,
            block,
            pl.BlockSpec((n, 128), lambda g: (0, g)),
            whole((n, 48)),
            whole((n, 48)),
            whole((n, 640)),
            whole((n, 640)),
        ],
        [block, block, block],
        [jax.ShapeDtypeStruct((n, d), BF)] * 3,
        [pltpu.VMEM((n, 640), F32), pltpu.VMEM((n, 640), F32)],
        flops=10 * n * n * d,
        moved=16 * n * d,
    )(qkv, qkv, qkv, grads, attended, lse, qm, km, cos_t, sin_t)


def tables(picture, patch_row, patch_col):
    cosine, sine = rotary_tables(patch_row, patch_col, HD)
    half = HD // 2
    signed = jnp.concatenate([-sine[:, :half], sine[:, half:]], axis=1)
    count = picture.shape[0]
    change = (picture[1:] != picture[:-1]).astype(jnp.int32)
    places = lax.broadcasted_iota(jnp.int32, (count, count - 1), 0)
    before = lax.broadcasted_iota(jnp.int32, (count, count - 1), 1) < places
    index = jnp.sum(jnp.where(before, change[None, :], 0), axis=1)
    lanes = lax.broadcasted_iota(jnp.int32, (1, 48), 1)
    own = lanes == index[:, None]
    qm = jnp.where(own | (lanes >= 16), 0.0, -BIG).astype(BF)
    km = (own | ((lanes >= 16) & (lanes < 19))).astype(BF)
    return (*widen_call(cosine, signed), qm, km)


def stats(values):
    centre = jnp.mean(values, axis=-1, keepdims=True)
    centred = values - centre
    spread = lax.rsqrt(jnp.mean(centred * centred, axis=-1, keepdims=True) + EPS)
    return centred * spread, spread


def once(shape, index):
    return pl.BlockSpec(shape, index, pipeline_mode=pl.Buffered(1))


def proj_body(
    att_ref, w_ref, a_ref, bt_ref, bias_ref, ad_ref, tok_ref, gain_ref, shift_ref,
    mid_ref, norm_ref, inner_ref,
):
    sub = 256
    held = []
    for begin in range(0, att_ref.shape[0], sub):
        sl = pl.ds(begin, sub)
        x = att_ref[sl, :]
        inner = (mm(x, a_ref[...]) * pick(ad_ref.at[sl, :], sub)).astype(BF)
        inner_ref[sl, :] = inner
        held.append((sl, mm(x, w_ref[...]) + bias_ref[...] + mm_nt(inner, bt_ref[...])))
    for sl, branch in held:
        middle = tok_ref[sl, :].astype(F32) + branch
        mid_ref[sl, :] = middle
        unit, _ = stats(middle)
        norm_ref[sl, :] = (unit * gain_ref[...] + shift_ref[...]).astype(BF)


def proj_call(att, pack, first_col, a_col, bt_col, bias, adapter, tokens, gain, shift):
    n, d = att.shape
    step = 512
    row = pl.BlockSpec((step, d), lambda i: (i, 0))
    return call(
        proj_body,
        "proj_norm",
        (n // step,),
        [
            row,
            once((d, d), lambda i: (0, first_col // d)),
            once((d, 128), lambda i: (0, a_col // 128)),
            once((d, 128), lambda i: (0, bt_col // 128)),
            whole((1, d)),
            pl.BlockSpec((step, 1), lambda i: (i, 0)),
            row,
            whole((1, d)),
            whole((1, d)),
        ],
        [row, row, pl.BlockSpec((step, 128), lambda i: (i, 0))],
        [
            jax.ShapeDtypeStruct((n, d), F32),
            jax.ShapeDtypeStruct((n, d), BF),
            jax.ShapeDtypeStruct((n, 128), BF),
        ],
        flops=2 * n * d * d,
        moved=2 * d * d + 10 * n * d,
    )(att, pack, pack, pack, bias, adapter, tokens, gain, shift)


def feed_body(*refs, parts, first, last):
    refs = list(refs)
    take = lambda count: [refs.pop(0) for _ in range(count)]
    x_ref, g_ref = take(2)
    w1, w2, bt1, a2, b1 = take(parts), take(parts), take(parts), take(parts), take(parts)
    ad_ref, a1_ref, bt2_ref = take(3)
    if first:
        base_ref, b2_ref = take(2)
    else:
        base_ref, gx_in, in1_ref, ig2_ref, in2_in, ig1_in = take(6)
        val_ref = take(1)[0]
    if first:
        acc_ref, gx_ref, in1_out, ig2_out, in2_out, ig1_out = take(6)
    if last:
        out_ref, gx_ref, ta1_ref, tb2_ref = take(4)
    ta2, tb1 = take(parts), take(parts)
    if last:
        ta1_s, tb2_s = take(2)
    ta2_s, tb1_s = take(parts), take(parts)
    sums = ta2_s + tb1_s + ([ta1_s, tb2_s] if last else [])
    i = pl.program_id(0)
    end = i == pl.num_programs(0) - 1

    @pl.when(i == 0)
    def _():
        for ref in sums:
            ref[...] = jnp.zeros_like(ref)

    sub = 256
    jobs = []
    for begin in range(0, x_ref.shape[0], sub):
        sl = pl.ds(begin, sub)
        x = x_ref[sl, :]
        g = g_ref[sl, :]
        sel = pick(ad_ref.at[sl, :], sub)
        if first:
            in1 = (mm(x, a1_ref[...]) * sel).astype(BF)
            ig2 = (mm(g, bt2_ref[...]) * sel).astype(BF)
            in1_out[sl, :] = in1
            ig2_out[sl, :] = ig2
            acc = base_ref[sl, :] + b2_ref[...]
            gx = in2 = ig1 = None
        else:
            in1 = in1_ref[sl, :]
            ig2 = ig2_ref[sl, :]
            acc, gx, in2, ig1 = base_ref[sl, :], gx_in[sl, :], in2_in[sl, :], ig1_in[sl, :]
        hs = [mm(x, w1[q][...]) + mm_nt(in1, bt1[q][...]) + b1[q][...] for q in range(parts)]
        gas = [mm_nt(g, w2[q][...]) + mm_nt(ig2, a2[q][...]) for q in range(parts)]
        jobs.append((sl, x, g, sel, in1, ig2, acc, gx, in2, ig1, hs, gas))
    lows = []
    for job in jobs:
        pairs = []
        for h, ga in zip(*job[-2:]):
            s = 0.5 * jnp.tanh(0.851 * h) + 0.5
            pairs.append(((h * s).astype(BF), (ga * (s + 1.702 * h * s * (1.0 - s))).astype(BF)))
        lows.append(pairs)
    for job, pairs in zip(jobs, lows):
        sl, x, g, sel, in1, ig2, acc, gx, in2, ig1, _, _ = job
        in1_t = in1.T
        ig2_t = ig2.T
        for q, (act, gh) in enumerate(pairs):
            more = (mm_nt(gh, w1[q][...]), mm(act, a2[q][...]), mm(gh, bt1[q][...]))
            acc = acc + mm(act, w2[q][...])
            gx, in2, ig1 = more if gx is None else (gx + more[0], in2 + more[1], ig1 + more[2])
            ta2_s[q][...] += mm(ig2_t, act)
            tb1_s[q][...] += mm(in1_t, gh)
        if last:
            low2 = (in2 * sel).astype(BF)
            low1 = (ig1 * sel).astype(BF)
            out_ref[sl, :] = ((acc + mm_nt(low2, bt2_ref[...])) * val_ref[sl, :]).astype(BF)
            gx_ref[sl, :] = gx + mm_nt(low1, a1_ref[...])
            ta1_s[...] += mm(low1.T, x)
            tb2_s[...] += mm(low2.T, g)
        else:
            acc_ref[sl, :] = acc
            gx_ref[sl, :] = gx
            in2_out[sl, :] = in2
            ig1_out[sl, :] = ig1

    @pl.when(end)
    def _():
        for q in range(parts):
            ta2[q][...] = ta2_s[q][...].T.astype(BF)
            tb1[q][...] = tb1_s[q][...].T.astype(BF)
        if last:
            ta1_ref[...] = ta1_s[...].T.astype(BF)
            tb2_ref[...] = tb2_s[...].T.astype(BF)


def feed_call(x, grads, w2, w1, bt1, a2, b1, adapter, a1, bt2, state, first, last):
    n, d = x.shape
    parts = len(w1)
    step = 512 if parts < 3 else 256
    row = pl.BlockSpec((step, d), lambda i: (i, 0))
    thin_row = pl.BlockSpec((step, 128), lambda i: (i, 0))
    one = pl.BlockSpec((step, 1), lambda i: (i, 0))
    thin = once((d, 128), lambda i: (0, 0))
    line = once((1, d), lambda i: (0, 0))

    def wide(col):
        return once((d, d), lambda i: (0, col // d))

    def narrow(col):
        return once((d, 128), lambda i: (0, col // 128))

    in_specs = [row, row] + [wide(c) for _, c in w1] + [wide(c) for _, c in w2]
    in_specs += [narrow(c) for _, c in bt1] + [narrow(c) for _, c in a2] + [line] * parts
    in_specs += [one, narrow(a1[1]), narrow(bt2[1])]
    args = [x, grads] + [v for v, _ in w1 + w2 + bt1 + a2] + list(b1) + [adapter, a1[0], bt2[0]]
    if first:
        in_specs += [row, line]
    else:
        in_specs += [row, row, thin_row, thin_row, thin_row, thin_row, one]
    args += list(state)
    out_specs, out_shape, scratch = [], [], []
    if first:
        out_specs += [row, row, thin_row, thin_row, thin_row, thin_row]
        out_shape += [jax.ShapeDtypeStruct((n, d), F32)] * 2
        out_shape += [jax.ShapeDtypeStruct((n, 128), BF)] * 2 + [jax.ShapeDtypeStruct((n, 128), F32)] * 2
    if last:
        out_specs += [row, row, thin, thin]
        out_shape += [jax.ShapeDtypeStruct((n, d), BF), jax.ShapeDtypeStruct((n, d), F32)]
        out_shape += [jax.ShapeDtypeStruct((d, 128), BF)] * 2
        scratch += [pltpu.VMEM((128, d), F32)] * 2
    out_specs += [thin] * (2 * parts)
    out_shape += [jax.ShapeDtypeStruct((d, 128), BF)] * (2 * parts)
    scratch += [pltpu.VMEM((128, d), F32)] * (2 * parts)
    return call(
        functools.partial(feed_body, parts=parts, first=first, last=last),
        "feed_first" if first else "feed_last",
        (n // step,),
        in_specs,
        out_specs,
        out_shape,
        scratch,
        flops=8 * n * d * d * parts,
        moved=4 * d * d * parts + 24 * n * d,
    )(*args)


def proj_back_body(
    gx_ref, mid_ref, cot_ref, val_ref, gain_ref, w_ref, a_ref, bt_ref, ad_ref, att_ref, inner_ref,
    gm_ref, ga_ref, ta_ref, tb_ref, ta_s, tb_s,
):
    i = pl.program_id(0)
    sub = 256

    @pl.when(i == 0)
    def _():
        ta_s[...] = jnp.zeros_like(ta_s)
        tb_s[...] = jnp.zeros_like(tb_s)

    for begin in range(0, gx_ref.shape[0], sub):
        sl = pl.ds(begin, sub)
        unit, spread = stats(mid_ref[sl, :])
        gm = cot_ref[sl, :].astype(F32) * val_ref[sl, :]
        gm = gm + normalize_back(gx_ref[sl, :], unit, spread, gain_ref[...])
        gm_ref[sl, :] = gm
        gb = gm.astype(BF)
        ig = (mm(gb, bt_ref[...]) * pick(ad_ref.at[sl, :], sub)).astype(BF)
        ga_ref[sl, :] = (mm_nt(gb, w_ref[...]) + mm_nt(ig, a_ref[...])).astype(BF)
        ta_s[...] += mm(ig.T, att_ref[sl, :])
        tb_s[...] += mm(inner_ref[sl, :].T, gb)

    @pl.when(i == pl.num_programs(0) - 1)
    def _():
        ta_ref[...] = ta_s[...].T.astype(BF)
        tb_ref[...] = tb_s[...].T.astype(BF)


def proj_back_call(gx, middle, cot, valid, gain, pack, first_col, a_col, bt_col, adapter, att, inner):
    n, d = gx.shape
    step = 256
    row = pl.BlockSpec((step, d), lambda i: (i, 0))
    one = pl.BlockSpec((step, 1), lambda i: (i, 0))
    thin = once((d, 128), lambda i: (0, 0))
    return call(
        proj_back_body,
        "proj_back",
        (n // step,),
        [
            row,
            row,
            row,
            one,
            whole((1, d)),
            once((d, d), lambda i: (0, first_col // d)),
            once((d, 128), lambda i: (0, a_col // 128)),
            once((d, 128), lambda i: (0, bt_col // 128)),
            one,
            row,
            pl.BlockSpec((step, 128), lambda i: (i, 0)),
        ],
        [row, row, thin, thin],
        [
            jax.ShapeDtypeStruct((n, d), F32),
            jax.ShapeDtypeStruct((n, d), BF),
            jax.ShapeDtypeStruct((d, 128), BF),
            jax.ShapeDtypeStruct((d, 128), BF),
        ],
        [pltpu.VMEM((128, d), F32), pltpu.VMEM((128, d), F32)],
        flops=2 * n * d * d,
        moved=2 * d * d + 18 * n * d,
    )(gx, middle, cot, valid, gain, pack, pack, pack, adapter, att, inner)


def qkv_terms_body(gq_ref, gk_ref, gv_ref, x_ref, bt_ref, inner_ref, ad_ref, ig_ref, ta_ref, tb_ref, ta_s, tb_s):
    i = pl.program_id(0)
    rows, d = x_ref.shape

    @pl.when(i == 0)
    def _():
        ta_s[...] = jnp.zeros_like(ta_s)
        tb_s[...] = jnp.zeros_like(tb_s)

    inner_t = inner_ref[...].T
    total = None
    for part, ref in enumerate((gq_ref, gk_ref, gv_ref)):
        g = ref[...]
        sl = slice(part * d, part * d + d)
        piece = mm(g, bt_ref[sl, :])
        total = piece if total is None else total + piece
        tb_s[:, sl] += mm(inner_t, g)
    ig = (total * pick(ad_ref, rows)).astype(BF)
    ig_ref[...] = ig
    ta_s[...] += mm(ig.T, x_ref[...])

    @pl.when(i == pl.num_programs(0) - 1)
    def _():
        ta_ref[...] = ta_s[...].T.astype(BF)
        tb_ref[...] = tb_s[...].T.astype(BF)


def qkv_terms_call(gq, gk, gv, x, bt, inner, adapter):
    n, d = x.shape
    step = 256
    row = pl.BlockSpec((step, d), lambda i: (i, 0))
    thin_row = pl.BlockSpec((step, 128), lambda i: (i, 0))
    return call(
        qkv_terms_body,
        "qkv_terms",
        (n // step,),
        [row, row, row, row, whole(bt.shape), thin_row, pl.BlockSpec((step, 1), lambda i: (i, 0))],
        [thin_row, whole((d, 128)), whole((3 * d, 128))],
        [
            jax.ShapeDtypeStruct((n, 128), BF),
            jax.ShapeDtypeStruct((d, 128), BF),
            jax.ShapeDtypeStruct((3 * d, 128), BF),
        ],
        [pltpu.VMEM((128, d), F32), pltpu.VMEM((128, 3 * d), F32)],
        flops=4 * n * d * 128 * 4,
        moved=10 * n * d,
    )(gq, gk, gv, x, bt, inner, adapter)


def qkv_back_body(gq_ref, gk_ref, gv_ref, w_ref, ig_ref, a_ref, tok_ref, gain_ref, gm_ref, out_ref, acc_ref):
    part = pl.program_id(0)
    sub = 256
    pieces = [pl.ds(begin, sub) for begin in range(0, tok_ref.shape[0], sub)]

    @pl.when(part == 0)
    def _():
        for sl in pieces:
            acc_ref[sl, :] = mm_nt(gq_ref[sl, :], w_ref[...]) + mm_nt(ig_ref[sl, :], a_ref[...])

    @pl.when(part == 1)
    def _():
        for sl in pieces:
            acc_ref[sl, :] += mm_nt(gk_ref[sl, :], w_ref[...])

    @pl.when(part == 2)
    def _():
        for sl in pieces:
            grad = acc_ref[sl, :] + mm_nt(gv_ref[sl, :], w_ref[...])
            unit, spread = stats(tok_ref[sl, :].astype(F32))
            out_ref[sl, :] = gm_ref[sl, :] + normalize_back(grad, unit, spread, gain_ref[...])


def qkv_back_call(gq, gk, gv, pack, ig, tokens, gain, gm, half):
    n, d = tokens.shape
    rows = n // 2
    row = pl.BlockSpec((rows, d), lambda p: (half, 0))
    return pl.pallas_call(
        qkv_back_body,
        name="qkv_back",
        grid=(3,),
        in_specs=[
            row,
            row,
            row,
            pl.BlockSpec((d, d), lambda p: (0, p)),
            pl.BlockSpec((rows, 128), lambda p: (half, 0)),
            once((d, 128), lambda p: (0, 3 * d // 128)),
            row,
            whole((1, d)),
            row,
        ],
        out_specs=row,
        out_shape=jax.ShapeDtypeStruct((n, d), F32),
        scratch_shapes=[pltpu.VMEM((rows, d), F32)],
        input_output_aliases={8: 0},
        cost_estimate=pl.CostEstimate(flops=3 * n * d * d, transcendentals=0, bytes_accessed=6 * d * d + 9 * n * d),
        compiler_params=pltpu.CompilerParams(
            dimension_semantics=("arbitrary",), vmem_limit_bytes=56 * 1024 * 1024
        ),
    )(gq, gk, gv, pack, ig, pack, tokens, gain, gm)


def unfold_rows(block, devices):
    rows = block.shape[0] // devices
    pieces = block.shape[1] // 128
    split = block.reshape(devices, rows, pieces, 128)
    return split.transpose(0, 2, 1, 3).reshape(-1, 128)


def gather_rows(packed):
    return lax.all_gather(packed, ("dp", "fsdp"), axis=0, tiled=True)


def place_body(table_ref, *refs, pieces):
    out_ref = refs[-1]
    mask = table_ref[2]
    begin = 0
    for ref in refs[:pieces]:
        end = begin + ref.shape[-1]
        for k in range(ref.shape[1]):
            out_ref[mask ^ k, 0, 0, :, begin:end] = ref[0, k]
        begin = end


class Gather:
    def __init__(self, *parts):
        self.zs, self.fs = lax.axis_size("dp") // 2, lax.axis_size("fsdp")
        self.rows, self.cols = parts[0].shape[0], sum(p.shape[1] for p in parts)
        self.parts = list(parts)
        self.phase = 0

    def swap(self, value, axis, mask):
        return lax.ppermute(value, axis, [(i, i ^ mask) for i in range(lax.axis_size(axis))])

    def start(self):
        z_masks, f_masks = list(range(2, 2 * self.zs, 2)), list(range(1, self.fs))
        orders = [[("dp", z_masks), ("fsdp", f_masks)], [("fsdp", f_masks), ("dp", z_masks)]]
        self.got = []
        for part, order in zip(self.parts, orders):
            axis, masks = order[self.phase] if self.phase < 2 else ("dp", [1])
            self.got.append([part] + [self.swap(part, axis, m) for m in masks])

    def finish(self, *others):
        sizes = [len(group) for group in self.got]
        held = lax.optimization_barrier(tuple(v for group in self.got for v in group) + others)
        groups, at = [], 0
        for size in sizes:
            groups.append(held[at : at + size])
            at += size
        if self.phase == 0:
            self.parts = [jnp.stack(group) for group in groups]
        elif self.phase == 1:
            self.parts = [jnp.stack(group, axis=1 if i else 0) for i, group in enumerate(groups)]
        if self.phase < 2:
            held = lax.optimization_barrier(tuple(self.parts) + tuple(held[at:]))
            self.parts = list(held[: len(sizes)])
            at = len(sizes)
        else:
            self.far = [group[1] for group in groups[::-1]]
        self.phase += 1
        return held[at:]

    def place(self, side, earlier):
        zs, fs, rows, cols = self.zs, self.fs, self.rows, self.cols
        spot, column = lax.axis_index("dp"), lax.axis_index("fsdp")
        table = jnp.stack([(spot & 1) ^ side, column, spot >> 1]).astype(jnp.int32)
        parts = self.far if side else self.parts[::-1]
        specs = [pl.BlockSpec((1, zs, rows, p.shape[-1]), lambda m, t: (m, 0, 0, 0)) for p in parts]
        specs += [pl.BlockSpec(memory_space=pl.ANY)] * len(earlier)
        return pl.pallas_call(
            functools.partial(place_body, pieces=len(parts)),
            name="place_blocks",
            grid_spec=pltpu.PrefetchScalarGridSpec(
                num_scalar_prefetch=1,
                grid=(fs,),
                in_specs=specs,
                out_specs=pl.BlockSpec((zs, 1, 1, rows, cols), lambda m, t: (0, t[0], t[1] ^ m, 0, 0)),
            ),
            out_shape=jax.ShapeDtypeStruct((zs, 2, fs, rows, cols), BF),
            input_output_aliases={1 + len(parts): 0} if earlier else {},
            cost_estimate=pl.CostEstimate(flops=0, transcendentals=0, bytes_accessed=4 * zs * fs * rows * cols),
            compiler_params=pltpu.CompilerParams(vmem_limit_bytes=48 * 1024 * 1024),
        )(table, *parts, *earlier)


def widen_body(cos_ref, sin_ref, cos_out, sin_out):
    for src, dst in ((cos_ref, cos_out), (sin_ref, sin_out)):
        value = src[...]
        dst[...] = jnp.concatenate([value] * 8, axis=1)


def widen_call(cosine, signed):
    n = cosine.shape[0]
    out = jax.ShapeDtypeStruct((n, 8 * HD), F32)
    specs = [whole((n, 8 * HD))] * 2
    return call(widen_body, "widen_tables", (1,), [whole(cosine.shape)] * 2, specs, [out, out], moved=72 * n * HD)(
        cosine, signed
    )


def pack_body(
    qkv_w, proj_w, fc1_w, fc2_w, qkv_a, proj_a, fc1_a, fc2_a, qkv_b, proj_b, fc1_b, fc2_b, *outs, devices, cut, groups
):
    rows, d = proj_w.shape
    quarters = fc1_w.shape[1] // d

    def turned(ref):
        flipped = ref[...].astype(F32)
        return [flipped[i * rows : (i + 1) * rows].astype(BF) for i in range(flipped.shape[0] // rows)]

    def fill(out, pieces):
        at = 0
        for piece in pieces:
            out[:, at : at + piece.shape[1]] = piece
            at += piece.shape[1]

    fill(outs[1], [qkv_w[:, :cut]])
    fill(outs[0], [qkv_w[:, cut:], qkv_a[...]] + turned(qkv_b))
    up1 = turned(fc1_b)
    for out, group in zip(outs[2:], groups):
        pieces = [fc2_w[q * rows : (q + 1) * rows, :] for q in group]
        for q in group:
            starts = [(i * quarters + q) * rows for i in range(devices)]
            pieces.append(jnp.concatenate([fc1_w[:, c : c + rows] for c in starts], axis=1))
        if group[0] == 0:
            pieces.append(proj_w[...])
        pieces += [up1[q] for q in group]
        pieces += [fc2_a[q * rows : (q + 1) * rows, :] for q in group]
        if group[0] == 0:
            pieces += [fc1_a[...], proj_a[...]] + turned(proj_b) + turned(fc2_b)
        fill(out, pieces)


def pack_call(arrays, devices, groups):
    rows, d = arrays[1].shape
    total = arrays[0].shape[1] + 4 * 128
    cut = total // 128 // 3 * 128
    widths = [total - cut, cut] + [len(g) * (2 * d + 256) + (d + 512 if g[0] == 0 else 0) for g in groups]
    return call(
        functools.partial(pack_body, devices=devices, cut=cut, groups=groups),
        "pack_shards",
        (1,),
        [whole(v.shape) for v in arrays],
        [whole((rows, w)) for w in widths],
        [jax.ShapeDtypeStruct((rows, w), BF) for w in widths],
        moved=4 * rows * sum(widths),
    )(*arrays)


class Scatter:
    def __init__(self, terms):
        zs, fs = lax.axis_size("dp") // 2, lax.axis_size("fsdp")
        self.values = [t.reshape(zs, 2, fs, -1, 128) for t in terms]
        self.phases = [("dp", 1, [1]), ("fsdp", 1, list(range(1, fs))), ("dp", 0, list(range(2, 2 * zs, 2)))]
        self.open = None

    def start(self):
        axis, dim, masks = self.phases.pop(0)
        size = lax.axis_size(axis)
        place = lax.axis_index(axis)
        shift = 0
        if axis == "dp":
            place, shift = (place & 1, 0) if dim else (place >> 1, 1)

        def pick_one(at):
            found = [lax.dynamic_index_in_dim(v, at, dim, keepdims=False) for v in self.values]
            return found[0] if len(found) == 1 else jnp.concatenate(found, axis=-2)

        sends = [pick_one(place ^ (mask >> shift)).astype(BF) for mask in masks]
        got = [lax.ppermute(v, axis, [(i, i ^ mask) for i in range(size)]) for v, mask in zip(sends, masks)]
        self.open = (lambda: pick_one(place), got)

    def finish(self, *others):
        mine, got = self.open
        held = lax.optimization_barrier(tuple(got) + others)
        total = mine().astype(F32)
        for piece in held[: len(got)]:
            total = total + piece.astype(F32)
        self.values = [total]
        return held[len(got) :]


def local(
    tokens,
    cotangent,
    picture,
    adapter,
    patch_row,
    patch_col,
    qkv_weight,
    qkv_bias,
    proj_weight,
    proj_bias,
    fc1_weight,
    fc1_bias,
    fc2_weight,
    fc2_bias,
    norm1_gain,
    norm1_bias,
    norm2_gain,
    norm2_bias,
    qkv_down,
    qkv_up,
    proj_down,
    proj_up,
    fc1_down,
    fc1_up,
    fc2_down,
    fc2_up,
):
    devices = lax.axis_size(("dp", "fsdp"))
    rows, d = proj_weight.shape
    quarters = fc1_weight.shape[1] // d
    q_cols = qkv_weight.shape[1]
    groups = [list(range(quarters - 1)), [quarters - 1]]
    shards = (qkv_weight, proj_weight, fc1_weight, fc2_weight, qkv_down, proj_down, fc1_down, fc2_down)
    shards += (qkv_up.T, proj_up.T, fc1_up.T, fc2_up.T)
    part_b, part_a, pack_a, pack_b = pack_call(shards, devices, groups)
    one = Gather(part_b, part_a)
    one.start()

    def spots(source, count, extra):
        wide = [(source, q * d) for q in range(2 * count)]
        base = (2 * count + extra) * d
        thin = [(source, base + q * 128) for q in range(2 * count)]
        return [wide[:count], wide[count:], thin[:count], thin[count:]]

    count = len(groups[0])
    row_count = tokens.shape[0]
    unit_one, _ = stats(tokens.astype(F32))
    normed = (unit_one * norm1_gain + norm1_bias).astype(BF)
    (normed,) = one.finish(normed)
    second = gather_rows(pack_a)
    third = gather_rows(pack_b)
    proj_col = 2 * count * d
    a1_col = proj_col + d + 2 * count * 128
    ap_col, btp_col, bt2_col = a1_col + 128, a1_col + 256, a1_col + 384
    one.start()
    ad = adapter[:, None]
    valid = (picture >= 0).astype(F32)[:, None]
    grad_low = (cotangent.astype(F32) * valid).astype(BF)
    bias1 = fc1_bias.reshape(devices, quarters, rows).transpose(1, 0, 2).reshape(quarters, 1, d)
    small = [qkv_bias[None], proj_bias[None], norm1_gain[None], norm2_gain[None], norm2_bias[None], fc2_bias[None]]
    small += [bias1[q] for q in range(quarters)] + [ad, valid, grad_low, *tables(picture, patch_row, patch_col)]
    small = one.finish(*small)
    bias_qkv, bias_proj, gain1, gain2, shift2, bias2, *bias1 = small[: 6 + quarters]
    ad, valid, grad_low, cos_t, sin_t, qm, km = small[6 + quarters :]
    one.start()
    first = one.place(0, ())
    (first,) = one.finish(first)
    first = one.place(1, (first,)).reshape(devices * rows, -1)
    bt_qkv = unfold_rows(first[:, q_cols + 128 :], devices)
    qkv, inner_qkv = qkv_call(normed, first, bt_qkv, bias_qkv, ad, cos_t, sin_t)
    attended, lse = attend_call(qkv, qm, km)
    middle, normed_two, inner_proj = proj_call(
        attended, second, proj_col, ap_col, btp_col, bias_proj, ad, tokens, gain2, shift2
    )
    a1, bt2 = (second, a1_col), (second, bt2_col)
    early = spots(second, count, 1)
    final = spots(third, quarters - count, 0)
    acc, grad_x, in1, ig2, in2, ig1, *terms_a = feed_call(
        normed_two, grad_low, *early, bias1[:count], ad, a1, bt2, (middle, bias2), True, False
    )
    na, nb = count, quarters - count
    state = (acc, grad_x, in1, ig2, in2, ig1, valid)
    block_out, grad_two, ta_fc1, tb_fc2, *terms_b = feed_call(
        normed_two, grad_low, *final, bias1[count:], ad, a1, bt2, state, False, True
    )

    feed_sum = Scatter([ta_fc1, *terms_a[na:], *terms_b[nb:], *terms_a[:na], *terms_b[:nb], tb_fc2])
    feed_sum.start()
    grad_middle, grad_att, ta_proj, tb_proj = proj_back_call(
        grad_two, middle, cotangent, valid, gain2, second, proj_col, ap_col, btp_col, ad, attended, inner_proj
    )
    (grad_att,) = feed_sum.finish(grad_att)
    feed_sum.start()
    grads = attend_back_call(qkv, grad_att, attended, lse, qm, km, cos_t, sin_t)
    gq, gk, gv = feed_sum.finish(*grads)
    feed_sum.start()
    ig_qkv, ta_qkv, tb_qkv = qkv_terms_call(gq, gk, gv, normed, bt_qkv, inner_qkv, ad)
    ig_qkv, ta_qkv, tb_qkv = feed_sum.finish(ig_qkv, ta_qkv, tb_qkv)
    last_sum = Scatter([ta_proj, tb_proj, ta_qkv, tb_qkv])
    last_sum.start()
    back = functools.partial(qkv_back_call, gq, gk, gv, first, ig_qkv, tokens, gain1)
    held = back(grad_middle, 0)
    (held,) = last_sum.finish(held)
    last_sum.start()
    tokens_grad = back(held, 1)
    (tokens_grad,) = last_sum.finish(tokens_grad)
    last_sum.start()
    last_sum.finish()
    early, late = feed_sum.values[0], last_sum.values[0]
    factor = 1.0 / math.sqrt(row_count * devices)
    early = factor * early
    late = factor * late
    return (
        block_out,
        tokens_grad,
        late[2 * rows : 3 * rows],
        late[3 * rows :].T,
        late[:rows],
        late[rows : 2 * rows].T,
        early[:rows],
        early[rows : rows * (1 + quarters)].T,
        early[rows * (1 + quarters) : rows * (1 + 2 * quarters)],
        early[rows * (1 + 2 * quarters) :].T,
    )


def solution(mesh):
    return jax.shard_map(
        local,
        mesh=mesh,
        in_specs=(
            P(("dp", "fsdp"), None),
            P(("dp", "fsdp"), None),
            P(("dp", "fsdp")),
            P(("dp", "fsdp")),
            P(("dp", "fsdp")),
            P(("dp", "fsdp")),
            P(("dp", "fsdp"), None),
            P(),
            P(("dp", "fsdp"), None),
            P(),
            P(("dp", "fsdp"), None),
            P(),
            P(("dp", "fsdp"), None),
            P(),
            P(),
            P(),
            P(),
            P(),
            P(("dp", "fsdp"), None),
            P(None, ("dp", "fsdp")),
            P(("dp", "fsdp"), None),
            P(None, ("dp", "fsdp")),
            P(("dp", "fsdp"), None),
            P(None, ("dp", "fsdp")),
            P(("dp", "fsdp"), None),
            P(None, ("dp", "fsdp")),
        ),
        out_specs=(
            P(("dp", "fsdp"), None),
            P(("dp", "fsdp"), None),
            P(("dp", "fsdp"), None),
            P(None, ("dp", "fsdp")),
            P(("dp", "fsdp"), None),
            P(None, ("dp", "fsdp")),
            P(("dp", "fsdp"), None),
            P(None, ("dp", "fsdp")),
            P(("dp", "fsdp"), None),
            P(None, ("dp", "fsdp")),
        ),
        check_vma=False,
    )
```

```python
import functools
import math

import jax
import jax.numpy as jnp
from jax import lax
from jax.experimental import pallas as pl
from jax.experimental.pallas import tpu as pltpu
from jax.sharding import PartitionSpec as P

HEADS = 16
HD = 80
RANK = 16


EPS = 1e-06


BIG = 2.0**60
LOG2E = 1.4426950408889634
BF = jnp.bfloat16
F32 = jnp.float32


def normalize_back(grad_out, unit, spread, gain):
    scaled = grad_out * gain
    return spread * (
        scaled
        - jnp.mean(scaled, axis=-1, keepdims=True)
        - unit * jnp.mean(scaled * unit, axis=-1, keepdims=True)
    )


def rotary_tables(patch_row, patch_col, head_size):
    quarter = head_size // 4
    inverse = 1.0 / 10000.0 ** (jnp.arange(quarter, dtype=jnp.float32) * 2.0 / (head_size // 2))
    angles = jnp.concatenate(
        [
            patch_row.astype(jnp.float32)[:, None] * inverse,
            patch_col.astype(jnp.float32)[:, None] * inverse,
        ],
        axis=1,
    )
    angles = jnp.concatenate([angles, angles], axis=1)
    return (jnp.cos(angles), jnp.sin(angles))


def mm(left, right):
    return lax.dot_general(left, right, (((1,), (0,)), ((), ())), preferred_element_type=F32)


def mm_nt(left, right):
    return lax.dot_general(left, right, (((1,), (1,)), ((), ())), preferred_element_type=F32)


def call(body, name, grid, in_specs, out_specs, out_shape, scratch=(), flops=0, moved=0):
    return pl.pallas_call(
        body,
        name=name,
        grid=grid,
        in_specs=in_specs,
        out_specs=out_specs,
        out_shape=out_shape,
        scratch_shapes=scratch,
        cost_estimate=pl.CostEstimate(flops=flops, transcendentals=0, bytes_accessed=moved),
        compiler_params=pltpu.CompilerParams(
            dimension_semantics=("arbitrary",) * len(grid), vmem_limit_bytes=56 * 1024 * 1024
        ),
    )


def whole(shape):
    return pl.BlockSpec(shape, lambda *_: (0,) * len(shape))


def pick(adapter_ref, count):
    lanes = lax.broadcasted_iota(jnp.int32, (count, 128), 1) // RANK
    return (lanes == adapter_ref[...]).astype(F32)


def turn(values, low):
    size = values.shape[1]
    left = pltpu.roll(values, size - HD // 2, 1)
    right = pltpu.roll(values, HD // 2, 1)
    return jnp.where(low, left, right)


def qkv_body(x_ref, w_ref, a_ref, bt_ref, bias_ref, ad_ref, cos_ref, sin_ref, out_ref, inner_ref):
    part = pl.program_id(0)
    rows = x_ref.shape[0]
    step = 256

    @pl.when(part == 0)
    def _():
        inner_ref[...] = (mm(x_ref[...], a_ref[...]) * pick(ad_ref, rows)).astype(BF)

    def one(start, rotated):
        sl = pl.ds(start, step)
        y = mm(x_ref[sl, :], w_ref[...]) + mm_nt(inner_ref[sl, :], bt_ref[...]) + bias_ref[...]
        if rotated:
            low = lax.broadcasted_iota(jnp.int32, (step, 640), 1) % HD < HD // 2
            for begin in (0, 640):
                piece = y[:, begin : begin + 640]
                done = piece * cos_ref[sl, :] + turn(piece, low) * sin_ref[sl, :]
                out_ref[sl, begin : begin + 640] = done.astype(BF)
        else:
            out_ref[sl, :] = y.astype(BF)

    @pl.when(part < 2)
    def _():
        for i in range(0, rows, step):
            one(i, True)

    @pl.when(part == 2)
    def _():
        for i in range(0, rows, step):
            one(i, False)


def qkv_call(x, pack, bt, bias, adapter, cos_t, sin_t):
    n, d = x.shape
    return call(
        qkv_body,
        "qkv_rotary",
        (3,),
        [
            whole((n, d)),
            pl.BlockSpec((d, d), lambda j: (0, j)),
            pl.BlockSpec((d, 128), lambda j: (0, 3 * d // 128)),
            pl.BlockSpec((d, 128), lambda j: (j, 0)),
            pl.BlockSpec((1, d), lambda j: (0, j)),
            whole((n, 1)),
            whole((n, 640)),
            whole((n, 640)),
        ],
        [pl.BlockSpec((n, d), lambda j: (0, j)), whole((n, 128))],
        [jax.ShapeDtypeStruct((n, 3 * d), BF), jax.ShapeDtypeStruct((n, 128), BF)],
        flops=2 * n * d * 3 * d,
        moved=8 * d * d + 12 * n * d,
    )(x, pack, pack, bt, bias, adapter, cos_t, sin_t)


def attend_body(q_ref, k_ref, v_ref, qm_ref, km_ref, out_ref, lse_ref):
    rows = q_ref.shape[0]
    step = 256
    factor = LOG2E / math.sqrt(HD)
    lanes = lax.broadcasted_iota(jnp.int32, (step, 128), 1)
    for i in range(0, rows, step):
        lse_ref[i : i + step, :] = jnp.zeros((step, 128), F32)
    for h in range(8):
        cols = slice(HD * h, HD * h + HD)
        keys = jnp.concatenate([k_ref[:, cols], km_ref[...]], axis=1)
        vals = v_ref[:, cols]
        for i in range(0, rows, step):
            query = jnp.concatenate([q_ref[i : i + step, cols], qm_ref[i : i + step, :]], axis=1)
            s = mm_nt(query, keys)
            top = jnp.max(s, axis=1, keepdims=True)
            e = jnp.exp2((s - top) * factor)
            total = jnp.sum(e, axis=1, keepdims=True)
            o = mm(e.astype(BF), vals) * (1.0 / total)
            out_ref[i : i + step, cols] = o.astype(BF)
            lse = top + jnp.log(total) * math.sqrt(HD)
            lse_ref[i : i + step, :] = jnp.where(lanes == h, lse, lse_ref[i : i + step, :])


def attend_call(qkv, qm, km):
    n = qkv.shape[0]
    d = qkv.shape[1] // 3
    groups = d // 640
    return call(
        attend_body,
        "attend",
        (groups,),
        [
            pl.BlockSpec((n, 640), lambda g: (0, g)),
            pl.BlockSpec((n, 640), lambda g: (0, groups + g)),
            pl.BlockSpec((n, 640), lambda g: (0, 2 * groups + g)),
            whole((n, 48)),
            whole((n, 48)),
        ],
        [pl.BlockSpec((n, 640), lambda g: (0, g)), pl.BlockSpec((n, 128), lambda g: (0, g))],
        [jax.ShapeDtypeStruct((n, d), BF), jax.ShapeDtypeStruct((n, 128 * groups), F32)],
        flops=4 * n * n * d,
        moved=8 * n * d,
    )(qkv, qkv, qkv, qm, km)


def split_low(values, count):
    parts = []
    for _ in range(count):
        part = values.astype(BF)
        parts.append(part)
        values = values - part.astype(F32)
    return parts


def attend_back_body(
    q_ref, k_ref, v_ref, g_ref, o_ref, lse_ref, qm_ref, km_ref, cos_ref, sin_ref,
    dq_ref, dk_ref, dv_ref, dq_s, dk_s,
):
    rows = q_ref.shape[0]
    step = 256
    factor = LOG2E / math.sqrt(HD)
    scale = 1.0 / math.sqrt(HD)
    lanes = lax.broadcasted_iota(jnp.int32, (rows, 48), 1)
    ones_two = jnp.where((lanes == 16) | (lanes == 17), 1.0, 0.0).astype(BF)
    for h in range(8):
        cols = slice(HD * h, HD * h + HD)
        gh = g_ref[:, cols]
        delta = jnp.sum(gh.astype(F32) * o_ref[:, cols].astype(F32), axis=1, keepdims=True)
        d_hi, d_lo = split_low(-delta, 2)
        l_hi, l_mid, l_lo = split_low(-lse_ref[:, h : h + 1], 3)
        q_aug = jnp.where(
            lanes == 16,
            l_hi.astype(F32),
            jnp.where(
                lanes == 17,
                l_mid.astype(F32),
                jnp.where(lanes == 18, l_lo.astype(F32), qm_ref[...].astype(F32)),
            ),
        ).astype(BF)
        g_aug = jnp.where(
            lanes == 16, d_hi.astype(F32), jnp.where(lanes == 17, d_lo.astype(F32), 0.0)
        ).astype(BF)
        query = jnp.concatenate([q_ref[:, cols], q_aug], axis=1)
        grads = jnp.concatenate([gh, g_aug], axis=1)
        keys = jnp.concatenate([k_ref[:, cols], km_ref[...]], axis=1)
        vals = jnp.concatenate([v_ref[:, cols], ones_two], axis=1)
        keys_t = keys.T
        dk = jnp.zeros((rows, 128), F32)
        dv = jnp.zeros((rows, 128), F32)
        for i in range(0, rows, step):
            qb = query[i : i + step, :]
            gb = grads[i : i + step, :]
            p = jnp.exp2(mm_nt(keys, qb) * factor)
            dp = mm_nt(vals, gb)
            ds = (p * dp).astype(BF)
            dv = dv + mm(p.astype(BF), gb)
            dk = dk + mm(ds, qb)
            dq = mm(keys_t, ds)
            dq_s[i : i + step, cols] = dq.T[:, :HD]
        dk_s[:, cols] = dk[:, :HD]
        dv_ref[:, cols] = dv[:, :HD].astype(BF)
    low = lax.broadcasted_iota(jnp.int32, (step, 640), 1) % HD < HD // 2
    for i in range(0, rows, step):
        sl = slice(i, i + step)
        for src, dst in ((dq_s, dq_ref), (dk_s, dk_ref)):
            piece = src[sl, :] * scale
            dst[sl, :] = (piece * cos_ref[sl, :] - turn(piece, low) * sin_ref[sl, :]).astype(BF)


def attend_back_call(qkv, grads, attended, lse, qm, km, cos_t, sin_t):
    n = qkv.shape[0]
    d = qkv.shape[1] // 3
    groups = d // 640
    block = pl.BlockSpec((n, 640), lambda g: (0, g))
    return call(
        attend_back_body,
        "attend_back",
        (groups,),
        [
            block,
            pl.BlockSpec((n, 640), lambda g: (0, groups + g)),
            pl.BlockSpec((n, 640), lambda g: (0, 2 * groups + g)),
            block,
            block,
            pl.BlockSpec((n, 128), lambda g: (0, g)),
            whole((n, 48)),
            whole((n, 48)),
            whole((n, 640)),
            whole((n, 640)),
        ],
        [block, block, block],
        [jax.ShapeDtypeStruct((n, d), BF)] * 3,
        [pltpu.VMEM((n, 640), F32), pltpu.VMEM((n, 640), F32)],
        flops=10 * n * n * d,
        moved=16 * n * d,
    )(qkv, qkv, qkv, grads, attended, lse, qm, km, cos_t, sin_t)


def tables(picture, patch_row, patch_col):
    cosine, sine = rotary_tables(patch_row, patch_col, HD)
    half = HD // 2
    signed = jnp.concatenate([-sine[:, :half], sine[:, half:]], axis=1)
    count = picture.shape[0]
    change = (picture[1:] != picture[:-1]).astype(jnp.int32)
    places = lax.broadcasted_iota(jnp.int32, (count, count - 1), 0)
    before = lax.broadcasted_iota(jnp.int32, (count, count - 1), 1) < places
    index = jnp.sum(jnp.where(before, change[None, :], 0), axis=1)
    lanes = lax.broadcasted_iota(jnp.int32, (1, 48), 1)
    own = lanes == index[:, None]
    qm = jnp.where(own | (lanes >= 16), 0.0, -BIG).astype(BF)
    km = (own | ((lanes >= 16) & (lanes < 19))).astype(BF)
    return (*widen_call(cosine, signed), qm, km)


def stats(values):
    centre = jnp.mean(values, axis=-1, keepdims=True)
    centred = values - centre
    spread = lax.rsqrt(jnp.mean(centred * centred, axis=-1, keepdims=True) + EPS)
    return centred * spread, spread


def once(shape, index):
    return pl.BlockSpec(shape, index, pipeline_mode=pl.Buffered(1))


def proj_body(
    att_ref, w_ref, a_ref, bt_ref, bias_ref, ad_ref, tok_ref, gain_ref, shift_ref,
    mid_ref, norm_ref, inner_ref,
):
    sub = 256
    held = []
    for begin in range(0, att_ref.shape[0], sub):
        sl = pl.ds(begin, sub)
        x = att_ref[sl, :]
        inner = (mm(x, a_ref[...]) * pick(ad_ref.at[sl, :], sub)).astype(BF)
        inner_ref[sl, :] = inner
        held.append((sl, mm(x, w_ref[...]) + bias_ref[...] + mm_nt(inner, bt_ref[...])))
    for sl, branch in held:
        middle = tok_ref[sl, :].astype(F32) + branch
        mid_ref[sl, :] = middle
        unit, _ = stats(middle)
        norm_ref[sl, :] = (unit * gain_ref[...] + shift_ref[...]).astype(BF)


def proj_call(att, pack, first_col, a_col, bt_col, bias, adapter, tokens, gain, shift):
    n, d = att.shape
    step = 512
    row = pl.BlockSpec((step, d), lambda i: (i, 0))
    return call(
        proj_body,
        "proj_norm",
        (n // step,),
        [
            row,
            once((d, d), lambda i: (0, first_col // d)),
            once((d, 128), lambda i: (0, a_col // 128)),
            once((d, 128), lambda i: (0, bt_col // 128)),
            whole((1, d)),
            pl.BlockSpec((step, 1), lambda i: (i, 0)),
            row,
            whole((1, d)),
            whole((1, d)),
        ],
        [row, row, pl.BlockSpec((step, 128), lambda i: (i, 0))],
        [
            jax.ShapeDtypeStruct((n, d), F32),
            jax.ShapeDtypeStruct((n, d), BF),
            jax.ShapeDtypeStruct((n, 128), BF),
        ],
        flops=2 * n * d * d,
        moved=2 * d * d + 10 * n * d,
    )(att, pack, pack, pack, bias, adapter, tokens, gain, shift)


def feed_body(*refs, parts, first, last):
    refs = list(refs)
    take = lambda count: [refs.pop(0) for _ in range(count)]
    x_ref, g_ref = take(2)
    w1, w2, bt1, a2, b1 = take(parts), take(parts), take(parts), take(parts), take(parts)
    ad_ref, a1_ref, bt2_ref = take(3)
    if first:
        base_ref, b2_ref = take(2)
    else:
        base_ref, gx_in, in1_ref, ig2_ref, in2_in, ig1_in = take(6)
        val_ref = take(1)[0]
    if first:
        acc_ref, gx_ref, in1_out, ig2_out, in2_out, ig1_out = take(6)
    if last:
        out_ref, gx_ref, ta1_ref, tb2_ref = take(4)
    ta2, tb1 = take(parts), take(parts)
    if last:
        ta1_s, tb2_s = take(2)
    ta2_s, tb1_s = take(parts), take(parts)
    sums = ta2_s + tb1_s + ([ta1_s, tb2_s] if last else [])
    i = pl.program_id(0)
    end = i == pl.num_programs(0) - 1

    @pl.when(i == 0)
    def _():
        for ref in sums:
            ref[...] = jnp.zeros_like(ref)

    sub = 256
    jobs = []
    for begin in range(0, x_ref.shape[0], sub):
        sl = pl.ds(begin, sub)
        x = x_ref[sl, :]
        g = g_ref[sl, :]
        sel = pick(ad_ref.at[sl, :], sub)
        if first:
            in1 = (mm(x, a1_ref[...]) * sel).astype(BF)
            ig2 = (mm(g, bt2_ref[...]) * sel).astype(BF)
            in1_out[sl, :] = in1
            ig2_out[sl, :] = ig2
            acc = base_ref[sl, :] + b2_ref[...]
            gx = in2 = ig1 = None
        else:
            in1 = in1_ref[sl, :]
            ig2 = ig2_ref[sl, :]
            acc, gx, in2, ig1 = base_ref[sl, :], gx_in[sl, :], in2_in[sl, :], ig1_in[sl, :]
        hs = [mm(x, w1[q][...]) + mm_nt(in1, bt1[q][...]) + b1[q][...] for q in range(parts)]
        gas = [mm_nt(g, w2[q][...]) + mm_nt(ig2, a2[q][...]) for q in range(parts)]
        jobs.append((sl, x, g, sel, in1, ig2, acc, gx, in2, ig1, hs, gas))
    lows = []
    for job in jobs:
        pairs = []
        for h, ga in zip(*job[-2:]):
            s = 0.5 * jnp.tanh(0.851 * h) + 0.5
            pairs.append(((h * s).astype(BF), (ga * (s + 1.702 * h * s * (1.0 - s))).astype(BF)))
        lows.append(pairs)
    for job, pairs in zip(jobs, lows):
        sl, x, g, sel, in1, ig2, acc, gx, in2, ig1, _, _ = job
        in1_t = in1.T
        ig2_t = ig2.T
        for q, (act, gh) in enumerate(pairs):
            more = (mm_nt(gh, w1[q][...]), mm(act, a2[q][...]), mm(gh, bt1[q][...]))
            acc = acc + mm(act, w2[q][...])
            gx, in2, ig1 = more if gx is None else (gx + more[0], in2 + more[1], ig1 + more[2])
            ta2_s[q][...] += mm(ig2_t, act)
            tb1_s[q][...] += mm(in1_t, gh)
        if last:
            low2 = (in2 * sel).astype(BF)
            low1 = (ig1 * sel).astype(BF)
            out_ref[sl, :] = ((acc + mm_nt(low2, bt2_ref[...])) * val_ref[sl, :]).astype(BF)
            gx_ref[sl, :] = gx + mm_nt(low1, a1_ref[...])
            ta1_s[...] += mm(low1.T, x)
            tb2_s[...] += mm(low2.T, g)
        else:
            acc_ref[sl, :] = acc
            gx_ref[sl, :] = gx
            in2_out[sl, :] = in2
            ig1_out[sl, :] = ig1

    @pl.when(end)
    def _():
        for q in range(parts):
            ta2[q][...] = ta2_s[q][...].T.astype(BF)
            tb1[q][...] = tb1_s[q][...].T.astype(BF)
        if last:
            ta1_ref[...] = ta1_s[...].T.astype(BF)
            tb2_ref[...] = tb2_s[...].T.astype(BF)


def feed_call(x, grads, w2, w1, bt1, a2, b1, adapter, a1, bt2, state, first, last):
    n, d = x.shape
    parts = len(w1)
    step = 512 if parts < 3 else 256
    row = pl.BlockSpec((step, d), lambda i: (i, 0))
    thin_row = pl.BlockSpec((step, 128), lambda i: (i, 0))
    one = pl.BlockSpec((step, 1), lambda i: (i, 0))
    thin = once((d, 128), lambda i: (0, 0))
    line = once((1, d), lambda i: (0, 0))

    def wide(col):
        return once((d, d), lambda i: (0, col // d))

    def narrow(col):
        return once((d, 128), lambda i: (0, col // 128))

    in_specs = [row, row] + [wide(c) for _, c in w1] + [wide(c) for _, c in w2]
    in_specs += [narrow(c) for _, c in bt1] + [narrow(c) for _, c in a2] + [line] * parts
    in_specs += [one, narrow(a1[1]), narrow(bt2[1])]
    args = [x, grads] + [v for v, _ in w1 + w2 + bt1 + a2] + list(b1) + [adapter, a1[0], bt2[0]]
    if first:
        in_specs += [row, line]
    else:
        in_specs += [row, row, thin_row, thin_row, thin_row, thin_row, one]
    args += list(state)
    out_specs, out_shape, scratch = [], [], []
    if first:
        out_specs += [row, row, thin_row, thin_row, thin_row, thin_row]
        out_shape += [jax.ShapeDtypeStruct((n, d), F32)] * 2
        out_shape += [jax.ShapeDtypeStruct((n, 128), BF)] * 2 + [jax.ShapeDtypeStruct((n, 128), F32)] * 2
    if last:
        out_specs += [row, row, thin, thin]
        out_shape += [jax.ShapeDtypeStruct((n, d), BF), jax.ShapeDtypeStruct((n, d), F32)]
        out_shape += [jax.ShapeDtypeStruct((d, 128), BF)] * 2
        scratch += [pltpu.VMEM((128, d), F32)] * 2
    out_specs += [thin] * (2 * parts)
    out_shape += [jax.ShapeDtypeStruct((d, 128), BF)] * (2 * parts)
    scratch += [pltpu.VMEM((128, d), F32)] * (2 * parts)
    return call(
        functools.partial(feed_body, parts=parts, first=first, last=last),
        "feed_first" if first else "feed_last",
        (n // step,),
        in_specs,
        out_specs,
        out_shape,
        scratch,
        flops=8 * n * d * d * parts,
        moved=4 * d * d * parts + 24 * n * d,
    )(*args)


def proj_back_body(
    gx_ref, mid_ref, cot_ref, val_ref, gain_ref, w_ref, a_ref, bt_ref, ad_ref, att_ref, inner_ref,
    gm_ref, ga_ref, ta_ref, tb_ref, ta_s, tb_s,
):
    i = pl.program_id(0)
    sub = 256

    @pl.when(i == 0)
    def _():
        ta_s[...] = jnp.zeros_like(ta_s)
        tb_s[...] = jnp.zeros_like(tb_s)

    for begin in range(0, gx_ref.shape[0], sub):
        sl = pl.ds(begin, sub)
        unit, spread = stats(mid_ref[sl, :])
        gm = cot_ref[sl, :].astype(F32) * val_ref[sl, :]
        gm = gm + normalize_back(gx_ref[sl, :], unit, spread, gain_ref[...])
        gm_ref[sl, :] = gm
        gb = gm.astype(BF)
        ig = (mm(gb, bt_ref[...]) * pick(ad_ref.at[sl, :], sub)).astype(BF)
        ga_ref[sl, :] = (mm_nt(gb, w_ref[...]) + mm_nt(ig, a_ref[...])).astype(BF)
        ta_s[...] += mm(ig.T, att_ref[sl, :])
        tb_s[...] += mm(inner_ref[sl, :].T, gb)

    @pl.when(i == pl.num_programs(0) - 1)
    def _():
        ta_ref[...] = ta_s[...].T.astype(BF)
        tb_ref[...] = tb_s[...].T.astype(BF)


def proj_back_call(gx, middle, cot, valid, gain, pack, first_col, a_col, bt_col, adapter, att, inner):
    n, d = gx.shape
    step = 256
    row = pl.BlockSpec((step, d), lambda i: (i, 0))
    one = pl.BlockSpec((step, 1), lambda i: (i, 0))
    thin = once((d, 128), lambda i: (0, 0))
    return call(
        proj_back_body,
        "proj_back",
        (n // step,),
        [
            row,
            row,
            row,
            one,
            whole((1, d)),
            once((d, d), lambda i: (0, first_col // d)),
            once((d, 128), lambda i: (0, a_col // 128)),
            once((d, 128), lambda i: (0, bt_col // 128)),
            one,
            row,
            pl.BlockSpec((step, 128), lambda i: (i, 0)),
        ],
        [row, row, thin, thin],
        [
            jax.ShapeDtypeStruct((n, d), F32),
            jax.ShapeDtypeStruct((n, d), BF),
            jax.ShapeDtypeStruct((d, 128), BF),
            jax.ShapeDtypeStruct((d, 128), BF),
        ],
        [pltpu.VMEM((128, d), F32), pltpu.VMEM((128, d), F32)],
        flops=2 * n * d * d,
        moved=2 * d * d + 18 * n * d,
    )(gx, middle, cot, valid, gain, pack, pack, pack, adapter, att, inner)


def qkv_terms_body(gq_ref, gk_ref, gv_ref, x_ref, bt_ref, inner_ref, ad_ref, ig_ref, ta_ref, tb_ref, ta_s, tb_s):
    i = pl.program_id(0)
    rows, d = x_ref.shape

    @pl.when(i == 0)
    def _():
        ta_s[...] = jnp.zeros_like(ta_s)
        tb_s[...] = jnp.zeros_like(tb_s)

    inner_t = inner_ref[...].T
    total = None
    for part, ref in enumerate((gq_ref, gk_ref, gv_ref)):
        g = ref[...]
        sl = slice(part * d, part * d + d)
        piece = mm(g, bt_ref[sl, :])
        total = piece if total is None else total + piece
        tb_s[:, sl] += mm(inner_t, g)
    ig = (total * pick(ad_ref, rows)).astype(BF)
    ig_ref[...] = ig
    ta_s[...] += mm(ig.T, x_ref[...])

    @pl.when(i == pl.num_programs(0) - 1)
    def _():
        ta_ref[...] = ta_s[...].T.astype(BF)
        tb_ref[...] = tb_s[...].T.astype(BF)


def qkv_terms_call(gq, gk, gv, x, bt, inner, adapter):
    n, d = x.shape
    step = 256
    row = pl.BlockSpec((step, d), lambda i: (i, 0))
    thin_row = pl.BlockSpec((step, 128), lambda i: (i, 0))
    return call(
        qkv_terms_body,
        "qkv_terms",
        (n // step,),
        [row, row, row, row, whole(bt.shape), thin_row, pl.BlockSpec((step, 1), lambda i: (i, 0))],
        [thin_row, whole((d, 128)), whole((3 * d, 128))],
        [
            jax.ShapeDtypeStruct((n, 128), BF),
            jax.ShapeDtypeStruct((d, 128), BF),
            jax.ShapeDtypeStruct((3 * d, 128), BF),
        ],
        [pltpu.VMEM((128, d), F32), pltpu.VMEM((128, 3 * d), F32)],
        flops=4 * n * d * 128 * 4,
        moved=10 * n * d,
    )(gq, gk, gv, x, bt, inner, adapter)


def qkv_back_body(gq_ref, gk_ref, gv_ref, w_ref, ig_ref, a_ref, tok_ref, gain_ref, gm_ref, out_ref, acc_ref, unit_ref, spread_ref):
    part = pl.program_id(0)
    sub = 256
    pieces = [pl.ds(begin, sub) for begin in range(0, tok_ref.shape[0], sub)]

    @pl.when(part == 0)
    def _():
        for sl in pieces:
            acc_ref[sl, :] = mm_nt(gq_ref[sl, :], w_ref[...]) + mm_nt(ig_ref[sl, :], a_ref[...])
        for sl in pieces:
            unit, spread = stats(tok_ref[sl, :].astype(F32))
            unit_ref[sl, :] = unit
            spread_ref[sl, :] = spread

    @pl.when(part == 1)
    def _():
        for sl in pieces:
            acc_ref[sl, :] += mm_nt(gk_ref[sl, :], w_ref[...])

    @pl.when(part == 2)
    def _():
        grads = [acc_ref[sl, :] + mm_nt(gv_ref[sl, :], w_ref[...]) for sl in pieces]
        for sl, grad in zip(pieces, grads):
            back = normalize_back(grad, unit_ref[sl, :], spread_ref[sl, :], gain_ref[...])
            out_ref[sl, :] = gm_ref[sl, :] + back


def qkv_back_call(gq, gk, gv, pack, ig, tokens, gain, gm, half):
    n, d = tokens.shape
    rows = n // 2
    row = pl.BlockSpec((rows, d), lambda p: (half, 0))
    return pl.pallas_call(
        qkv_back_body,
        name="qkv_back",
        grid=(3,),
        in_specs=[
            row,
            row,
            row,
            pl.BlockSpec((d, d), lambda p: (0, p)),
            pl.BlockSpec((rows, 128), lambda p: (half, 0)),
            once((d, 128), lambda p: (0, 3 * d // 128)),
            row,
            whole((1, d)),
            row,
        ],
        out_specs=row,
        out_shape=jax.ShapeDtypeStruct((n, d), F32),
        scratch_shapes=[pltpu.VMEM((rows, d), F32), pltpu.VMEM((rows, d), F32), pltpu.VMEM((rows, 1), F32)],
        input_output_aliases={8: 0},
        cost_estimate=pl.CostEstimate(flops=3 * n * d * d, transcendentals=0, bytes_accessed=6 * d * d + 9 * n * d),
        compiler_params=pltpu.CompilerParams(
            dimension_semantics=("arbitrary",), vmem_limit_bytes=56 * 1024 * 1024
        ),
    )(gq, gk, gv, pack, ig, pack, tokens, gain, gm)


def unfold_rows(block, devices):
    rows = block.shape[0] // devices
    pieces = block.shape[1] // 128
    split = block.reshape(devices, rows, pieces, 128)
    return split.transpose(0, 2, 1, 3).reshape(-1, 128)


def gather_rows(packed):
    return lax.all_gather(packed, ("dp", "fsdp"), axis=0, tiled=True)


def place_body(table_ref, *refs, pieces):
    out_ref = refs[-1]
    mask = table_ref[2]
    begin = 0
    for ref in refs[:pieces]:
        end = begin + ref.shape[-1]
        for k in range(ref.shape[1]):
            out_ref[mask ^ k, 0, 0, :, begin:end] = ref[0, k]
        begin = end


class Gather:
    def __init__(self, *parts):
        self.zs, self.fs = lax.axis_size("dp") // 2, lax.axis_size("fsdp")
        self.rows, self.cols = parts[0].shape[0], sum(p.shape[1] for p in parts)
        self.parts = list(parts)
        self.phase = 0

    def swap(self, value, axis, mask):
        return lax.ppermute(value, axis, [(i, i ^ mask) for i in range(lax.axis_size(axis))])

    def start(self):
        z_masks, f_masks = list(range(2, 2 * self.zs, 2)), list(range(1, self.fs))
        orders = [[("dp", z_masks), ("fsdp", f_masks)], [("fsdp", f_masks), ("dp", z_masks)]]
        self.got = []
        for part, order in zip(self.parts, orders):
            axis, masks = order[self.phase] if self.phase < 2 else ("dp", [1])
            self.got.append([part] + [self.swap(part, axis, m) for m in masks])

    def finish(self, *others):
        sizes = [len(group) for group in self.got]
        held = lax.optimization_barrier(tuple(v for group in self.got for v in group) + others)
        groups, at = [], 0
        for size in sizes:
            groups.append(held[at : at + size])
            at += size
        if self.phase == 0:
            self.parts = [jnp.stack(group) for group in groups]
        elif self.phase == 1:
            self.parts = [jnp.stack(group, axis=1 if i else 0) for i, group in enumerate(groups)]
        if self.phase < 2:
            held = lax.optimization_barrier(tuple(self.parts) + tuple(held[at:]))
            self.parts = list(held[: len(sizes)])
            at = len(sizes)
        else:
            self.far = [group[1] for group in groups[::-1]]
        self.phase += 1
        return held[at:]

    def place(self, side, earlier):
        zs, fs, rows, cols = self.zs, self.fs, self.rows, self.cols
        spot, column = lax.axis_index("dp"), lax.axis_index("fsdp")
        table = jnp.stack([(spot & 1) ^ side, column, spot >> 1]).astype(jnp.int32)
        parts = self.far if side else self.parts[::-1]
        specs = [pl.BlockSpec((1, zs, rows, p.shape[-1]), lambda m, t: (m, 0, 0, 0)) for p in parts]
        specs += [pl.BlockSpec(memory_space=pl.ANY)] * len(earlier)
        return pl.pallas_call(
            functools.partial(place_body, pieces=len(parts)),
            name="place_blocks",
            grid_spec=pltpu.PrefetchScalarGridSpec(
                num_scalar_prefetch=1,
                grid=(fs,),
                in_specs=specs,
                out_specs=pl.BlockSpec((zs, 1, 1, rows, cols), lambda m, t: (0, t[0], t[1] ^ m, 0, 0)),
            ),
            out_shape=jax.ShapeDtypeStruct((zs, 2, fs, rows, cols), BF),
            input_output_aliases={1 + len(parts): 0} if earlier else {},
            cost_estimate=pl.CostEstimate(flops=0, transcendentals=0, bytes_accessed=4 * zs * fs * rows * cols),
            compiler_params=pltpu.CompilerParams(vmem_limit_bytes=48 * 1024 * 1024),
        )(table, *parts, *earlier)


def widen_body(cos_ref, sin_ref, cos_out, sin_out):
    for src, dst in ((cos_ref, cos_out), (sin_ref, sin_out)):
        value = src[...]
        dst[...] = jnp.concatenate([value] * 8, axis=1)


def widen_call(cosine, signed):
    n = cosine.shape[0]
    out = jax.ShapeDtypeStruct((n, 8 * HD), F32)
    specs = [whole((n, 8 * HD))] * 2
    return call(widen_body, "widen_tables", (1,), [whole(cosine.shape)] * 2, specs, [out, out], moved=72 * n * HD)(
        cosine, signed
    )


def pack_body(
    qkv_w, proj_w, fc1_w, fc2_w, qkv_a, proj_a, fc1_a, fc2_a, qkv_b, proj_b, fc1_b, fc2_b, *outs, devices, cut, groups
):
    rows, d = proj_w.shape
    quarters = fc1_w.shape[1] // d

    def turned(ref):
        flipped = ref[...].astype(F32)
        return [flipped[i * rows : (i + 1) * rows].astype(BF) for i in range(flipped.shape[0] // rows)]

    def fill(out, pieces):
        at = 0
        for piece in pieces:
            out[:, at : at + piece.shape[1]] = piece
            at += piece.shape[1]

    fill(outs[1], [qkv_w[:, :cut]])
    fill(outs[0], [qkv_w[:, cut:], qkv_a[...]] + turned(qkv_b))
    up1 = turned(fc1_b)
    for out, group in zip(outs[2:], groups):
        pieces = [fc2_w[q * rows : (q + 1) * rows, :] for q in group]
        for q in group:
            starts = [(i * quarters + q) * rows for i in range(devices)]
            pieces.append(jnp.concatenate([fc1_w[:, c : c + rows] for c in starts], axis=1))
        if group[0] == 0:
            pieces.append(proj_w[...])
        pieces += [up1[q] for q in group]
        pieces += [fc2_a[q * rows : (q + 1) * rows, :] for q in group]
        if group[0] == 0:
            pieces += [fc1_a[...], proj_a[...]] + turned(proj_b) + turned(fc2_b)
        fill(out, pieces)


def pack_call(arrays, devices, groups):
    rows, d = arrays[1].shape
    total = arrays[0].shape[1] + 4 * 128
    cut = total // 128 // 3 * 128
    widths = [total - cut, cut] + [len(g) * (2 * d + 256) + (d + 512 if g[0] == 0 else 0) for g in groups]
    return call(
        functools.partial(pack_body, devices=devices, cut=cut, groups=groups),
        "pack_shards",
        (1,),
        [whole(v.shape) for v in arrays],
        [whole((rows, w)) for w in widths],
        [jax.ShapeDtypeStruct((rows, w), BF) for w in widths],
        moved=4 * rows * sum(widths),
    )(*arrays)


class Scatter:
    def __init__(self, terms):
        zs, fs = lax.axis_size("dp") // 2, lax.axis_size("fsdp")
        self.values = [t.reshape(zs, 2, fs, -1, 128) for t in terms]
        self.phases = [("dp", 1, [1]), ("fsdp", 1, list(range(1, fs))), ("dp", 0, list(range(2, 2 * zs, 2)))]
        self.open = None

    def start(self):
        axis, dim, masks = self.phases.pop(0)
        size = lax.axis_size(axis)
        place = lax.axis_index(axis)
        shift = 0
        if axis == "dp":
            place, shift = (place & 1, 0) if dim else (place >> 1, 1)

        def pick_one(at):
            found = [lax.dynamic_index_in_dim(v, at, dim, keepdims=False) for v in self.values]
            return found[0] if len(found) == 1 else jnp.concatenate(found, axis=-2)

        sends = [pick_one(place ^ (mask >> shift)).astype(BF) for mask in masks]
        got = [lax.ppermute(v, axis, [(i, i ^ mask) for i in range(size)]) for v, mask in zip(sends, masks)]
        self.open = (lambda: pick_one(place), got)

    def finish(self, *others):
        mine, got = self.open
        held = lax.optimization_barrier(tuple(got) + others)
        total = mine().astype(F32)
        for piece in held[: len(got)]:
            total = total + piece.astype(F32)
        self.values = [total]
        return held[len(got) :]


def local(
    tokens,
    cotangent,
    picture,
    adapter,
    patch_row,
    patch_col,
    qkv_weight,
    qkv_bias,
    proj_weight,
    proj_bias,
    fc1_weight,
    fc1_bias,
    fc2_weight,
    fc2_bias,
    norm1_gain,
    norm1_bias,
    norm2_gain,
    norm2_bias,
    qkv_down,
    qkv_up,
    proj_down,
    proj_up,
    fc1_down,
    fc1_up,
    fc2_down,
    fc2_up,
):
    devices = lax.axis_size(("dp", "fsdp"))
    rows, d = proj_weight.shape
    quarters = fc1_weight.shape[1] // d
    q_cols = qkv_weight.shape[1]
    groups = [list(range(quarters - 1)), [quarters - 1]]
    shards = (qkv_weight, proj_weight, fc1_weight, fc2_weight, qkv_down, proj_down, fc1_down, fc2_down)
    shards += (qkv_up.T, proj_up.T, fc1_up.T, fc2_up.T)
    part_b, part_a, pack_a, pack_b = pack_call(shards, devices, groups)
    one = Gather(part_b, part_a)
    one.start()

    def spots(source, count, extra):
        wide = [(source, q * d) for q in range(2 * count)]
        base = (2 * count + extra) * d
        thin = [(source, base + q * 128) for q in range(2 * count)]
        return [wide[:count], wide[count:], thin[:count], thin[count:]]

    count = len(groups[0])
    row_count = tokens.shape[0]
    unit_one, _ = stats(tokens.astype(F32))
    normed = (unit_one * norm1_gain + norm1_bias).astype(BF)
    (normed,) = one.finish(normed)
    second = gather_rows(pack_a)
    third = gather_rows(pack_b)
    proj_col = 2 * count * d
    a1_col = proj_col + d + 2 * count * 128
    ap_col, btp_col, bt2_col = a1_col + 128, a1_col + 256, a1_col + 384
    one.start()
    ad = adapter[:, None]
    valid = (picture >= 0).astype(F32)[:, None]
    grad_low = (cotangent.astype(F32) * valid).astype(BF)
    bias1 = fc1_bias.reshape(devices, quarters, rows).transpose(1, 0, 2).reshape(quarters, 1, d)
    small = [qkv_bias[None], proj_bias[None], norm1_gain[None], norm2_gain[None], norm2_bias[None], fc2_bias[None]]
    small += [bias1[q] for q in range(quarters)] + [ad, valid, grad_low, *tables(picture, patch_row, patch_col)]
    small = one.finish(*small)
    bias_qkv, bias_proj, gain1, gain2, shift2, bias2, *bias1 = small[: 6 + quarters]
    ad, valid, grad_low, cos_t, sin_t, qm, km = small[6 + quarters :]
    one.start()
    first = one.place(0, ())
    (first,) = one.finish(first)
    first = one.place(1, (first,)).reshape(devices * rows, -1)
    bt_qkv = unfold_rows(first[:, q_cols + 128 :], devices)
    qkv, inner_qkv = qkv_call(normed, first, bt_qkv, bias_qkv, ad, cos_t, sin_t)
    attended, lse = attend_call(qkv, qm, km)
    middle, normed_two, inner_proj = proj_call(
        attended, second, proj_col, ap_col, btp_col, bias_proj, ad, tokens, gain2, shift2
    )
    a1, bt2 = (second, a1_col), (second, bt2_col)
    early = spots(second, count, 1)
    final = spots(third, quarters - count, 0)
    acc, grad_x, in1, ig2, in2, ig1, *terms_a = feed_call(
        normed_two, grad_low, *early, bias1[:count], ad, a1, bt2, (middle, bias2), True, False
    )
    na, nb = count, quarters - count
    state = (acc, grad_x, in1, ig2, in2, ig1, valid)
    block_out, grad_two, ta_fc1, tb_fc2, *terms_b = feed_call(
        normed_two, grad_low, *final, bias1[count:], ad, a1, bt2, state, False, True
    )

    feed_sum = Scatter([ta_fc1, *terms_a[na:], *terms_b[nb:], *terms_a[:na], *terms_b[:nb], tb_fc2])
    feed_sum.start()
    grad_middle, grad_att, ta_proj, tb_proj = proj_back_call(
        grad_two, middle, cotangent, valid, gain2, second, proj_col, ap_col, btp_col, ad, attended, inner_proj
    )
    (grad_att,) = feed_sum.finish(grad_att)
    feed_sum.start()
    grads = attend_back_call(qkv, grad_att, attended, lse, qm, km, cos_t, sin_t)
    gq, gk, gv = feed_sum.finish(*grads)
    feed_sum.start()
    ig_qkv, ta_qkv, tb_qkv = qkv_terms_call(gq, gk, gv, normed, bt_qkv, inner_qkv, ad)
    ig_qkv, ta_qkv, tb_qkv = feed_sum.finish(ig_qkv, ta_qkv, tb_qkv)
    last_sum = Scatter([ta_proj, tb_proj, ta_qkv, tb_qkv])
    last_sum.start()
    back = functools.partial(qkv_back_call, gq, gk, gv, first, ig_qkv, tokens, gain1)
    held = back(grad_middle, 0)
    (held,) = last_sum.finish(held)
    last_sum.start()
    tokens_grad = back(held, 1)
    (tokens_grad,) = last_sum.finish(tokens_grad)
    last_sum.start()
    last_sum.finish()
    early, late = feed_sum.values[0], last_sum.values[0]
    factor = 1.0 / math.sqrt(row_count * devices)
    early = factor * early
    late = factor * late
    return (
        block_out,
        tokens_grad,
        late[2 * rows : 3 * rows],
        late[3 * rows :].T,
        late[:rows],
        late[rows : 2 * rows].T,
        early[:rows],
        early[rows : rows * (1 + quarters)].T,
        early[rows * (1 + quarters) : rows * (1 + 2 * quarters)],
        early[rows * (1 + 2 * quarters) :].T,
    )


def solution(mesh):
    return jax.shard_map(
        local,
        mesh=mesh,
        in_specs=(
            P(("dp", "fsdp"), None),
            P(("dp", "fsdp"), None),
            P(("dp", "fsdp")),
            P(("dp", "fsdp")),
            P(("dp", "fsdp")),
            P(("dp", "fsdp")),
            P(("dp", "fsdp"), None),
            P(),
            P(("dp", "fsdp"), None),
            P(),
            P(("dp", "fsdp"), None),
            P(),
            P(("dp", "fsdp"), None),
            P(),
            P(),
            P(),
            P(),
            P(),
            P(("dp", "fsdp"), None),
            P(None, ("dp", "fsdp")),
            P(("dp", "fsdp"), None),
            P(None, ("dp", "fsdp")),
            P(("dp", "fsdp"), None),
            P(None, ("dp", "fsdp")),
            P(("dp", "fsdp"), None),
            P(None, ("dp", "fsdp")),
        ),
        out_specs=(
            P(("dp", "fsdp"), None),
            P(("dp", "fsdp"), None),
            P(("dp", "fsdp"), None),
            P(None, ("dp", "fsdp")),
            P(("dp", "fsdp"), None),
            P(None, ("dp", "fsdp")),
            P(("dp", "fsdp"), None),
            P(None, ("dp", "fsdp")),
            P(("dp", "fsdp"), None),
            P(None, ("dp", "fsdp")),
        ),
        check_vma=False,
    )
```
